32 devices in a mesh: seq: 8 (over y, x, core), hid: 4 (over z).
Axes of the slice: x: 2, y: 2, z: 4, core: 2. Of those that a mesh axis runs over, the one named last changes fastest.
Arguments:
- tokens: bfloat16 [2048, 768], P('seq'), may hold values from -6 to 6
- query_weight: bfloat16 [768, 768], P(None, 'hid'), may hold values from -0.21875 to 0.21875
- query_shift: float32 [768], P('hid'), may hold values from -3 to 3
- key_weight: bfloat16 [768, 768], P(None, 'hid'), may hold values from -0.21875 to 0.21875
- key_shift: float32 [768], P('hid'), may hold values from -3 to 3
- value_weight: bfloat16 [768, 768], P(None, 'hid'), may hold values from -0.21875 to 0.21875
- value_shift: float32 [768], P('hid'), may hold values from -3 to 3
- mixer_weight: bfloat16 [768, 768], P('hid'), may hold values from -0.875 to 0.875
- mixer_shift: float32 [768], replicated, may hold values from -3 to 3
- conv_taps: float32 [12, 35], P('hid'), may hold values from -0.18 to 0.18
- first_gain: float32 [768], replicated, may hold values from 0.5 to 1.5
- first_shift: float32 [768], replicated, may hold values from -1.75 to 1.75
- up_weight: bfloat16 [768, 3072], P(None, 'hid'), may hold values from -0.21875 to 0.21875
- up_shift: float32 [3072], P('hid'), may hold values from -3 to 3
- down_weight: bfloat16 [3072, 768], P('hid'), may hold values from -0.109375 to 0.109375
- down_shift: float32 [768], replicated, may hold values from -1.75 to 1.75
- second_gain: float32 [768], replicated, may hold values from 0.5 to 1.5
- second_shift: float32 [768], replicated, may hold values from -1.75 to 1.75
- hyperplanes: float32 [32, 64], replicated, may hold values from -6 to 6
- plane_choice: int32 [4, 8], replicated, may hold values from 0 to 31
- doc_lengths: int32 [2], replicated, may hold values from 1 to 1536, 2048 in all
- out_grad: float32 [2048, 768], P('seq'), may hold values from -6 to 6
Outputs:
- layer_out: bfloat16 [2048, 768], P('seq')
- tokens_grad: float32 [2048, 768], P('seq')
- query_grad: float32 [768, 768], P(None, 'hid')
- query_offsets: float32 [768], P('hid')
- key_grad: float32 [768, 768], P(None, 'hid')
- key_offsets: float32 [768], P('hid')
- value_grad: float32 [768, 768], P(None, 'hid')
- value_offsets: float32 [768], P('hid')
- mixer_grad: float32 [768, 768], P('hid')
- mixer_offsets: float32 [768], replicated
- taps_grad: float32 [12, 35], P('hid')
- first_gains: float32 [768], replicated
- first_shifts: float32 [768], replicated
- up_grad: float32 [768, 3072], P(None, 'hid')
- up_offsets: float32 [3072], P('hid')
- down_grad: float32 [3072, 768], P('hid')
- down_offsets: float32 [768], replicated
- second_gains: float32 [768], replicated
- second_shifts: float32 [768], replicated
The draws below stay inside these ranges and needn't reach their ends.
Inputs may be any that keep to these rules, and one draw needn't show every extreme that they name: `doc_lengths`: the item holds 2 documents one after another; the longest has at most 1536 tokens.
All inputs are finite; a program needn't handle non-finite values.
Results may differ from the reference program's by a relative error of at most 0.034.
Values may be sent and summed in bfloat16 or wider, within the bound.
No kernel may reach another device: no remote copies, remote signals or barrier semaphores. Data moves between devices by JAX's collectives and lax.ppermute only.
A program may use at most 128 MiB of HBM per device.

```python
import math
import jax
import jax.numpy as jnp
import numpy as np
from jax import lax

D = 768
H = 12
FF = 3072
HD = 64
BITS = 8
PLANES = 32
HASH_ROUNDS = 4
CONV = 35
ITEM_LEN = 2048
DOCS = 2
DOC_MOST = 1536


def place_ends(drawn, stream_key, low, high):
    extent = drawn.shape
    place = [jax.random.randint(jax.random.fold_in(stream_key, axis), (), 0, extent[axis]) for axis in range(len(extent))]
    drawn = drawn.at[tuple(place)].set(low)
    longest = extent.index(max(extent))
    place[longest] = (place[longest] + 1) % extent[longest]
    return drawn.at[tuple(place)].set(high)


def steps_of(stream_key, shape, cuts, low, high):
    level = 1.0
    for axis_at, blocks in cuts:
        draws = jax.random.uniform(jax.random.fold_in(jax.random.fold_in(stream_key, 6), axis_at), (blocks,), jnp.float32, low / len(cuts), high / len(cuts))
        level = level * jnp.repeat(jnp.exp(draws), shape[axis_at] // blocks).reshape((-1,) + (1,) * (len(shape) - 1 - axis_at))
    return level


def split_up(count, total, most, lean):
    portions = [(1 << 20) // math.isqrt(standing ** lean) + 1 for standing in range(2, count + 1)]
    spare, given = total - most - (count - 1), [1] * (count - 1)
    while spare > 0:
        free = [i for i in range(count - 1) if given[i] < most]
        mass, left = sum([portions[i] for i in free]), spare
        for i in free:
            more = min(most - given[i], max(1, left * portions[i] // mass), spare)
            given[i] = given[i] + more
            spare = spare - more
    return np.array([most] + given)


def uneven_parts(rng, count, total, most, slope):
    if count == 2:
        one = jax.random.randint(rng, (), max(1, total - most), min(most, total - 1) + 1)
        return jnp.stack([one, total - one])
    lengths = jnp.asarray(split_up(count, total, most, slope), jnp.int32)
    couples = (count - 1) // 2
    source_of, sink = lengths[1:1 + 2 * couples:2], lengths[2:2 + 2 * couples:2]
    room = jnp.minimum(source_of - 1, most - sink)
    moved = jax.random.randint(jax.random.fold_in(rng, 1), (couples,), 0, 1 << 20) % (room + 1)
    lengths = lengths.at[1:1 + 2 * couples:2].set(source_of - moved).at[2:2 + 2 * couples:2].set(sink + moved)
    return lengths[jax.random.permutation(jax.random.fold_in(rng, 2), count)]


def normal_values(rng, shape, scale, limit, cuts=(), held_as=jnp.bfloat16):
    entries = jax.random.normal(rng, shape, jnp.float32) * scale
    if len(cuts) > 0:
        entries = steps_of(rng, shape, cuts, -0.22, 0.18) * entries
    return jnp.clip(entries, min=-limit, max=limit).astype(held_as)


def setup_inputs(seed: int = 0) -> dict:
    keys = jax.random.split(jax.random.key(seed), 23)
    return {
        "tokens": normal_values(keys[0], (ITEM_LEN, D), 1.0, 6.0, ((0, 8),)),
        "query_weight": normal_values(keys[1], (D, D), D ** -0.5, 0.21875, ((1, 4),)),
        "query_shift": normal_values(keys[2], (D,), 0.5, 3.0, ((0, 4),), jnp.float32),
        "key_weight": normal_values(keys[3], (D, D), D ** -0.5, 0.21875, ((1, 4),)),
        "key_shift": normal_values(keys[4], (D,), 0.5, 3.0, ((0, 4),), jnp.float32),
        "value_weight": normal_values(keys[5], (D, D), D ** -0.5, 0.21875, ((1, 4),)),
        "value_shift": normal_values(keys[6], (D,), 0.5, 3.0, ((0, 4),), jnp.float32),
        "mixer_weight": normal_values(keys[7], (D, D), (D // 16) ** -0.5, 0.875, ((0, 4),)),
        "mixer_shift": normal_values(keys[8], (D,), 0.5, 3.0, (), jnp.float32),
        "conv_taps": normal_values(keys[9], (H, CONV), 0.03, 0.18, ((0, 4),), jnp.float32),
        "first_gain": jnp.clip(1.0 + 0.1 * jax.random.normal(keys[10], (D,), jnp.float32), 0.5, 1.5),
        "first_shift": normal_values(keys[11], (D,), 0.3, 1.75, (), jnp.float32),
        "up_weight": normal_values(keys[12], (D, FF), D ** -0.5, 0.21875, ((1, 4),)),
        "up_shift": normal_values(keys[13], (FF,), 0.5, 3.0, ((0, 4),), jnp.float32),
        "down_weight": normal_values(keys[14], (FF, D), FF ** -0.5, 0.109375, ((0, 4),)),
        "down_shift": normal_values(keys[15], (D,), 0.3, 1.75, (), jnp.float32),
        "second_gain": jnp.clip(1.0 + 0.1 * jax.random.normal(keys[16], (D,), jnp.float32), 0.5, 1.5),
        "second_shift": normal_values(keys[17], (D,), 0.3, 1.75, (), jnp.float32),
        "hyperplanes": normal_values(keys[18], (PLANES, HD), 1.0, 6.0, (), jnp.float32),
        "plane_choice": place_ends(jax.random.randint(keys[19], (HASH_ROUNDS, BITS), 0, PLANES), jax.random.fold_in(keys[19], 1), 0, PLANES - 1).astype(jnp.int32),
        "doc_lengths": uneven_parts(keys[20], DOCS, ITEM_LEN, DOC_MOST, 2).astype(jnp.int32),
        "out_grad": normal_values(keys[21], (ITEM_LEN, D), 1.0, 6.0, ((0, 8),), jnp.float32),
    }


@jax.custom_vjp
def low(v):
    return lax.optimization_barrier(v.astype(jnp.bfloat16)).astype(jnp.float32)

@jax.custom_vjp
def low_back(v):
    return v

def low_keep(v):
    return (low(v), None)

def low_pass(kept, grad):
    return (grad,)

def back_keep(v):
    return (v, None)

def back_low(kept, grad):
    return (low(grad),)
low.defvjp(low_keep, low_pass)
low_back.defvjp(back_keep, back_low)
SHARP = 2.0
NORM_EPS = 1e-05
UNIT_EPS = 1e-06
UPPER_PRECISION = lax.Precision.HIGHEST

def doc_index(positions, doc_lengths):
    starts = jnp.cumsum(doc_lengths) - doc_lengths
    inside = (positions >= 0) & (positions < jnp.sum(doc_lengths))
    found = lax.optimization_barrier(jnp.sum((positions[:, None] >= starts[None, :]).astype(jnp.int32), axis=1)) - 1
    return jnp.where(inside, found, -1).astype(jnp.int32)

def feature_tree(picked):
    lead = picked.shape[:-1]
    parts = picked.reshape(lead + (HASH_ROUNDS, BITS))
    features = jnp.ones(lead + (HASH_ROUNDS, 1), jnp.float32)
    for bit in range(BITS):
        features = jnp.concatenate([features, features * parts[..., bit:bit + 1]], axis=-1)
    return (features * 2.0 ** (-0.5 * BITS)).reshape(lead + (HASH_ROUNDS * 2 ** BITS,))

def norm(rows, gain, shift):
    center = rows - lax.optimization_barrier(jnp.mean(rows, axis=-1, keepdims=True))
    return center * lax.rsqrt(lax.optimization_barrier(jnp.mean(center * center, axis=-1, keepdims=True)) + NORM_EPS) * gain + shift

def forward(tokens, weights, hyperplanes, chooser, segment):
    query_weight, query_shift, key_weight, key_shift, value_weight, value_shift, mixer_weight, mixer_shift, conv_taps, first_gain, first_shift, up_weight, up_shift, down_weight, down_shift, second_gain, second_shift = weights
    length = tokens.shape[0]
    head_size = D // H
    width = HASH_ROUNDS * 2 ** BITS

    def project(weight, shift):
        return low_back(jnp.dot(tokens, weight, precision=UPPER_PRECISION) + shift).reshape(length, H, head_size)

    def features(raw):
        unit = raw * lax.rsqrt(lax.optimization_barrier(jnp.sum(raw * raw, axis=-1, keepdims=True)) + UNIT_EPS)
        codes = low(jnp.tanh(SHARP * jnp.einsum('thd,pd->thp', unit, hyperplanes, precision=UPPER_PRECISION)))
        return low(feature_tree(jnp.einsum('thp,pc->thc', codes, chooser, precision=UPPER_PRECISION)))
    query_feature_rows = features(project(query_weight, query_shift))
    key_feature_rows = features(project(key_weight, key_shift))
    value_low = low(project(value_weight, value_shift))
    block = math.gcd(length, 512)

    def attend(pair):
        block_feature_rows, block_segment = pair
        collision_scores = jnp.einsum('rbl,jbl->brj', block_feature_rows, key_feature_rows, precision=UPPER_PRECISION) / HASH_ROUNDS
        same = block_segment[:, None] == segment[None, :]
        weights_block = low_back(jnp.where(same[None], collision_scores, 0.0))
        weighted = low_back(jnp.einsum('hqk,khe->qhe', low(weights_block), value_low, precision=UPPER_PRECISION))
        total = 1.0 + lax.optimization_barrier(jnp.sum(weights_block, axis=-1)).T
        return weighted / total[:, :, None]
    attention = lax.map(jax.checkpoint(attend), (query_feature_rows.reshape(length // block, block, H, width), segment.reshape(length // block, block)))
    attention = attention.reshape(length, H, head_size)
    radius = (CONV - 1) // 2
    padded = jnp.pad(value_low, ((radius, radius), (0, 0), (0, 0)))
    padded_segment = jnp.pad(segment, (radius, radius), constant_values=-1)
    conv_out = jnp.zeros_like(value_low)
    for tap in range(CONV):
        same = padded_segment[tap:tap + length] == segment
        conv_out = conv_out + conv_taps[:, tap][None, :, None] * jnp.where(same[:, None, None], padded[tap:tap + length], 0.0)
    context = low((attention + conv_out).reshape(length, D))
    mixed = low_back(jnp.dot(context, mixer_weight, precision=UPPER_PRECISION) + mixer_shift)
    first_out = norm(tokens + mixed, first_gain, first_shift)
    upward = low_back(jnp.dot(low(first_out), up_weight, precision=UPPER_PRECISION) + up_shift)
    hidden = low(jax.nn.gelu(upward, approximate=False))
    downward = low_back(jnp.dot(hidden, down_weight, precision=UPPER_PRECISION) + down_shift)
    return norm(first_out + downward, second_gain, second_shift)

def reference(tokens, query_weight, query_shift, key_weight, key_shift, value_weight, value_shift, mixer_weight, mixer_shift, conv_taps, first_gain, first_shift, up_weight, up_shift, down_weight, down_shift, second_gain, second_shift, hyperplanes, plane_choice, doc_lengths, out_grad):
    segment = doc_index(jnp.arange(ITEM_LEN, dtype=jnp.int32), doc_lengths)
    chooser = (jnp.arange(PLANES, dtype=jnp.int32)[:, None] == plane_choice.reshape(1, -1)).astype(jnp.float32)
    weights = (query_weight.astype(jnp.float32), query_shift, key_weight.astype(jnp.float32), key_shift, value_weight.astype(jnp.float32), value_shift, mixer_weight.astype(jnp.float32), mixer_shift, conv_taps, first_gain, first_shift, up_weight.astype(jnp.float32), up_shift, down_weight.astype(jnp.float32), down_shift, second_gain, second_shift)

    def wrapped(inputs, weight_tuple):
        return forward(inputs, weight_tuple, hyperplanes, chooser, segment)
    result, pull = jax.vjp(wrapped, tokens.astype(jnp.float32), weights)
    tokens_grad, grads = pull(out_grad.astype(jnp.float32))
    return (result.astype(jnp.bfloat16), tokens_grad, grads[0], grads[1], grads[2], grads[3], grads[4], grads[5], grads[6], grads[7], grads[8], grads[9], grads[10], grads[11], grads[12], grads[13], grads[14], grads[15], grads[16])
```

```python
import functools
import math

import jax
import jax.numpy as jnp
from jax import lax
from jax.experimental import pallas as pl
from jax.experimental.pallas import tpu as pltpu
from jax.sharding import PartitionSpec as P

D = 768
H = 12
HS = 64
BITS = 8
PLANES = 32
HASHES = 4
CONV = 35
RADIUS = 17
FEATS = HASHES * 2**BITS
SHARP = 2.0
NORM_EPS = 1e-05
UNIT_EPS = 1e-06
EXACT = lax.Precision.HIGHEST
F32 = jnp.float32
BF16 = jnp.bfloat16
ROWS = 256
HEADS = 3
TAP_LANE = 111
VMEM = pl.BlockSpec(memory_space=pltpu.VMEM)
SMEM = pl.BlockSpec(memory_space=pltpu.SMEM)
LIMIT = 60 * 1024 * 1024


def dot(a, b):
    return lax.dot_general(a, b, (((1,), (0,)), ((), ())), preferred_element_type=F32)


def dot_nt(a, b):
    return lax.dot_general(a, b, (((1,), (1,)), ((), ())), preferred_element_type=F32)


def dot_exact(a, b):
    return lax.dot_general(
        a, b, (((1,), (0,)), ((), ())), precision=EXACT, preferred_element_type=F32
    )


def doc_count(pos, lengths):
    start = jnp.int32(0)
    found = jnp.zeros_like(pos)
    for d in range(lengths.shape[0]):
        found = found + (pos >= start).astype(jnp.int32)
        start = start + lengths[d]
    return found + (pos >= start).astype(jnp.int32)


def blocks_meet(mine, other, lengths):
    a0 = doc_count(mine * ROWS, lengths)
    a1 = doc_count(mine * ROWS + (ROWS - 1), lengths)
    b0 = doc_count(other * ROWS, lengths)
    b1 = doc_count(other * ROWS + (ROWS - 1), lengths)
    return jnp.logical_and(a0 <= b1, b0 <= a1)


def same_doc(row_start, rows, col_start, cols, lengths, reverse=False):
    rid = row_start + lax.broadcasted_iota(jnp.int32, (rows, 1), 0)
    cid = lax.broadcasted_iota(jnp.int32, (1, cols), 1)
    cid = col_start + ((cols - 1) - cid if reverse else cid)
    return doc_count(rid, lengths) == doc_count(cid, lengths)


def hash_base(picks, m, lanes):
    bit = lax.broadcasted_iota(jnp.int32, (8, lanes), 0)
    factors = []
    for b in range(3):
        on = (bit & (1 << b)) != 0
        row = jnp.broadcast_to(picks[m * BITS + b : m * BITS + b + 1, :], (8, lanes))
        factors.append((on, jnp.where(on, row, 1.0)))
    return factors


def hash_feats(picks, m, lanes):
    factors = hash_base(picks, m, lanes)
    scale = 2.0 ** (-0.5 * BITS)
    feats = [(factors[0][1] * scale) * (factors[1][1] * factors[2][1])]
    rows = {}
    for b in range(3, BITS):
        rows[b] = jnp.broadcast_to(picks[m * BITS + b : m * BITS + b + 1, :], (8, lanes))
        feats = feats + [f * rows[b] for f in feats]
    return feats, rows, factors


def expand(picks, phi_ref):
    lanes = picks.shape[1]
    for m in range(HASHES):
        feats = hash_feats(picks, m, lanes)[0]
        for i in range(0, len(feats), 2):
            both = jnp.concatenate([feats[i], feats[i + 1]], axis=0)
            phi_ref[m * 256 + i * 8 : m * 256 + i * 8 + 16, :] = both.astype(BF16)


def expand_back(picks, dphi_ref, lane0, lanes):
    out = []
    scale = 2.0 ** (-0.5 * BITS)
    for m in range(HASHES):
        feats, rows, factors = hash_feats(picks, m, lanes)
        grads = [
            dphi_ref[m * 256 + i * 8 : m * 256 + i * 8 + 8, lane0 : lane0 + lanes]
            for i in range(32)
        ]
        found = {}
        for b in range(BITS - 1, 2, -1):
            half = len(grads) // 2
            total = grads[half] * feats[0]
            for i in range(1, half):
                total = total + grads[half + i] * feats[i]
            found[b] = jnp.sum(total, axis=0, keepdims=True)
            grads = [grads[i] + grads[half + i] * rows[b] for i in range(half)]
        g = grads[0] * scale
        (on0, f0), (on1, f1), (on2, f2) = factors
        found[0] = jnp.sum(jnp.where(on0, g * (f1 * f2), 0.0), axis=0, keepdims=True)
        found[1] = jnp.sum(jnp.where(on1, g * (f0 * f2), 0.0), axis=0, keepdims=True)
        found[2] = jnp.sum(jnp.where(on2, g * (f0 * f1), 0.0), axis=0, keepdims=True)
        out.extend(found[b] for b in range(BITS))
    return jnp.concatenate(out, axis=0)


def heads_on_lanes(rows):
    turned = rows.T
    return jnp.concatenate([turned[h * HS : (h + 1) * HS] for h in range(HEADS)], axis=1)


def heads_on_rows(turned):
    return jnp.concatenate(
        [turned[:, h * ROWS : (h + 1) * ROWS] for h in range(HEADS)], axis=0
    ).T


def project_body(
    tokens, wq, bq, wk, bk, wv, bv, planes, choose, raw_q, raw_k, tan_q, tan_k, pick_q, pack
):
    x = tokens[...]

    def codes(w, b, raw_ref, tan_ref):
        raw = heads_on_lanes(dot(x, w[...]) + b[...])
        raw_ref[...] = raw
        unit = raw * lax.rsqrt(jnp.sum(raw * raw, axis=0, keepdims=True) + UNIT_EPS)
        tan = jnp.tanh(SHARP * dot_exact(planes[...], unit))
        tan_ref[...] = tan
        return dot(choose[...], tan.astype(BF16)).astype(BF16)

    pack[0:PLANES, :] = codes(wk, bk, raw_k, tan_k)
    values = heads_on_lanes(dot(x, wv[...]) + bv[...])
    pack[PLANES : PLANES + HS, :] = values.astype(BF16)
    pick_q[...] = codes(wq, bq, raw_q, tan_q)


def project(tokens, wq, bq, wk, bk, wv, bv, planes, choose):
    wide = HEADS * ROWS
    shapes = (
        jax.ShapeDtypeStruct((HS, wide), F32),
        jax.ShapeDtypeStruct((HS, wide), F32),
        jax.ShapeDtypeStruct((PLANES, wide), F32),
        jax.ShapeDtypeStruct((PLANES, wide), F32),
        jax.ShapeDtypeStruct((PLANES, wide), BF16),
        jax.ShapeDtypeStruct((PLANES + HS, wide), BF16),
    )
    return pl.pallas_call(
        project_body,
        out_shape=shapes,
        in_specs=[VMEM] * 9,
        out_specs=tuple([VMEM] * 6),
        name="project",
        compiler_params=pltpu.CompilerParams(vmem_limit_bytes=LIMIT),
        cost_estimate=pl.CostEstimate(flops=300_000_000, bytes_accessed=3_000_000, transcendentals=0),
    )(tokens, wq, bq, wk, bk, wv, bv, planes, choose)


def local_feats_body(pick_q, pack, feat_q, feat_k, phi):
    for src, dst in ((pick_q, feat_q), (pack, feat_k)):
        for h in range(HEADS):
            picks = src[0:PLANES, h * ROWS : (h + 1) * ROWS].astype(F32)
            expand(picks, phi)
            dst[h] = phi[...].T


def local_feats(pick_q, pack):
    shape = jax.ShapeDtypeStruct((HEADS, ROWS, FEATS), BF16)
    return pl.pallas_call(
        local_feats_body,
        out_shape=(shape, shape),
        in_specs=[VMEM] * 2,
        out_specs=(VMEM, VMEM),
        scratch_shapes=[pltpu.VMEM((FEATS, ROWS), BF16)],
        name="local_feats",
        compiler_params=pltpu.CompilerParams(vmem_limit_bytes=LIMIT),
        cost_estimate=pl.CostEstimate(flops=100_000_000, bytes_accessed=6_000_000, transcendentals=0),
    )(pick_q, pack)


def window(packs, mine, low, high, n):
    def at(h):
        before = jnp.bitwise_xor(mine, jnp.maximum(mine - 1, 0))
        after = jnp.bitwise_xor(mine, jnp.minimum(mine + 1, n - 1))
        lane = h * ROWS
        return jnp.concatenate(
            [
                packs[before, low:high, lane + 128 : lane + 256],
                packs[0, low:high, lane : lane + 256],
                packs[after, low:high, lane : lane + 128],
            ],
            axis=1,
        )

    return at


def band(row):
    return pltpu.roll(jnp.broadcast_to(row, (ROWS, 512)), 0, 1, stride=1, stride_axis=0)


def split_dot(a, b, mul):
    high = a.astype(BF16)
    low = (a - high.astype(F32)).astype(BF16)
    return mul(high, b) + mul(low, b)


def forward_body(n, lengths, place, feat_q, taps, *refs):
    pack_in, (context, weighted, total_out) = refs[:n], refs[n : n + 3]
    packs, phi0, phi1, phi2, acc, tot = refs[n + 3 :]
    phis = (phi0, phi1, phi2)
    mine = place[0]
    for k in range(n):
        packs[k] = pack_in[k][...]
    acc[...] = jnp.zeros_like(acc)
    tot[...] = jnp.zeros_like(tot)

    def block(k, carry):
        other = jnp.bitwise_xor(mine, k)

        @pl.when(blocks_meet(mine, other, lengths))
        def _():
            same = same_doc(mine * ROWS, ROWS, other * ROWS, ROWS, lengths)
            for h in range(HEADS):
                lane = h * ROWS
                expand(packs[k, 0:PLANES, lane : lane + ROWS].astype(F32), phis[h])
                score = dot(feat_q[h], phis[h][...])
                w = jnp.where(same, score * (1.0 / HASHES), 0.0)
                tot[h] += w[:, :128] + w[:, 128:]
                acc[h] += dot_nt(w.astype(BF16), packs[k, PLANES : PLANES + HS, lane : lane + ROWS])

        return carry

    lax.fori_loop(0, n, block, 0)
    near = same_doc(mine * ROWS, ROWS, mine * ROWS - 128, 512, lengths)
    ext = window(packs, mine, PLANES, PLANES + HS, n)
    outs, sums, parts = [], [], []
    for h in range(HEADS):
        total = 1.0 + jnp.sum(tot[h], axis=1, keepdims=True)
        taps_band = jnp.where(near, band(taps[h : h + 1, :]), 0.0)
        conv = split_dot(taps_band, ext(h), dot_nt)
        sums.append(jnp.broadcast_to(total, (ROWS, HS)))
        parts.append(acc[h])
        outs.append(acc[h] / total + conv)
    context[...] = jnp.concatenate(outs, axis=1).astype(BF16)
    weighted[...] = jnp.concatenate(parts, axis=1)
    total_out[...] = jnp.concatenate(sums, axis=1)


def forward(lengths, place, feat_q, taps, packs):
    n = len(packs)
    wide = HEADS * HS
    return pl.pallas_call(
        functools.partial(forward_body, n),
        out_shape=(
            jax.ShapeDtypeStruct((ROWS, wide), BF16),
            jax.ShapeDtypeStruct((ROWS, wide), F32),
            jax.ShapeDtypeStruct((ROWS, wide), F32),
        ),
        in_specs=[SMEM, SMEM] + [VMEM] * (n + 2),
        out_specs=(VMEM, VMEM, VMEM),
        scratch_shapes=[
            pltpu.VMEM((n, PLANES + HS, HEADS * ROWS), BF16),
            pltpu.VMEM((FEATS, ROWS), BF16),
            pltpu.VMEM((FEATS, ROWS), BF16),
            pltpu.VMEM((FEATS, ROWS), BF16),
            pltpu.VMEM((HEADS, ROWS, HS), F32),
            pltpu.VMEM((HEADS, ROWS, 128), F32),
        ],
        name="attend",
        compiler_params=pltpu.CompilerParams(vmem_limit_bytes=LIMIT),
        cost_estimate=pl.CostEstimate(
            flops=n * 400_000_000, bytes_accessed=4_000_000, transcendentals=0
        ),
    )(lengths, place, feat_q, taps, *packs)


def unit_back(code_grad, tan, raw, planes_t):
    scale = lax.rsqrt(jnp.sum(raw * raw, axis=0, keepdims=True) + UNIT_EPS)
    unit_grad = dot_exact(planes_t, code_grad * (SHARP * (1.0 - tan * tan)))
    inner = jnp.sum(raw * unit_grad, axis=0, keepdims=True)
    return unit_grad * scale - raw * (scale * scale * scale) * inner


def codes_to_raw(dphi, picks, tan, raw, choose_back, planes_t):
    parts = []
    for h in range(HEADS):
        for u in range(2):
            lane = h * ROWS + u * 128
            parts.append(
                expand_back(picks[0:PLANES, lane : lane + 128].astype(F32), dphi.at[h], u * 128, 128)
            )
    pick_grad = jnp.concatenate(parts, axis=1) * (1.0 / HASHES)
    code_grad = dot_exact(choose_back[...], pick_grad)
    return unit_back(code_grad, tan[...], raw[...], planes_t[...])


def query_back_body(
    n, lengths, place, grads, row_totals, pick_q, tan, raw, choose_back, planes_t, *refs
):
    pack_in, (grad_out,) = refs[:n], refs[n : n + 1]
    packs, phi0, phi1, phi2, dphi = refs[n + 1 :]
    phis = (phi0, phi1, phi2)
    mine = place[0]
    for k in range(n):
        packs[k] = pack_in[k][...]
    dphi[...] = jnp.zeros_like(dphi)

    def block(k, carry):
        other = jnp.bitwise_xor(mine, k)

        @pl.when(blocks_meet(mine, other, lengths))
        def _():
            same = same_doc(other * ROWS, ROWS, mine * ROWS, ROWS, lengths)
            for h in range(HEADS):
                lane = h * ROWS
                expand(packs[k, 0:PLANES, lane : lane + ROWS].astype(F32), phis[h])
                values = packs[k, PLANES : PLANES + HS, lane : lane + ROWS].T
                dw = dot_nt(values, grads[:, h * HS : (h + 1) * HS]) + row_totals[h : h + 1, :]
                dw = jnp.where(same, dw, 0.0).astype(BF16)
                dphi[h] += dot(phis[h][...], dw)

        return carry

    lax.fori_loop(0, n, block, 0)
    raw_grad = codes_to_raw(dphi, pick_q, tan, raw, choose_back, planes_t)
    grad_out[...] = heads_on_rows(raw_grad).astype(BF16)


def query_back(lengths, place, grads, row_totals, pick_q, tan, raw, choose_back, planes_t, packs):
    n = len(packs)
    return pl.pallas_call(
        functools.partial(query_back_body, n),
        out_shape=(jax.ShapeDtypeStruct((ROWS, HEADS * HS), BF16),),
        in_specs=[SMEM, SMEM] + [VMEM] * (n + 7),
        out_specs=(VMEM,),
        scratch_shapes=[
            pltpu.VMEM((n, PLANES + HS, HEADS * ROWS), BF16),
            pltpu.VMEM((FEATS, ROWS), BF16),
            pltpu.VMEM((FEATS, ROWS), BF16),
            pltpu.VMEM((FEATS, ROWS), BF16),
            pltpu.VMEM((HEADS, FEATS, ROWS), F32),
        ],
        name="query_back",
        compiler_params=pltpu.CompilerParams(vmem_limit_bytes=LIMIT),
        cost_estimate=pl.CostEstimate(
            flops=n * 400_000_000, bytes_accessed=4_000_000, transcendentals=0
        ),
    )(lengths, place, grads, row_totals, pick_q, tan, raw, choose_back, planes_t, *packs)[0]


def key_back_body(
    n, lengths, place, feat_k, pack, tan, raw, taps_back, choose_back, planes_t, *refs
):
    pick_in, grad_in = refs[:n], refs[n : 2 * n]
    key_out, value_out, taps_out = refs[2 * n : 2 * n + 3]
    picks, grads, phi0, phi1, phi2, dphi, acc = refs[2 * n + 3 :]
    phis = (phi0, phi1, phi2)
    mine = place[0]
    for k in range(n):
        picks[k] = pick_in[k][...]
        grads[k] = grad_in[k][...]
    dphi[...] = jnp.zeros_like(dphi)
    acc[...] = jnp.zeros_like(acc)

    def block(k, carry):
        other = jnp.bitwise_xor(mine, k)

        @pl.when(blocks_meet(mine, other, lengths))
        def _():
            same = same_doc(mine * ROWS, ROWS, other * ROWS, ROWS, lengths)
            same_t = same_doc(other * ROWS, ROWS, mine * ROWS, ROWS, lengths)
            for h in range(HEADS):
                lane = h * ROWS
                expand(picks[k, :, lane : lane + ROWS].astype(F32), phis[h])
                score = dot(feat_k[h], phis[h][...])
                w = jnp.where(same, score * (1.0 / HASHES), 0.0).astype(BF16)
                grad = grads[k, :, h * HS : (h + 1) * HS]
                acc[h] += dot(w, grad)
                values_t = pack[PLANES : PLANES + HS, lane : lane + ROWS]
                side = grads[k, :, 3 * HS : 4 * HS].astype(F32)
                row_total = side[:, h : h + 1] + side[:, 2 * HEADS + h : 2 * HEADS + h + 1]
                dw = dot(grad, values_t) + row_total
                dw = jnp.where(same_t, dw, 0.0).astype(BF16)
                dphi[h] += dot(phis[h][...], dw)

        return carry

    lax.fori_loop(0, n, block, 0)
    raw_grad = codes_to_raw(dphi, pack, tan, raw, choose_back, planes_t)
    key_out[...] = heads_on_rows(raw_grad).astype(BF16)

    before = jnp.bitwise_xor(mine, jnp.maximum(mine - 1, 0))
    after = jnp.bitwise_xor(mine, jnp.minimum(mine + 1, n - 1))
    near = same_doc(mine * ROWS, ROWS, mine * ROWS - 128, 512, lengths)
    ext = jnp.concatenate([grads[before, 128:, :], grads[0], grads[after, :128, :]], axis=0)
    side = ext[:, 3 * HS : 4 * HS].astype(F32)
    near_rev = same_doc(mine * ROWS, ROWS, mine * ROWS - 128, 512, lengths, reverse=True)
    turn = lax.broadcasted_iota(jnp.int32, (512, 512), 0) + lax.broadcasted_iota(
        jnp.int32, (512, 512), 1
    )
    flip = (turn == 511).astype(BF16)
    outs, tap_rows = [], []
    for h in range(HEADS):
        total = side[:, HEADS + h : HEADS + h + 1]
        context_grad = (ext[:, h * HS : (h + 1) * HS].astype(F32) * total).astype(BF16)
        taps_band = jnp.where(near, band(taps_back[h : h + 1, :]), 0.0)
        outs.append(acc[h] + split_dot(taps_band, context_grad, dot))
        flipped = dot(flip, context_grad).astype(BF16)
        values = pack[PLANES : PLANES + HS, h * ROWS : (h + 1) * ROWS].T
        cross = jnp.where(near_rev, dot_nt(values, flipped), 0.0)
        cross = pltpu.roll(cross, 0, 1, stride=1, stride_axis=0)
        tap_rows.append(jnp.sum(cross, axis=0, keepdims=True))
    value_out[...] = jnp.concatenate(outs, axis=1).astype(BF16)
    taps_out[...] = jnp.concatenate(tap_rows + [jnp.zeros((5, 512), F32)], axis=0)


def key_back(lengths, place, feat_k, pack, tan, raw, taps_back, choose_back, planes_t, picks, grads):
    n = len(picks)
    shape = jax.ShapeDtypeStruct((ROWS, HEADS * HS), BF16)
    return pl.pallas_call(
        functools.partial(key_back_body, n),
        out_shape=(shape, shape, jax.ShapeDtypeStruct((8, 512), F32)),
        in_specs=[SMEM, SMEM] + [VMEM] * (2 * n + 7),
        out_specs=(VMEM, VMEM, VMEM),
        scratch_shapes=[
            pltpu.VMEM((n, PLANES, HEADS * ROWS), BF16),
            pltpu.VMEM((n, ROWS, 4 * HS), BF16),
            pltpu.VMEM((FEATS, ROWS), BF16),
            pltpu.VMEM((FEATS, ROWS), BF16),
            pltpu.VMEM((FEATS, ROWS), BF16),
            pltpu.VMEM((HEADS, FEATS, ROWS), F32),
            pltpu.VMEM((HEADS, ROWS, HS), F32),
        ],
        name="key_back",
        compiler_params=pltpu.CompilerParams(vmem_limit_bytes=LIMIT),
        cost_estimate=pl.CostEstimate(
            flops=n * 800_000_000, bytes_accessed=6_000_000, transcendentals=0
        ),
    )(lengths, place, feat_k, pack, tan, raw, taps_back, choose_back, planes_t, *picks, *grads)


def to_all(value, axis):
    n = lax.axis_size(axis)
    return [value] + [
        lax.ppermute(value, axis, [(i, i ^ k) for i in range(n)]) for k in range(1, n)
    ]


def norm_forward(rows, gain, shift):
    center = rows - jnp.mean(rows, axis=-1, keepdims=True)
    inverse = lax.rsqrt(jnp.mean(center * center, axis=-1, keepdims=True) + NORM_EPS)
    normed = center * inverse
    return (normed * gain + shift, normed, inverse)


def norm_backward(grad, normed, inverse, gain):
    scaled = grad * gain
    rows_grad = inverse * (
        scaled
        - jnp.mean(scaled, axis=-1, keepdims=True)
        - normed * jnp.mean(scaled * normed, axis=-1, keepdims=True)
    )
    return (rows_grad, jnp.sum(grad * normed, axis=0), jnp.sum(grad, axis=0))


def on_device(
    tokens,
    query_weight,
    query_shift,
    key_weight,
    key_shift,
    value_weight,
    value_shift,
    mixer_weight,
    mixer_shift,
    conv_taps,
    first_gain,
    first_shift,
    up_weight,
    up_shift,
    down_weight,
    down_shift,
    second_gain,
    second_shift,
    hyperplanes,
    plane_choice,
    doc_lengths,
    out_grad,
):
    place = lax.axis_index("seq").reshape(1).astype(jnp.int32)
    hot = plane_choice.reshape(-1, 1) == jnp.arange(PLANES, dtype=jnp.int32)
    choose = hot.astype(BF16)
    choose_back = hot.astype(F32).T
    planes_t = hyperplanes.T
    raw_q, raw_k, tan_q, tan_k, pick_q, pack = project(
        tokens,
        query_weight,
        query_shift.reshape(1, -1),
        key_weight,
        key_shift.reshape(1, -1),
        value_weight,
        value_shift.reshape(1, -1),
        hyperplanes,
        choose,
    )
    packs = to_all(pack, "seq")
    picks = to_all(pick_q, "seq")
    feat_q, feat_k = local_feats(pick_q, pack)
    side = (TAP_LANE, 512 - TAP_LANE - CONV)
    taps = jnp.pad(conv_taps, ((0, 5), side))
    taps_back = jnp.pad(conv_taps[:, ::-1], ((0, 5), side))
    context, weighted, total = forward(doc_lengths, place, feat_q, taps, packs)
    mixed = (
        lax.psum(jnp.dot(context, mixer_weight, preferred_element_type=jnp.float32), "hid")
        + mixer_shift
    )
    first_out, first_normed, first_inverse = norm_forward(
        tokens.astype(jnp.float32) + mixed, first_gain, first_shift
    )
    first_low = first_out.astype(jnp.bfloat16)
    upward = jnp.dot(first_low, up_weight, preferred_element_type=jnp.float32) + up_shift
    hidden = jax.nn.gelu(upward, approximate=False).astype(jnp.bfloat16)
    downward = (
        lax.psum(jnp.dot(hidden, down_weight, preferred_element_type=jnp.float32), "hid")
        + down_shift
    )
    second_out, second_normed, second_inverse = norm_forward(
        first_out + downward, second_gain, second_shift
    )
    layer_out = second_out.astype(jnp.bfloat16)
    second_grad, second_gains, second_shifts = norm_backward(
        out_grad, second_normed, second_inverse, second_gain
    )
    down_low = second_grad.astype(jnp.bfloat16)
    down_grad = jnp.einsum("rf,rd->fd", hidden, down_low, preferred_element_type=jnp.float32)
    down_offsets = jnp.sum(down_low.astype(jnp.float32), axis=0)
    hidden_grad = jnp.einsum("rd,fd->rf", down_low, down_weight, preferred_element_type=jnp.float32)
    unused, gelu_pull = jax.vjp(
        lambda inner_value: jax.nn.gelu(inner_value, approximate=False), upward
    )
    up_low = gelu_pull(hidden_grad)[0].astype(jnp.bfloat16)
    up_grad = jnp.einsum("rd,rf->df", first_low, up_low, preferred_element_type=jnp.float32)
    up_offsets = jnp.sum(up_low.astype(jnp.float32), axis=0)
    first_back = (
        lax.psum(
            jnp.einsum("rf,df->rd", up_low, up_weight, preferred_element_type=jnp.float32), "hid"
        )
        + second_grad
    )
    first_grad, first_gains, first_shifts = norm_backward(
        first_back, first_normed, first_inverse, first_gain
    )
    mixed_low = first_grad.astype(jnp.bfloat16)
    mixer_grad = jnp.einsum("rc,rd->cd", context, mixed_low, preferred_element_type=jnp.float32)
    mixer_offsets = jnp.sum(mixed_low.astype(jnp.float32), axis=0)
    context_grad = jnp.einsum(
        "rd,cd->rc", mixed_low, mixer_weight, preferred_element_type=jnp.float32
    )
    weighted_grad = (context_grad / total).astype(BF16)
    total3 = total.reshape(ROWS, HEADS, HS)[:, :, 0]
    total_grad = -jnp.sum((context_grad * weighted).reshape(ROWS, HEADS, HS), axis=-1) / (
        total3 * total3
    )
    grad_high = total_grad.astype(BF16)
    grad_low = (total_grad - grad_high.astype(F32)).astype(BF16)
    grad_pack = jnp.concatenate(
        [weighted_grad, grad_high, total3.astype(BF16), grad_low, jnp.zeros((ROWS, 55), BF16)], axis=1
    )
    grad_packs = to_all(grad_pack, "seq")
    query_low = query_back(
        doc_lengths,
        place,
        weighted_grad,
        jnp.pad(total_grad.T, ((0, 5), (0, 0))),
        pick_q,
        tan_q,
        raw_q,
        choose_back,
        planes_t,
        packs,
    )
    key_low, value_grad_low, tap_rows = key_back(
        doc_lengths, place, feat_k, pack, tan_k, raw_k, taps_back, choose_back, planes_t, picks, grad_packs
    )
    taps_grad = tap_rows[:HEADS, 366 : 366 + CONV]

    def weight_grad(grad_low):
        return jnp.einsum("rd,rc->dc", tokens, grad_low, preferred_element_type=jnp.float32)

    def back_input(grad_low, weight):
        return jnp.einsum("rc,dc->rd", grad_low, weight, preferred_element_type=jnp.float32)

    tokens_grad = (
        lax.psum(
            (
                back_input(query_low, query_weight)
                + back_input(key_low, key_weight)
                + back_input(value_grad_low, value_weight)
            ).astype(jnp.bfloat16),
            "hid",
        ).astype(jnp.float32)
        + first_grad
    )
    summed = (
        lax.psum(weight_grad(query_low).astype(jnp.bfloat16), "seq").astype(jnp.float32),
        lax.psum(jnp.sum(query_low.astype(jnp.float32), axis=0).astype(jnp.bfloat16), "seq").astype(
            jnp.float32
        ),
        lax.psum(weight_grad(key_low).astype(jnp.bfloat16), "seq").astype(jnp.float32),
        lax.psum(jnp.sum(key_low.astype(jnp.float32), axis=0).astype(jnp.bfloat16), "seq").astype(
            jnp.float32
        ),
        lax.psum(weight_grad(value_grad_low).astype(jnp.bfloat16), "seq").astype(jnp.float32),
        lax.psum(
            jnp.sum(value_grad_low.astype(jnp.float32), axis=0).astype(jnp.bfloat16), "seq"
        ).astype(jnp.float32),
        lax.psum(mixer_grad.astype(jnp.bfloat16), "seq").astype(jnp.float32),
        lax.psum(mixer_offsets.astype(jnp.bfloat16), "seq").astype(jnp.float32),
        lax.psum(taps_grad.astype(jnp.bfloat16), "seq").astype(jnp.float32),
        lax.psum(first_gains.astype(jnp.bfloat16), "seq").astype(jnp.float32),
        lax.psum(first_shifts.astype(jnp.bfloat16), "seq").astype(jnp.float32),
        lax.psum(up_grad.astype(jnp.bfloat16), "seq").astype(jnp.float32),
        lax.psum(up_offsets.astype(jnp.bfloat16), "seq").astype(jnp.float32),
        lax.psum(down_grad.astype(jnp.bfloat16), "seq").astype(jnp.float32),
        lax.psum(down_offsets.astype(jnp.bfloat16), "seq").astype(jnp.float32),
        lax.psum(second_gains.astype(jnp.bfloat16), "seq").astype(jnp.float32),
        lax.psum(second_shifts.astype(jnp.bfloat16), "seq").astype(jnp.float32),
    )
    return (
        layer_out,
        tokens_grad,
        summed[0],
        summed[1],
        summed[2],
        summed[3],
        summed[4],
        summed[5],
        summed[6],
        summed[7],
        summed[8],
        summed[9],
        summed[10],
        summed[11],
        summed[12],
        summed[13],
        summed[14],
        summed[15],
        summed[16],
    )


def solution(mesh):
    placed = (
        P("seq", None),
        P(None, "hid"),
        P("hid"),
        P(None, "hid"),
        P("hid"),
        P(None, "hid"),
        P("hid"),
        P("hid", None),
        P(),
        P("hid", None),
        P(),
        P(),
        P(None, "hid"),
        P("hid"),
        P("hid", None),
        P(),
        P(),
        P(),
        P(),
        P(),
        P(),
        P("seq", None),
    )
    return jax.shard_map(
        on_device,
        mesh=mesh,
        in_specs=placed,
        out_specs=(
            P("seq", None),
            P("seq", None),
            P(None, "hid"),
            P("hid"),
            P(None, "hid"),
            P("hid"),
            P(None, "hid"),
            P("hid"),
            P("hid", None),
            P(),
            P("hid", None),
            P(),
            P(),
            P(None, "hid"),
            P("hid"),
            P("hid", None),
            P(),
            P(),
            P(),
        ),
        check_vma=False,
    )
```

```python
import functools
import math

import jax
import jax.numpy as jnp
from jax import lax
from jax.experimental import pallas as pl
from jax.experimental.pallas import tpu as pltpu
from jax.sharding import PartitionSpec as P

D = 768
H = 12
HS = 64
BITS = 8
PLANES = 32
HASHES = 4
CONV = 35
RADIUS = 17
FEATS = HASHES * 2**BITS
SHARP = 2.0
NORM_EPS = 1e-05
UNIT_EPS = 1e-06
EXACT = lax.Precision.HIGHEST
F32 = jnp.float32
BF16 = jnp.bfloat16
ROWS = 256
HEADS = 3
TAP_LANE = 111
VMEM = pl.BlockSpec(memory_space=pltpu.VMEM)
SMEM = pl.BlockSpec(memory_space=pltpu.SMEM)
LIMIT = 60 * 1024 * 1024


def dot(a, b):
    return lax.dot_general(a, b, (((1,), (0,)), ((), ())), preferred_element_type=F32)


def dot_nt(a, b):
    return lax.dot_general(a, b, (((1,), (1,)), ((), ())), preferred_element_type=F32)


def dot_exact(a, b):
    return lax.dot_general(
        a, b, (((1,), (0,)), ((), ())), precision=EXACT, preferred_element_type=F32
    )


def doc_count(pos, lengths):
    start = jnp.int32(0)
    found = jnp.zeros_like(pos)
    for d in range(lengths.shape[0]):
        found = found + (pos >= start).astype(jnp.int32)
        start = start + lengths[d]
    return found + (pos >= start).astype(jnp.int32)


def blocks_meet(mine, other, lengths):
    a0 = doc_count(mine * ROWS, lengths)
    a1 = doc_count(mine * ROWS + (ROWS - 1), lengths)
    b0 = doc_count(other * ROWS, lengths)
    b1 = doc_count(other * ROWS + (ROWS - 1), lengths)
    return jnp.logical_and(a0 <= b1, b0 <= a1)


def same_doc(row_start, rows, col_start, cols, lengths, reverse=False):
    rid = row_start + lax.broadcasted_iota(jnp.int32, (rows, 1), 0)
    cid = lax.broadcasted_iota(jnp.int32, (1, cols), 1)
    cid = col_start + ((cols - 1) - cid if reverse else cid)
    return doc_count(rid, lengths) == doc_count(cid, lengths)


def hash_base(picks, m, lanes):
    bit = lax.broadcasted_iota(jnp.int32, (8, lanes), 0)
    factors = []
    for b in range(3):
        on = (bit & (1 << b)) != 0
        row = jnp.broadcast_to(picks[m * BITS + b : m * BITS + b + 1, :], (8, lanes))
        factors.append((on, jnp.where(on, row, 1.0)))
    return factors


def hash_feats(picks, m, lanes):
    factors = hash_base(picks, m, lanes)
    scale = 2.0 ** (-0.5 * BITS)
    feats = [(factors[0][1] * scale) * (factors[1][1] * factors[2][1])]
    rows = {}
    for b in range(3, BITS):
        rows[b] = jnp.broadcast_to(picks[m * BITS + b : m * BITS + b + 1, :], (8, lanes))
        feats = feats + [f * rows[b] for f in feats]
    return feats, rows, factors


def expand(picks, phi_ref):
    lanes = picks.shape[1]
    for m in range(HASHES):
        feats = hash_feats(picks, m, lanes)[0]
        for i in range(0, len(feats), 2):
            both = jnp.concatenate([feats[i], feats[i + 1]], axis=0)
            phi_ref[m * 256 + i * 8 : m * 256 + i * 8 + 16, :] = both.astype(BF16)


def expand_back(picks, dphi_ref, lane0, lanes):
    out = []
    scale = 2.0 ** (-0.5 * BITS)
    for m in range(HASHES):
        feats, rows, factors = hash_feats(picks, m, lanes)
        grads = [
            dphi_ref[m * 256 + i * 8 : m * 256 + i * 8 + 8, lane0 : lane0 + lanes]
            for i in range(32)
        ]
        found = {}
        for b in range(BITS - 1, 2, -1):
            half = len(grads) // 2
            total = grads[half] * feats[0]
            for i in range(1, half):
                total = total + grads[half + i] * feats[i]
            found[b] = jnp.sum(total, axis=0, keepdims=True)
            grads = [grads[i] + grads[half + i] * rows[b] for i in range(half)]
        g = grads[0] * scale
        (on0, f0), (on1, f1), (on2, f2) = factors
        found[0] = jnp.sum(jnp.where(on0, g * (f1 * f2), 0.0), axis=0, keepdims=True)
        found[1] = jnp.sum(jnp.where(on1, g * (f0 * f2), 0.0), axis=0, keepdims=True)
        found[2] = jnp.sum(jnp.where(on2, g * (f0 * f1), 0.0), axis=0, keepdims=True)
        out.extend(found[b] for b in range(BITS))
    return jnp.concatenate(out, axis=0)


def stacked(turned):
    return jnp.concatenate([turned[:, h * ROWS : (h + 1) * ROWS] for h in range(HEADS)], axis=0)


def column(row):
    n = row.shape[1]
    here = lax.broadcasted_iota(jnp.int32, (n, n), 0) == lax.broadcasted_iota(jnp.int32, (n, n), 1)
    return jnp.sum(jnp.where(here, row, 0.0), axis=1, keepdims=True)


def beside(rows):
    return jnp.concatenate([rows[h * HS : (h + 1) * HS] for h in range(HEADS)], axis=1)


def project_body(
    tokens, wq, bq, wk, bk, wv, bv, planes, choose, raw_q, raw_k, tan_q, tan_k, pick_q, pack
):
    x = tokens[...]

    def codes(w, b, raw_ref, tan_ref):
        raw = beside(dot_nt(w[...], x) + column(b[...].reshape(1, -1)))
        raw_ref[...] = raw
        unit = raw * lax.rsqrt(jnp.sum(raw * raw, axis=0, keepdims=True) + UNIT_EPS)
        tan = jnp.tanh(SHARP * dot_exact(planes[...], unit))
        tan_ref[...] = tan
        return dot(choose[...], tan.astype(BF16)).astype(BF16)

    pack[0:PLANES, :] = codes(wk, bk, raw_k, tan_k)
    values = beside(dot_nt(wv[...], x) + column(bv[...].reshape(1, -1)))
    pack[PLANES : PLANES + HS, :] = values.astype(BF16)
    pick_q[...] = codes(wq, bq, raw_q, tan_q)


def call(body, name, out_shape, ins, smem=0, scratch=(), us=2):
    single = not isinstance(out_shape, (tuple, list))
    outs = (out_shape,) if single else tuple(out_shape)
    got = pl.pallas_call(
        body,
        out_shape=outs,
        in_specs=[SMEM] * smem + [VMEM] * (len(ins) - smem),
        out_specs=tuple([VMEM] * len(outs)),
        scratch_shapes=list(scratch),
        name=name,
        compiler_params=pltpu.CompilerParams(vmem_limit_bytes=LIMIT),
        cost_estimate=pl.CostEstimate(
            flops=int(us * 1e9), bytes_accessed=100_000, transcendentals=0
        ),
    )(*ins)
    return got[0] if single else got


def f32(*shape):
    return jax.ShapeDtypeStruct(shape, F32)


def bf16(*shape):
    return jax.ShapeDtypeStruct(shape, BF16)


def project(*ins):
    wide = HEADS * ROWS
    return call(
        project_body,
        "project",
        (
            f32(HS, wide),
            f32(HS, wide),
            f32(PLANES, wide),
            f32(PLANES, wide),
            bf16(PLANES, wide),
            bf16(PLANES + HS, wide),
        ),
        ins,
        us=3,
    )


def local_feats_body(pick_q, pack, feat_q, feat_k, phi):
    for src, dst in ((pick_q, feat_q), (pack, feat_k)):
        for h in range(HEADS):
            picks = src[0:PLANES, h * ROWS : (h + 1) * ROWS].astype(F32)
            expand(picks, phi)
            dst[h] = phi[...].T


def local_feats(pick_q, pack):
    shape = bf16(HEADS, ROWS, FEATS)
    return call(
        local_feats_body,
        "local_feats",
        (shape, shape),
        (pick_q, pack),
        scratch=(pltpu.VMEM((FEATS, ROWS), BF16),),
        us=3,
    )


def window(packs, mine, low, high, n):
    def at(h):
        before = jnp.bitwise_xor(mine, jnp.maximum(mine - 1, 0))
        after = jnp.bitwise_xor(mine, jnp.minimum(mine + 1, n - 1))
        lane = h * ROWS
        return jnp.concatenate(
            [
                packs[before, low:high, lane + 128 : lane + 256],
                packs[0, low:high, lane : lane + 256],
                packs[after, low:high, lane : lane + 128],
            ],
            axis=1,
        )

    return at


def band(row):
    return pltpu.roll(jnp.broadcast_to(row, (ROWS, 512)), 0, 1, stride=1, stride_axis=0)


def split_dot(a, b, mul):
    high = a.astype(BF16)
    low = (a - high.astype(F32)).astype(BF16)
    return mul(high, b) + mul(low, b)


def forward_body(n, lengths, place, slot, feat_q, taps, *refs):
    pack_in, (context, near_half, far_half, weighted, total_out) = refs[:n], refs[n : n + 5]
    packs, phi0, phi1, phi2, acc, tot = refs[n + 5 :]
    phis = (phi0, phi1, phi2)
    mine = place[0]
    for k in range(n):
        packs[k] = pack_in[k][...]
    acc[...] = jnp.zeros_like(acc)
    tot[...] = jnp.zeros_like(tot)

    def block(k, carry):
        other = jnp.bitwise_xor(mine, k)

        @pl.when(blocks_meet(mine, other, lengths))
        def _():
            same = same_doc(mine * ROWS, ROWS, other * ROWS, ROWS, lengths)
            for h in range(HEADS):
                lane = h * ROWS
                expand(packs[k, 0:PLANES, lane : lane + ROWS].astype(F32), phis[h])
                score = dot(feat_q[h], phis[h][...])
                w = jnp.where(same, score * (1.0 / HASHES), 0.0)
                tot[h] += w[:, :128] + w[:, 128:]
                acc[h] += dot_nt(w.astype(BF16), packs[k, PLANES : PLANES + HS, lane : lane + ROWS])

        return carry

    lax.fori_loop(0, n, block, 0)
    near = same_doc(mine * ROWS, ROWS, mine * ROWS - 128, 512, lengths)
    ext = window(packs, mine, PLANES, PLANES + HS, n)
    outs, sums, parts = [], [], []
    for h in range(HEADS):
        total = 1.0 + jnp.sum(tot[h], axis=1, keepdims=True)
        taps_band = jnp.where(near, band(taps[h : h + 1, :]), 0.0)
        conv = split_dot(taps_band, ext(h), dot_nt)
        sums.append(jnp.broadcast_to(total, (ROWS, HS)))
        parts.append(acc[h])
        outs.append(acc[h] / total + conv)
    context[...] = jnp.concatenate(outs, axis=1).astype(BF16)
    half = ROWS // 2
    first = slot[0] >> 1
    near_half[...] = context[pl.ds(pl.multiple_of(first * half, 16), half), :]
    far_half[...] = context[pl.ds(pl.multiple_of((1 - first) * half, 16), half), :]
    weighted[...] = jnp.concatenate(parts, axis=1)
    total_out[...] = jnp.concatenate(sums, axis=1)


def forward(lengths, place, slot, feat_q, taps, packs):
    n = len(packs)
    wide = HEADS * HS
    return call(
        functools.partial(forward_body, n),
        "attend",
        (
            bf16(ROWS, wide),
            bf16(ROWS // 2, wide),
            bf16(ROWS // 2, wide),
            f32(ROWS, wide),
            f32(ROWS, wide),
        ),
        (lengths, place, slot, feat_q, taps, *packs),
        smem=3,
        scratch=(
            pltpu.VMEM((n, PLANES + HS, HEADS * ROWS), BF16),
            pltpu.VMEM((FEATS, ROWS), BF16),
            pltpu.VMEM((FEATS, ROWS), BF16),
            pltpu.VMEM((FEATS, ROWS), BF16),
            pltpu.VMEM((HEADS, ROWS, HS), F32),
            pltpu.VMEM((HEADS, ROWS, 128), F32),
        ),
        us=9,
    )


def unit_back(code_grad, tan, raw, planes_t):
    scale = lax.rsqrt(jnp.sum(raw * raw, axis=0, keepdims=True) + UNIT_EPS)
    unit_grad = dot_exact(planes_t, code_grad * (SHARP * (1.0 - tan * tan)))
    inner = jnp.sum(raw * unit_grad, axis=0, keepdims=True)
    return unit_grad * scale - raw * (scale * scale * scale) * inner


def codes_to_raw(dphi, picks, tan, raw, choose_back, planes_t):
    parts = []
    for h in range(HEADS):
        for u in range(2):
            lane = h * ROWS + u * 128
            parts.append(
                expand_back(picks[0:PLANES, lane : lane + 128].astype(F32), dphi.at[h], u * 128, 128)
            )
    pick_grad = jnp.concatenate(parts, axis=1) * (1.0 / HASHES)
    code_grad = dot_exact(choose_back[...], pick_grad)
    return unit_back(code_grad, tan[...], raw[...], planes_t[...])


def query_back_body(
    n, lengths, place, grads, row_totals, pick_q, tan, raw, choose_back, planes_t, weight, *refs
):
    pack_in, (grad_out, input_out, taps_out) = refs[:n], refs[n : n + 3]
    packs, phi0, phi1, phi2, dphi = refs[n + 3 :]
    phis = (phi0, phi1, phi2)
    mine = place[0]
    for k in range(n):
        packs[k] = pack_in[k][...]
    dphi[...] = jnp.zeros_like(dphi)

    def block(k, carry):
        other = jnp.bitwise_xor(mine, k)

        @pl.when(blocks_meet(mine, other, lengths))
        def _():
            same = same_doc(other * ROWS, ROWS, mine * ROWS, ROWS, lengths)
            for h in range(HEADS):
                lane = h * ROWS
                expand(packs[k, 0:PLANES, lane : lane + ROWS].astype(F32), phis[h])
                values = packs[k, PLANES : PLANES + HS, lane : lane + ROWS].T
                dw = dot_nt(values, grads[:, h * HS : (h + 1) * HS]) + row_totals[h : h + 1, :]
                dw = jnp.where(same, dw, 0.0).astype(BF16)
                dphi[h] += dot(phis[h][...], dw)

        return carry

    lax.fori_loop(0, n, block, 0)
    raw_grad = codes_to_raw(dphi, pick_q, tan, raw, choose_back, planes_t)
    turned = stacked(raw_grad).astype(BF16)
    grad_out[...] = turned
    input_out[...] = dot(turned.astype(F32).T.astype(BF16), weight[...])
    near_rev = same_doc(mine * ROWS, ROWS, mine * ROWS - 128, 512, lengths, reverse=True)
    turn = lax.broadcasted_iota(jnp.int32, (512, 512), 0) + lax.broadcasted_iota(
        jnp.int32, (512, 512), 1
    )
    flip = (turn == 511).astype(F32)
    flip_low = flip.astype(BF16)
    ext = window(packs, mine, PLANES, PLANES + HS, n)
    side = grads[:, 3 * HS : 4 * HS].astype(F32)
    tap_rows = []
    for h in range(HEADS):
        total = side[:, HEADS + h : HEADS + h + 1]
        context_grad = (grads[:, h * HS : (h + 1) * HS].astype(F32) * total).astype(BF16)
        flipped = dot(ext(h), flip_low).astype(BF16)
        cross = jnp.where(near_rev, dot(context_grad, flipped), 0.0)
        cross = pltpu.roll(cross, 0, 1, stride=1, stride_axis=0)
        tap_rows.append(jnp.sum(cross, axis=0, keepdims=True))
    tap_rows.append(jnp.zeros((8 - HEADS, 512), F32))
    taps_out[...] = dot_exact(jnp.concatenate(tap_rows, axis=0), flip)


def query_back(*ins):
    packs = ins[-1]
    n = len(packs)
    return call(
        functools.partial(query_back_body, n),
        "query_back",
        (bf16(HEADS * HS, ROWS), f32(ROWS, D), f32(8, 512)),
        (*ins[:-1], *packs),
        smem=2,
        scratch=(
            pltpu.VMEM((n, PLANES + HS, HEADS * ROWS), BF16),
            pltpu.VMEM((FEATS, ROWS), BF16),
            pltpu.VMEM((FEATS, ROWS), BF16),
            pltpu.VMEM((FEATS, ROWS), BF16),
            pltpu.VMEM((HEADS, FEATS, ROWS), F32),
        ),
        us=9,
    )


def key_back_body(
    n,
    parts,
    lengths,
    place,
    slot,
    feat_k,
    pack,
    tan,
    raw,
    taps_back,
    choose_back,
    planes_t,
    wk,
    wv,
    query_input,
    *refs,
):
    pick_in, grad_in = refs[:n], refs[n : 2 * n]
    turned_out = refs[2 * n]
    input_out = refs[2 * n + 1 : 2 * n + 1 + parts]
    picks, grads, phi0, phi1, phi2, dphi, acc, inputs = refs[2 * n + 1 + parts :]
    phis = (phi0, phi1, phi2)
    mine = place[0]
    for k in range(n):
        picks[k] = pick_in[k][...]
        grads[k] = grad_in[k][...]
    dphi[...] = jnp.zeros_like(dphi)
    acc[...] = jnp.zeros_like(acc)

    def block(k, carry):
        other = jnp.bitwise_xor(mine, k)

        @pl.when(blocks_meet(mine, other, lengths))
        def _():
            same = same_doc(mine * ROWS, ROWS, other * ROWS, ROWS, lengths)
            same_t = same_doc(other * ROWS, ROWS, mine * ROWS, ROWS, lengths)
            for h in range(HEADS):
                lane = h * ROWS
                expand(picks[k, :, lane : lane + ROWS].astype(F32), phis[h])
                score = dot(feat_k[h], phis[h][...])
                w = jnp.where(same, score * (1.0 / HASHES), 0.0).astype(BF16)
                grad = grads[k, :, h * HS : (h + 1) * HS]
                acc[h] += dot(w, grad)
                values_t = pack[PLANES : PLANES + HS, lane : lane + ROWS]
                side = grads[k, :, 3 * HS : 4 * HS].astype(F32)
                row_total = side[:, h : h + 1] + side[:, 2 * HEADS + h : 2 * HEADS + h + 1]
                dw = dot(grad, values_t) + row_total
                dw = jnp.where(same_t, dw, 0.0).astype(BF16)
                dphi[h] += dot(phis[h][...], dw)

        return carry

    lax.fori_loop(0, n, block, 0)
    raw_grad = codes_to_raw(dphi, pack, tan, raw, choose_back, planes_t)
    key_turned = stacked(raw_grad).astype(BF16)
    key_rows = key_turned.astype(F32).T

    before = jnp.bitwise_xor(mine, jnp.maximum(mine - 1, 0))
    after = jnp.bitwise_xor(mine, jnp.minimum(mine + 1, n - 1))
    near = same_doc(mine * ROWS, ROWS, mine * ROWS - 128, 512, lengths)
    ext = jnp.concatenate([grads[before, 128:, :], grads[0], grads[after, :128, :]], axis=0)
    side = ext[:, 3 * HS : 4 * HS].astype(F32)
    outs = []
    for h in range(HEADS):
        total = side[:, HEADS + h : HEADS + h + 1]
        context_grad = (ext[:, h * HS : (h + 1) * HS].astype(F32) * total).astype(BF16)
        taps_band = jnp.where(near, band(taps_back[h : h + 1, :]), 0.0)
        outs.append(acc[h] + split_dot(taps_band, context_grad, dot))
    value_rows = jnp.concatenate(outs, axis=1).astype(BF16)
    wide = HEADS * HS
    turned_out[0:wide, :] = key_turned
    turned_out[wide : 2 * wide, :] = value_rows.astype(F32).T.astype(BF16)
    inputs[...] = (
        query_input[...] + dot(key_rows.astype(BF16), wk[...]) + dot(value_rows, wv[...])
    ).astype(BF16)
    put_chunks(slot[0], inputs, input_out)


def key_back(ins, picks, grads, parts):
    n = len(picks)
    return call(
        functools.partial(key_back_body, n, parts),
        "key_back",
        (bf16(2 * HEADS * HS, ROWS), *[bf16(ROWS // parts, D)] * parts),
        (*ins, *picks, *grads),
        smem=3,
        scratch=(
            pltpu.VMEM((n, PLANES, HEADS * ROWS), BF16),
            pltpu.VMEM((n, ROWS, 4 * HS), BF16),
            pltpu.VMEM((FEATS, ROWS), BF16),
            pltpu.VMEM((FEATS, ROWS), BF16),
            pltpu.VMEM((FEATS, ROWS), BF16),
            pltpu.VMEM((HEADS, FEATS, ROWS), F32),
            pltpu.VMEM((HEADS, ROWS, HS), F32),
            pltpu.VMEM((ROWS, D), BF16),
        ),
        us=15,
    )


def padded(rows, n):
    return -(-rows // (16 * n)) * (16 * n)


def put_halves(place, whole, mine, other):
    half = whole.shape[0] // 2
    core = place & 1
    mine[...] = whole[pl.ds(pl.multiple_of(core * half, 16), half), :]
    other[...] = whole[pl.ds(pl.multiple_of((1 - core) * half, 16), half), :]


def put_chunks(index, whole, outs):
    rows = outs[0].shape[0]
    for k, out in enumerate(outs):
        start = pl.multiple_of(jnp.bitwise_xor(index, k) * rows, 16)
        out[...] = whole[pl.ds(start, rows), :]


def swap(value, axis, k):
    n = lax.axis_size(axis)
    return lax.ppermute(value, axis, [(i, i ^ k) for i in range(n)])


def over_seq(value):
    n = lax.axis_size("seq")
    got = [value] + [None] * (n - 1)
    for k in range(2, n, 2):
        got[k] = swap(value, "seq", k)
    for k in range(0, n, 2):
        got[k + 1] = swap(got[k], "seq", 1)
    return got


HID_ORDER = (0, 2, 1, 3)


def hid_swap(value, j):
    return swap(value, "hid", HID_ORDER[j])


def over_hid(value):
    return [value] + [hid_swap(value, j) for j in range(1, len(HID_ORDER))]


def exchange(chunks):
    return [chunks[0]] + [hid_swap(chunks[j], j) for j in range(1, len(chunks))]


def flat(ref):
    return ref[...].reshape(1, -1)


def norm_stats(rows):
    center = rows - jnp.mean(rows, axis=-1, keepdims=True)
    inverse = lax.rsqrt(jnp.mean(center * center, axis=-1, keepdims=True) + NORM_EPS)
    return center * inverse, inverse


def norm_grad(grad, normed, inverse, gain):
    scaled = grad * gain
    return inverse * (
        scaled
        - jnp.mean(scaled, axis=-1, keepdims=True)
        - normed * jnp.mean(scaled * normed, axis=-1, keepdims=True)
    )


def column_sums(*rows):
    sums = [jnp.sum(r, axis=0, keepdims=True) for r in rows]
    return jnp.concatenate(sums + [jnp.zeros((8 - len(sums), D), F32)], axis=0)


def two_parts(sums):
    high = sums.astype(BF16).astype(F32)
    return jnp.concatenate([high, sums - high], axis=0).astype(BF16)


def partner_weights(core, got, other, both):
    both[core] = got[...]
    both[1 - core] = other[...]


def gelu_parts(x):
    cdf = 0.5 * (1.0 + lax.erf(x * math.sqrt(0.5)))
    slope = cdf + x * (jnp.exp(-0.5 * x * x) * (1.0 / math.sqrt(2.0 * math.pi)))
    return (x * cdf).astype(BF16), slope


def keep_and_send(partial, quarter, keep, send):
    rows = keep.shape[0]
    keep[...] = partial[pl.ds(pl.multiple_of(quarter * rows, 8), rows), :]
    other = pl.multiple_of((1 - quarter) * rows, 8)
    send[...] = partial[pl.ds(other, rows), :].astype(BF16)


def feed_body(parts, place, slot, *refs):
    tokens, mixer_shift, gain, shift, up, up_shift, down, got, other, far_shift = refs[:10]
    contexts, mixers = refs[10 : 10 + parts], refs[10 + parts : 10 + 2 * parts]
    first_mine, normed_mine, inverse_mine, low_out, slope_out, keep, send = refs[
        10 + 2 * parts : 17 + 2 * parts
    ]
    first, normed, inverse, partial, both = refs[17 + 2 * parts :]
    half = ROWS // 2
    partner_weights(place[0] & 1, got, other, both)
    mine = tokens[pl.ds(pl.multiple_of((slot[0] >> 1) * half, 16), half), :]
    mixed = flat(mixer_shift) + mine.astype(F32)
    for c, m in zip(contexts, mixers):
        mixed = mixed + dot(c[...], m[...])
    n1, r1 = norm_stats(mixed)
    rows1 = n1 * flat(gain) + flat(shift)
    first[...] = rows1
    normed[...] = n1
    inverse[...] = jnp.broadcast_to(r1, inverse.shape)
    low = rows1.astype(BF16)
    low_out[...] = low
    hidden, slope = gelu_parts(dot(low, up[...]) + flat(up_shift))
    slope_out[:, 0:D] = slope
    far_hidden, far_slope = gelu_parts(dot(low, both[0]) + flat(far_shift))
    slope_out[:, D:] = far_slope
    partial[...] = dot(hidden, down[...]) + dot(far_hidden, both[1])
    quarter = slot[0] & 1
    keep_and_send(partial, quarter, keep, send)
    rows = first_mine.shape[0]
    start = pl.multiple_of(quarter * rows, 8)
    first_mine[...] = first[pl.ds(start, rows), :]
    normed_mine[...] = normed[pl.ds(start, rows), :]
    inverse_mine[...] = inverse[pl.ds(start, rows), :]


def second_body(slot, first, out_grad, down_shift, gain, shift, keep, got, layer, grad_out, low_out):
    rows = first.shape[0]
    total = first[...] + flat(down_shift) + keep[...] + got[...].astype(F32)
    n2, r2 = norm_stats(total)
    grad = out_grad[pl.ds(pl.multiple_of(slot[0] * rows, 8), rows), :]
    dh2 = norm_grad(grad, n2, r2, flat(gain))
    grad_out[...] = dh2
    low = dh2.astype(BF16)
    low_out[...] = low
    layer[0:rows, :] = (n2 * flat(gain) + flat(shift)).astype(BF16)
    layer[rows:, :] = two_parts(column_sums(grad * n2, grad, low.astype(F32)))


def feed_back_body(place, slot, slope, up, down, got, other, low_mine, low_got, low_half, keep, send, partial, both):
    partner_weights(place[0] & 1, got, other, both)
    quarter = slot[0] & 1
    take_chunks(quarter, (low_mine, low_got), low_half)
    low = low_half[...]
    near = (dot_nt(low, down[...]) * slope[:, 0:D]).astype(BF16)
    far = (dot_nt(low, both[1]) * slope[:, D:]).astype(BF16)
    partial[...] = dot_nt(near, up[...]) + dot_nt(far, both[0])
    keep_and_send(partial, quarter, keep, send)


def take_chunks(index, pieces, whole):
    rows = whole.shape[0] // len(pieces)
    for k, piece in enumerate(pieces):
        start = pl.multiple_of(jnp.bitwise_xor(index, k) * rows, 16)
        whole[pl.ds(start, rows), :] = piece[0:rows, :]


def first_back_body(parts, grad, normed, inverse, gain, keep, got, *refs):
    mixers = refs[:parts]
    dh1_out, payload = refs[parts : parts + 2]
    outs = refs[parts + 2 :]
    total = grad[...] + keep[...] + got[...].astype(F32)
    n1 = normed[...]
    dh1 = norm_grad(total, n1, inverse[:, 0:1], flat(gain))
    dh1_out[...] = dh1
    low = dh1.astype(BF16)
    rows = dh1.shape[0]
    payload[0:rows, :] = low
    payload[rows:, :] = two_parts(column_sums(total * n1, total, low.astype(F32)))
    for m, out in zip(mixers, outs):
        out[...] = dot_nt(low, m[...]).astype(BF16)


def split_body(parts, chunk, weighted, total, *refs):
    pieces, (grad_pack, row_totals), (whole,) = refs[:parts], refs[parts : parts + 2], refs[parts + 2 :]
    take_chunks(chunk[0], pieces, whole)
    dctx = whole[...].astype(F32)
    wide = HEADS * HS
    each = total[...]
    grad_pack[:, 0:wide] = (dctx / each).astype(BF16)
    product = dctx * weighted[...]
    cols = []
    for h in range(HEADS):
        norm = each[:, h * HS : h * HS + 1]
        inner = jnp.sum(product[:, h * HS : (h + 1) * HS], axis=1, keepdims=True)
        cols.append((-inner / (norm * norm), norm))
    lane = lax.broadcasted_iota(jnp.int32, (ROWS, 128), 1)
    side = jnp.zeros((ROWS, 128), F32)
    for h, (grad, norm) in enumerate(cols):
        high = grad.astype(BF16).astype(F32)
        side = jnp.where(lane == h, high, side)
        side = jnp.where(lane == HEADS + h, norm, side)
        side = jnp.where(lane == 2 * HEADS + h, grad - high, side)
        side = jnp.where(lane == 64 + h, grad, side)
    grad_pack[:, wide : wide + 64] = side[:, 0:64].astype(BF16)
    row_totals[...] = side.T[64:72, :]


def feed_grads_body(place, slot, low_mine, low_got, down_mine, down_got, up, up_shift, down, half_mine, half_other, sums, low_all, down_all, whole):
    take_chunks(slot[0] >> 1, (low_mine, low_got), low_all)
    take_chunks(slot[0] >> 1, (down_mine, down_got), down_all)
    low, grad = low_all[...], down_all[...]
    hidden, slope = gelu_parts(dot(low, up[...]) + flat(up_shift))
    up_low = (dot_nt(grad, down[...]) * slope).astype(BF16)
    ff = hidden.shape[1]
    whole[0:ff, :] = dot(hidden.T, grad).astype(BF16)
    whole[ff:, :] = dot(low.T, up_low).astype(BF16)
    put_halves(place[0], whole, half_mine, half_other)
    sums[...] = jnp.broadcast_to(jnp.sum(up_low.astype(F32), axis=0, keepdims=True), sums.shape)


def mixer_grads_body(parts, place, slot, context, up_sums, taps, *refs):
    layers, payloads = refs[:parts], refs[parts : 2 * parts]
    half_mine, half_other, layer_out, whole, mixed = refs[2 * parts :]
    wide = HEADS * HS
    take_chunks(slot[0], layers, layer_out)
    take_chunks(slot[0], payloads, mixed)
    rows = ROWS // parts

    def summed(refs):
        total = jnp.zeros((8, D), F32)
        for r in refs:
            total = total + r[rows : rows + 8, :].astype(F32) + r[rows + 8 : rows + 16, :].astype(F32)
        return total

    context_t = context[...].astype(F32).T.astype(BF16)
    whole[0:wide, :] = dot(context_t, mixed[...]).astype(BF16)
    tap_block = jnp.concatenate([taps[0:HEADS, :], jnp.zeros((HEADS, D - 512), F32)], axis=1)
    small = jnp.concatenate(
        [summed(layers)[0:3], summed(payloads)[0:3], up_sums[0:1, :], tap_block, jnp.zeros((6, D), F32)],
        axis=0,
    )
    whole[wide : wide + 16, :] = small.astype(BF16)
    rest = whole.shape[0] - wide - 16
    whole[wide + 16 :, :] = jnp.zeros((rest, D), BF16)
    put_halves(place[0], whole, half_mine, half_other)


def halve_body(place, mine, other, *refs):
    outs, (whole,) = refs[:-1], refs[-1:]
    whole[...] = (mine[...].astype(F32) + other[...].astype(F32)).astype(BF16)
    put_chunks(place[0] >> 1, whole, outs)


def settle_body(*refs):
    total = refs[0][...].astype(F32)
    for r in refs[1:-1]:
        total = total + r[...].astype(F32)
    refs[-1][...] = total.astype(BF16)


def join_body(place, *refs):
    take_chunks(place[0] >> 1, refs[:-1], refs[-1])


def chip_swaps(value, n):
    return [swap(value, "seq", 2 * k) for k in range(1, n // 2)]


def sum_over_seq(mine, other, place, n):
    chips = n // 2
    half, width = mine.shape
    piece = bf16(half // chips, width)
    got = swap(other, "seq", 1)
    pieces = call(
        halve_body,
        "halve",
        [piece] * chips,
        (place, mine, got),
        smem=1,
        scratch=(pltpu.VMEM((half, width), BF16),),
    )
    terms = [pieces[0]] + [swap(pieces[k], "seq", 2 * k) for k in range(1, chips)]
    settled = call(settle_body, "settle", piece, terms)
    full = call(
        join_body, "join", bf16(half, width), (place, settled, *chip_swaps(settled, n)), smem=1
    )
    return full, swap(full, "seq", 1)


def both_halves(place, mine, other, whole):
    half = mine.shape[0]
    core = place & 1
    whole[pl.ds(pl.multiple_of(core * half, 16), half), :] = mine[...]
    whole[pl.ds(pl.multiple_of((1 - core) * half, 16), half), :] = other[...]


def finish_feed_body(place, mine, other, down, up, whole):
    both_halves(place[0], mine, other, whole)
    ff = down.shape[0]
    down[...] = whole[0:ff, :].astype(F32)
    up[...] = whole[ff:, :].astype(F32)


def finish_small_body(place, mine, other, mixer, g2, s2, od, g1, s1, om, ou, taps, whole):
    both_halves(place[0], mine, other, whole)
    wide = HEADS * HS
    mixer[...] = whole[0:wide, :].astype(F32)
    rows = whole[wide : wide + 16, :].astype(F32)
    for i, out in enumerate((g2, s2, od, g1, s1, om, ou)):
        out[...] = rows[i : i + 1, :].reshape(D)
    taps[...] = rows[7 : 7 + HEADS, TAP_LANE : TAP_LANE + CONV]


def weight_grads_body(n, *refs):
    queries, others, tokens = refs[:n], refs[n : 2 * n], refs[2 * n : 3 * n]
    q, k, v, oq, ok, ov = refs[3 * n : 3 * n + 6]
    turned, rows = refs[3 * n + 6 :]
    wide = HEADS * HS
    for i in range(n):
        turned[0:wide, i * ROWS : (i + 1) * ROWS] = queries[i][...]
        turned[wide:, i * ROWS : (i + 1) * ROWS] = others[i][...]
        rows[i * ROWS : (i + 1) * ROWS, :] = tokens[i][...]
    ones = jnp.ones((16, n * ROWS), BF16)
    for i, (grad, sums) in enumerate(((q, oq), (k, ok), (v, ov))):
        part = turned[i * wide : (i + 1) * wide, :]
        grad[...] = dot(part, rows[...])
        sums[...] = dot_nt(ones, part)[0:1, :].reshape(wide)


def tokens_sum_body(grad, *refs):
    total = grad[...]
    for r in refs[:-1]:
        total = total + r[...].astype(F32)
    refs[-1][...] = total.astype(BF16)


def tokens_out_body(chunk, *refs):
    pieces, out = refs[:-1], refs[-1]
    rows = out.shape[0] // len(pieces)
    for k, piece in enumerate(pieces):
        start = pl.multiple_of(jnp.bitwise_xor(chunk[0], k) * rows, 16)
        out[pl.ds(start, rows), :] = piece[...].astype(F32)


def on_device(
    tokens,
    query_weight,
    query_shift,
    key_weight,
    key_shift,
    value_weight,
    value_shift,
    mixer_weight,
    mixer_shift,
    conv_taps,
    first_gain,
    first_shift,
    up_weight,
    up_shift,
    down_weight,
    down_shift,
    second_gain,
    second_shift,
    hyperplanes,
    plane_choice,
    doc_lengths,
    out_grad,
):
    n = lax.axis_size("seq")
    parts = lax.axis_size("hid")
    place = lax.axis_index("seq").reshape(1).astype(jnp.int32)
    hid = lax.axis_index("hid")
    slot = sum(jnp.where(hid == h, HID_ORDER[h], 0) for h in range(parts))
    slot = slot.reshape(1).astype(jnp.int32)
    rows, half = ROWS // parts, ROWS // 2
    units, wide = up_weight.shape[1], HEADS * HS
    hot = plane_choice.reshape(-1, 1) == jnp.arange(PLANES, dtype=jnp.int32)
    choose = hot.astype(BF16)
    choose_back = hot.astype(F32).T
    planes_t = hyperplanes.T
    wq, wk, wv = query_weight.T, key_weight.T, value_weight.T
    side = (TAP_LANE, 512 - TAP_LANE - CONV)
    taps = jnp.pad(conv_taps, ((0, 5), side))
    taps_back = jnp.pad(conv_taps[:, ::-1], ((0, 5), side))

    weights = jnp.where(place[0] % 2 == 0, up_weight, down_weight)
    got = hid_swap(weights, 2)
    other = swap(got, "seq", 1)
    far_shift = hid_swap(up_shift, 2)
    mixers = over_hid(mixer_weight)

    raw_q, raw_k, tan_q, tan_k, pick_q, pack = project(
        tokens, wq, query_shift, wk, key_shift, wv, value_shift, hyperplanes, choose
    )
    packs = over_seq(pack)
    feat_q, feat_k = local_feats(pick_q, pack)
    context, near_half, far_half, weighted, total = forward(
        doc_lengths, place, slot, feat_q, taps, packs
    )
    contexts = [
        near_half,
        hid_swap(near_half, 1),
        hid_swap(far_half, 2),
        hid_swap(far_half, 3),
    ]
    pick_later, tokens_later, context = lax.optimization_barrier((pick_q, tokens, context))
    picks = over_seq(pick_later)
    token_blocks = over_seq(tokens_later)
    first_mine, normed_mine, inverse_mine, low, slope, keep, send = call(
        functools.partial(feed_body, parts),
        "feed",
        (
            f32(rows, D),
            f32(rows, D),
            f32(rows, 128),
            bf16(half, D),
            f32(half, 2 * units),
            f32(rows, D),
            bf16(rows, D),
        ),
        (
            place,
            slot,
            tokens,
            mixer_shift,
            first_gain,
            first_shift,
            up_weight,
            up_shift,
            down_weight,
            got,
            other,
            far_shift,
            *contexts,
            *mixers,
        ),
        smem=2,
        scratch=(
            pltpu.VMEM((half, D), F32),
            pltpu.VMEM((half, D), F32),
            pltpu.VMEM((half, 128), F32),
            pltpu.VMEM((half, D), F32),
            pltpu.VMEM((2, D, units), BF16),
        ),
        us=5,
    )
    layer, dh2, down_low = call(
        second_body,
        "second_norm",
        (bf16(rows + 16, D), f32(rows, D), bf16(rows, D)),
        (
            slot,
            first_mine,
            out_grad,
            down_shift,
            second_gain,
            second_shift,
            keep,
            hid_swap(send, 1),
        ),
        smem=1,
    )
    down_half, keep, send = call(
        feed_back_body,
        "feed_back",
        (bf16(half, D), f32(rows, D), bf16(rows, D)),
        (
            place,
            slot,
            slope,
            up_weight,
            down_weight,
            got,
            other,
            down_low,
            hid_swap(down_low, 1),
        ),
        smem=2,
        scratch=(pltpu.VMEM((half, D), F32), pltpu.VMEM((2, D, units), BF16)),
        us=4,
    )
    first_back = call(
        functools.partial(first_back_body, parts),
        "first_norm_back",
        (f32(rows, D), bf16(rows + 16, D), *[bf16(rows, wide)] * parts),
        (dh2, normed_mine, inverse_mine, first_gain, keep, hid_swap(send, 1), *mixers),
        us=3,
    )
    dh1, payload = first_back[:2]
    grad_pack, row_totals = call(
        functools.partial(split_body, parts),
        "split",
        (bf16(ROWS, 4 * HS), f32(8, ROWS)),
        (slot, weighted, total, *exchange(first_back[2:])),
        smem=1,
        scratch=(pltpu.VMEM((ROWS, wide), BF16),),
    )
    grad_packs = over_seq(grad_pack)

    feed_half = padded(units + D, n) // 2
    feed_mine, feed_other, up_sums = call(
        feed_grads_body,
        "feed_grads",
        (bf16(feed_half, D), bf16(feed_half, D), f32(8, units)),
        (
            place,
            slot,
            low,
            hid_swap(low, 2),
            down_half,
            hid_swap(down_half, 2),
            up_weight,
            up_shift,
            down_weight,
        ),
        smem=2,
        scratch=(
            pltpu.VMEM((ROWS, D), BF16),
            pltpu.VMEM((ROWS, D), BF16),
            pltpu.VMEM((2 * feed_half, D), BF16),
        ),
        us=6,
    )
    feed_sums = sum_over_seq(feed_mine, feed_other, place, n)

    query_turned, query_input, tap_rows = query_back(
        doc_lengths,
        place,
        grad_pack,
        row_totals,
        pick_q,
        tan_q,
        raw_q,
        choose_back,
        planes_t,
        wq,
        packs,
    )
    query_blocks = over_seq(query_turned)
    layer_later, payload_later, grad_pack = lax.optimization_barrier((layer, payload, grad_pack))
    layers = over_hid(layer_later)
    payloads = over_hid(payload_later)
    small_half = padded(wide + 16, n) // 2
    small_mine, small_other, layer_out = call(
        functools.partial(mixer_grads_body, parts),
        "mixer_grads",
        (bf16(small_half, D), bf16(small_half, D), bf16(ROWS, D)),
        (place, slot, context, up_sums, tap_rows, *layers, *payloads),
        smem=2,
        scratch=(pltpu.VMEM((2 * small_half, D), BF16), pltpu.VMEM((ROWS, D), BF16)),
    )
    small_sums = sum_over_seq(small_mine, small_other, place, n)
    last = key_back(
        (
            doc_lengths,
            place,
            slot,
            feat_k,
            pack,
            tan_k,
            raw_k,
            taps_back,
            choose_back,
            planes_t,
            wk,
            wv,
            query_input,
        ),
        picks,
        grad_packs,
        parts,
    )
    other_blocks = over_seq(last[0])
    piece = call(tokens_sum_body, "tokens_sum", bf16(rows, D), (dh1, *exchange(last[1:])))
    tokens_grad = call(
        tokens_out_body, "tokens_out", f32(ROWS, D), (slot, *over_hid(piece)), smem=1
    )
    down_grad, up_grad = call(
        finish_feed_body,
        "finish_feed",
        (f32(units, D), f32(D, units)),
        (place, *feed_sums),
        smem=1,
        scratch=(pltpu.VMEM((2 * feed_half, D), BF16),),
        us=4,
    )
    mixer_grad, g2, s2, od, g1, s1, om, ou, taps_grad = call(
        finish_small_body,
        "finish_small",
        (f32(wide, D), *[f32(D)] * 6, f32(units), f32(HEADS, CONV)),
        (place, *small_sums),
        smem=1,
        scratch=(pltpu.VMEM((2 * small_half, D), BF16),),
    )
    q, k, v, oq, ok, ov = call(
        functools.partial(weight_grads_body, n),
        "weight_grads",
        (*[f32(wide, D)] * 3, *[f32(wide)] * 3),
        (*query_blocks, *other_blocks, *token_blocks),
        scratch=(pltpu.VMEM((3 * wide, n * ROWS), BF16), pltpu.VMEM((n * ROWS, D), BF16)),
        us=4,
    )
    return (
        layer_out,
        tokens_grad,
        q.T,
        oq,
        k.T,
        ok,
        v.T,
        ov,
        mixer_grad,
        om,
        taps_grad,
        g1,
        s1,
        up_grad,
        ou,
        down_grad,
        od,
        g2,
        s2,
    )


def solution(mesh):
    placed = (
        P("seq", None),
        P(None, "hid"),
        P("hid"),
        P(None, "hid"),
        P("hid"),
        P(None, "hid"),
        P("hid"),
        P("hid", None),
        P(),
        P("hid", None),
        P(),
        P(),
        P(None, "hid"),
        P("hid"),
        P("hid", None),
        P(),
        P(),
        P(),
        P(),
        P(),
        P(),
        P("seq", None),
    )
    return jax.shard_map(
        on_device,
        mesh=mesh,
        in_specs=placed,
        out_specs=(
            P("seq", None),
            P("seq", None),
            P(None, "hid"),
            P("hid"),
            P(None, "hid"),
            P("hid"),
            P(None, "hid"),
            P("hid"),
            P("hid", None),
            P(),
            P("hid", None),
            P(),
            P(),
            P(None, "hid"),
            P("hid"),
            P("hid", None),
            P(),
            P(),
            P(),
        ),
        check_vma=False,
    )
```

```python
import functools
import math

import jax
import jax.numpy as jnp
from jax import lax
from jax.experimental import pallas as pl
from jax.experimental.pallas import tpu as pltpu
from jax.sharding import PartitionSpec as P

D = 768
H = 12
HS = 64
BITS = 8
PLANES = 32
HASHES = 4
CONV = 35
RADIUS = 17
FEATS = HASHES * 2**BITS
SHARP = 2.0
NORM_EPS = 1e-05
UNIT_EPS = 1e-06
EXACT = lax.Precision.HIGHEST
F32 = jnp.float32
BF16 = jnp.bfloat16
ROWS = 256
HEADS = 3
KEPT = PLANES + HS
TAP_LANE = 111
VMEM = pl.BlockSpec(memory_space=pltpu.VMEM)
SMEM = pl.BlockSpec(memory_space=pltpu.SMEM)
LIMIT = 60 * 1024 * 1024


def dot(a, b):
    return lax.dot_general(a, b, (((1,), (0,)), ((), ())), preferred_element_type=F32)


def dot_nt(a, b):
    return lax.dot_general(a, b, (((1,), (1,)), ((), ())), preferred_element_type=F32)


def dot_exact(a, b):
    return lax.dot_general(
        a, b, (((1,), (0,)), ((), ())), precision=EXACT, preferred_element_type=F32
    )


def doc_count(pos, lengths):
    start = jnp.int32(0)
    found = jnp.zeros_like(pos)
    for d in range(lengths.shape[0]):
        found = found + (pos >= start).astype(jnp.int32)
        start = start + lengths[d]
    return found + (pos >= start).astype(jnp.int32)


def blocks_meet(mine, other, lengths):
    a0 = doc_count(mine * ROWS, lengths)
    a1 = doc_count(mine * ROWS + (ROWS - 1), lengths)
    b0 = doc_count(other * ROWS, lengths)
    b1 = doc_count(other * ROWS + (ROWS - 1), lengths)
    return jnp.logical_and(a0 <= b1, b0 <= a1)


def same_doc(row_start, rows, col_start, cols, lengths, reverse=False):
    rid = row_start + lax.broadcasted_iota(jnp.int32, (rows, 1), 0)
    cid = lax.broadcasted_iota(jnp.int32, (1, cols), 1)
    cid = col_start + ((cols - 1) - cid if reverse else cid)
    return doc_count(rid, lengths) == doc_count(cid, lengths)


def hash_base(picks, m, lanes):
    bit = lax.broadcasted_iota(jnp.int32, (8, lanes), 0)
    factors = []
    for b in range(3):
        on = (bit & (1 << b)) != 0
        row = jnp.broadcast_to(picks[m * BITS + b : m * BITS + b + 1, :], (8, lanes))
        factors.append((on, jnp.where(on, row, 1.0)))
    return factors


def hash_feats(picks, m, lanes):
    factors = hash_base(picks, m, lanes)
    scale = 2.0 ** (-0.5 * BITS)
    feats = [(factors[0][1] * scale) * (factors[1][1] * factors[2][1])]
    rows = {}
    for b in range(3, BITS):
        rows[b] = jnp.broadcast_to(picks[m * BITS + b : m * BITS + b + 1, :], (8, lanes))
        feats = feats + [f * rows[b] for f in feats]
    return feats, rows, factors


def expand(picks, phi_ref):
    lanes = picks.shape[1]
    for m in range(HASHES):
        feats = hash_feats(picks, m, lanes)[0]
        for i in range(0, len(feats), 2):
            both = jnp.concatenate([feats[i], feats[i + 1]], axis=0)
            phi_ref[m * 256 + i * 8 : m * 256 + i * 8 + 16, :] = both.astype(BF16)


def expand_back(picks, dphi_ref, lane0, lanes):
    out = []
    scale = 2.0 ** (-0.5 * BITS)
    for m in range(HASHES):
        feats, rows, factors = hash_feats(picks, m, lanes)
        grads = [
            dphi_ref[m * 256 + i * 8 : m * 256 + i * 8 + 8, lane0 : lane0 + lanes]
            for i in range(32)
        ]
        found = {}
        for b in range(BITS - 1, 2, -1):
            half = len(grads) // 2
            total = grads[half] * feats[0]
            for i in range(1, half):
                total = total + grads[half + i] * feats[i]
            found[b] = jnp.sum(total, axis=0, keepdims=True)
            grads = [grads[i] + grads[half + i] * rows[b] for i in range(half)]
        g = grads[0] * scale
        (on0, f0), (on1, f1), (on2, f2) = factors
        found[0] = jnp.sum(jnp.where(on0, g * (f1 * f2), 0.0), axis=0, keepdims=True)
        found[1] = jnp.sum(jnp.where(on1, g * (f0 * f2), 0.0), axis=0, keepdims=True)
        found[2] = jnp.sum(jnp.where(on2, g * (f0 * f1), 0.0), axis=0, keepdims=True)
        out.extend(found[b] for b in range(BITS))
    return jnp.concatenate(out, axis=0)


def stacked(turned):
    return jnp.concatenate([turned[:, h * ROWS : (h + 1) * ROWS] for h in range(HEADS)], axis=0)


def column(row):
    n = row.shape[1]
    here = lax.broadcasted_iota(jnp.int32, (n, n), 0) == lax.broadcasted_iota(jnp.int32, (n, n), 1)
    return jnp.sum(jnp.where(here, row, 0.0), axis=1, keepdims=True)


def beside(rows):
    return jnp.concatenate([rows[h * HS : (h + 1) * HS] for h in range(HEADS)], axis=1)


def project_body(
    tokens, wq, bq, wk, bk, wv, bv, planes, choose, raw_q, raw_k, tan_q, tan_k, pack
):
    x = tokens[...]

    def codes(w, b, raw_ref, tan_ref):
        raw = beside(dot_nt(w[...], x) + column(b[...].reshape(1, -1)))
        raw_ref[...] = raw
        unit = raw * lax.rsqrt(jnp.sum(raw * raw, axis=0, keepdims=True) + UNIT_EPS)
        tan = jnp.tanh(SHARP * dot_exact(planes[...], unit))
        tan_ref[...] = tan
        return dot(choose[...], tan.astype(BF16)).astype(BF16)

    pack[0:PLANES, :] = codes(wk, bk, raw_k, tan_k)
    values = beside(dot_nt(wv[...], x) + column(bv[...].reshape(1, -1)))
    pack[PLANES : PLANES + HS, :] = values.astype(BF16)
    pack[KEPT:, :] = codes(wq, bq, raw_q, tan_q)


def call(body, name, out_shape, ins, smem=0, scratch=(), us=2):
    single = not isinstance(out_shape, (tuple, list))
    outs = (out_shape,) if single else tuple(out_shape)
    got = pl.pallas_call(
        body,
        out_shape=outs,
        in_specs=[SMEM] * smem + [VMEM] * (len(ins) - smem),
        out_specs=tuple([VMEM] * len(outs)),
        scratch_shapes=list(scratch),
        name=name,
        compiler_params=pltpu.CompilerParams(vmem_limit_bytes=LIMIT),
        cost_estimate=pl.CostEstimate(
            flops=int(us * 1e9), bytes_accessed=100_000, transcendentals=0
        ),
    )(*ins)
    return got[0] if single else got


def f32(*shape):
    return jax.ShapeDtypeStruct(shape, F32)


def bf16(*shape):
    return jax.ShapeDtypeStruct(shape, BF16)


def project(*ins):
    wide = HEADS * ROWS
    return call(
        project_body,
        "project",
        (
            f32(HS, wide),
            f32(HS, wide),
            f32(PLANES, wide),
            f32(PLANES, wide),
            bf16(KEPT + PLANES, wide),
        ),
        ins,
        us=0.1,
    )


def local_feats_body(row, pack, feat, phi):
    for h in range(HEADS):
        picks = pack[row : row + PLANES, h * ROWS : (h + 1) * ROWS].astype(F32)
        expand(picks, phi)
        feat[h] = phi[...].T


def local_feats(row, pack):
    return call(
        functools.partial(local_feats_body, row),
        "local_feats",
        bf16(HEADS, ROWS, FEATS),
        (pack,),
        scratch=(pltpu.VMEM((FEATS, ROWS), BF16),),
    )


def window(packs, mine, low, high, n):
    def at(h):
        before = jnp.bitwise_xor(mine, jnp.maximum(mine - 1, 0))
        after = jnp.bitwise_xor(mine, jnp.minimum(mine + 1, n - 1))
        lane = h * ROWS
        return jnp.concatenate(
            [
                packs[before, low:high, lane + 128 : lane + 256],
                packs[0, low:high, lane : lane + 256],
                packs[after, low:high, lane : lane + 128],
            ],
            axis=1,
        )

    return at


def band(row):
    return pltpu.roll(jnp.broadcast_to(row, (ROWS, 512)), 0, 1, stride=1, stride_axis=0)


def split_dot(a, b, mul):
    high = a.astype(BF16)
    low = (a - high.astype(F32)).astype(BF16)
    return mul(high, b) + mul(low, b)


def forward_body(n, lengths, place, slot, feat_q, taps, *refs):
    pack_in, (context, near_half, far_half, weighted, total_out) = refs[:n], refs[n : n + 5]
    packs, phi0, phi1, phi2, acc, tot = refs[n + 5 :]
    phis = (phi0, phi1, phi2)
    mine = place[0]
    for k in range(n):
        packs[k] = pack_in[k][0:KEPT, :]
    acc[...] = jnp.zeros_like(acc)
    tot[...] = jnp.zeros_like(tot)

    def block(k, carry):
        other = jnp.bitwise_xor(mine, k)

        @pl.when(blocks_meet(mine, other, lengths))
        def _():
            same = same_doc(mine * ROWS, ROWS, other * ROWS, ROWS, lengths)
            for h in range(HEADS):
                lane = h * ROWS
                expand(packs[k, 0:PLANES, lane : lane + ROWS].astype(F32), phis[h])
                score = dot(feat_q[h], phis[h][...])
                w = jnp.where(same, score * (1.0 / HASHES), 0.0)
                tot[h] += w[:, :128] + w[:, 128:]
                acc[h] += dot_nt(w.astype(BF16), packs[k, PLANES : PLANES + HS, lane : lane + ROWS])

        return carry

    lax.fori_loop(0, n, block, 0)
    near = same_doc(mine * ROWS, ROWS, mine * ROWS - 128, 512, lengths)
    ext = window(packs, mine, PLANES, PLANES + HS, n)
    outs, sums, parts = [], [], []
    for h in range(HEADS):
        total = 1.0 + jnp.sum(tot[h], axis=1, keepdims=True)
        taps_band = jnp.where(near, band(taps[h : h + 1, :]), 0.0)
        conv = split_dot(taps_band, ext(h), dot_nt)
        sums.append(jnp.broadcast_to(total, (ROWS, HS)))
        parts.append(acc[h])
        outs.append(acc[h] / total + conv)
    context[...] = jnp.concatenate(outs, axis=1).astype(BF16)
    half = ROWS // 2
    first = slot[0] >> 1
    near_half[...] = context[pl.ds(pl.multiple_of(first * half, 16), half), :]
    far_half[...] = context[pl.ds(pl.multiple_of((1 - first) * half, 16), half), :]
    weighted[...] = jnp.concatenate(parts, axis=1)
    total_out[...] = jnp.concatenate(sums, axis=1)


def forward(lengths, place, slot, feat_q, taps, packs):
    n = len(packs)
    wide = HEADS * HS
    return call(
        functools.partial(forward_body, n),
        "attend",
        (
            bf16(ROWS, wide),
            bf16(ROWS // 2, wide),
            bf16(ROWS // 2, wide),
            f32(ROWS, wide),
            f32(ROWS, wide),
        ),
        (lengths, place, slot, feat_q, taps, *packs),
        smem=3,
        scratch=(
            pltpu.VMEM((n, PLANES + HS, HEADS * ROWS), BF16),
            pltpu.VMEM((FEATS, ROWS), BF16),
            pltpu.VMEM((FEATS, ROWS), BF16),
            pltpu.VMEM((FEATS, ROWS), BF16),
            pltpu.VMEM((HEADS, ROWS, HS), F32),
            pltpu.VMEM((HEADS, ROWS, 128), F32),
        ),
        us=9,
    )


def unit_back(code_grad, tan, raw, planes_t):
    scale = lax.rsqrt(jnp.sum(raw * raw, axis=0, keepdims=True) + UNIT_EPS)
    unit_grad = dot_exact(planes_t, code_grad * (SHARP * (1.0 - tan * tan)))
    inner = jnp.sum(raw * unit_grad, axis=0, keepdims=True)
    return unit_grad * scale - raw * (scale * scale * scale) * inner


def codes_to_raw(dphi, pack, row, tan, raw, choose_back, planes_t):
    parts = []
    for h in range(HEADS):
        for u in range(2):
            lane = h * ROWS + u * 128
            parts.append(
                expand_back(
                    pack[row : row + PLANES, lane : lane + 128].astype(F32), dphi.at[h], u * 128, 128
                )
            )
    pick_grad = jnp.concatenate(parts, axis=1) * (1.0 / HASHES)
    code_grad = dot_exact(choose_back[...], pick_grad)
    return unit_back(code_grad, tan[...], raw[...], planes_t[...])


def query_back_body(
    n, lengths, place, grads, row_totals, tan, raw, choose_back, planes_t, weight, *refs
):
    pack_in, (grad_out, input_out, taps_out) = refs[:n], refs[n : n + 3]
    packs, phi0, phi1, phi2, dphi = refs[n + 3 :]
    phis = (phi0, phi1, phi2)
    mine = place[0]
    for k in range(n):
        packs[k] = pack_in[k][0:KEPT, :]
    dphi[...] = jnp.zeros_like(dphi)

    def block(k, carry):
        other = jnp.bitwise_xor(mine, k)

        @pl.when(blocks_meet(mine, other, lengths))
        def _():
            same = same_doc(other * ROWS, ROWS, mine * ROWS, ROWS, lengths)
            for h in range(HEADS):
                lane = h * ROWS
                expand(packs[k, 0:PLANES, lane : lane + ROWS].astype(F32), phis[h])
                values = packs[k, PLANES : PLANES + HS, lane : lane + ROWS].T
                dw = dot_nt(values, grads[:, h * HS : (h + 1) * HS]) + row_totals[h : h + 1, :]
                dw = jnp.where(same, dw, 0.0).astype(BF16)
                dphi[h] += dot(phis[h][...], dw)

        return carry

    lax.fori_loop(0, n, block, 0)
    raw_grad = codes_to_raw(dphi, pack_in[0], KEPT, tan, raw, choose_back, planes_t)
    turned = stacked(raw_grad).astype(BF16)
    grad_out[...] = turned
    input_out[...] = dot(turned.astype(F32).T.astype(BF16), weight[...])
    near_rev = same_doc(mine * ROWS, ROWS, mine * ROWS - 128, 512, lengths, reverse=True)
    turn = lax.broadcasted_iota(jnp.int32, (512, 512), 0) + lax.broadcasted_iota(
        jnp.int32, (512, 512), 1
    )
    flip = (turn == 511).astype(F32)
    flip_low = flip.astype(BF16)
    ext = window(packs, mine, PLANES, PLANES + HS, n)
    side = grads[:, 3 * HS : 4 * HS].astype(F32)
    tap_rows = []
    for h in range(HEADS):
        total = side[:, HEADS + h : HEADS + h + 1]
        context_grad = (grads[:, h * HS : (h + 1) * HS].astype(F32) * total).astype(BF16)
        flipped = dot(ext(h), flip_low).astype(BF16)
        cross = jnp.where(near_rev, dot(context_grad, flipped), 0.0)
        cross = pltpu.roll(cross, 0, 1, stride=1, stride_axis=0)
        tap_rows.append(jnp.sum(cross, axis=0, keepdims=True))
    tap_rows.append(jnp.zeros((8 - HEADS, 512), F32))
    taps_out[...] = dot_exact(jnp.concatenate(tap_rows, axis=0), flip)


def query_back(*ins):
    packs = ins[-1]
    n = len(packs)
    return call(
        functools.partial(query_back_body, n),
        "query_back",
        (bf16(HEADS * HS, ROWS), f32(ROWS, D), f32(8, 512)),
        (*ins[:-1], *packs),
        smem=2,
        scratch=(
            pltpu.VMEM((n, PLANES + HS, HEADS * ROWS), BF16),
            pltpu.VMEM((FEATS, ROWS), BF16),
            pltpu.VMEM((FEATS, ROWS), BF16),
            pltpu.VMEM((FEATS, ROWS), BF16),
            pltpu.VMEM((HEADS, FEATS, ROWS), F32),
        ),
        us=9,
    )


def key_back_body(
    n,
    lengths,
    place,
    slot,
    feat_k,
    tan,
    raw,
    taps_back,
    choose_back,
    planes_t,
    wk,
    wv,
    query_input,
    query_turned,
    dh1,
    *refs,
):
    pack_in, grad_in = refs[:n], refs[n : 2 * n]
    pack = pack_in[0]
    turned_out, input_out = refs[2 * n : 2 * n + 2]
    picks, grads, phi0, phi1, phi2, dphi, acc, inputs = refs[2 * n + 2 :]
    phis = (phi0, phi1, phi2)
    mine = place[0]
    for k in range(n):
        picks[k] = pack_in[k][KEPT:, :]
        grads[k] = grad_in[k][...]
    dphi[...] = jnp.zeros_like(dphi)
    acc[...] = jnp.zeros_like(acc)

    def block(k, carry):
        other = jnp.bitwise_xor(mine, k)

        @pl.when(blocks_meet(mine, other, lengths))
        def _():
            same = same_doc(mine * ROWS, ROWS, other * ROWS, ROWS, lengths)
            same_t = same_doc(other * ROWS, ROWS, mine * ROWS, ROWS, lengths)
            for h in range(HEADS):
                lane = h * ROWS
                expand(picks[k, :, lane : lane + ROWS].astype(F32), phis[h])
                score = dot(feat_k[h], phis[h][...])
                w = jnp.where(same, score * (1.0 / HASHES), 0.0).astype(BF16)
                grad = grads[k, :, h * HS : (h + 1) * HS]
                acc[h] += dot(w, grad)
                values_t = pack[PLANES : PLANES + HS, lane : lane + ROWS]
                side = grads[k, :, 3 * HS : 4 * HS].astype(F32)
                row_total = side[:, h : h + 1] + side[:, 2 * HEADS + h : 2 * HEADS + h + 1]
                dw = dot(grad, values_t) + row_total
                dw = jnp.where(same_t, dw, 0.0).astype(BF16)
                dphi[h] += dot(phis[h][...], dw)

        return carry

    lax.fori_loop(0, n, block, 0)
    raw_grad = codes_to_raw(dphi, pack_in[0], 0, tan, raw, choose_back, planes_t)
    key_turned = stacked(raw_grad).astype(BF16)
    key_rows = key_turned.astype(F32).T

    before = jnp.bitwise_xor(mine, jnp.maximum(mine - 1, 0))
    after = jnp.bitwise_xor(mine, jnp.minimum(mine + 1, n - 1))
    near = same_doc(mine * ROWS, ROWS, mine * ROWS - 128, 512, lengths)
    ext = jnp.concatenate([grads[before, 128:, :], grads[0], grads[after, :128, :]], axis=0)
    side = ext[:, 3 * HS : 4 * HS].astype(F32)
    outs = []
    for h in range(HEADS):
        total = side[:, HEADS + h : HEADS + h + 1]
        context_grad = (ext[:, h * HS : (h + 1) * HS].astype(F32) * total).astype(BF16)
        taps_band = jnp.where(near, band(taps_back[h : h + 1, :]), 0.0)
        outs.append(acc[h] + split_dot(taps_band, context_grad, dot))
    value_rows = jnp.concatenate(outs, axis=1).astype(BF16)
    wide = HEADS * HS
    turned_out[0:wide, :] = query_turned[...]
    turned_out[wide : 2 * wide, :] = key_turned
    turned_out[2 * wide :, :] = value_rows.astype(F32).T.astype(BF16)
    inputs[...] = query_input[...] + dot(key_rows.astype(BF16), wk[...]) + dot(value_rows, wv[...])
    rows = dh1.shape[0]
    own = pl.ds(pl.multiple_of(slot[0] * rows, 16), rows)
    inputs[own, :] = inputs[own, :] + dh1[...]
    input_out[...] = inputs[...].astype(BF16)


def key_back(ins, picks, grads):
    n = len(picks)
    return call(
        functools.partial(key_back_body, n),
        "key_back",
        (bf16(3 * HEADS * HS, ROWS), bf16(ROWS, D)),
        (*ins, *picks, *grads),
        smem=3,
        scratch=(
            pltpu.VMEM((n, PLANES, HEADS * ROWS), BF16),
            pltpu.VMEM((n, ROWS, 4 * HS), BF16),
            pltpu.VMEM((FEATS, ROWS), BF16),
            pltpu.VMEM((FEATS, ROWS), BF16),
            pltpu.VMEM((FEATS, ROWS), BF16),
            pltpu.VMEM((HEADS, FEATS, ROWS), F32),
            pltpu.VMEM((HEADS, ROWS, HS), F32),
            pltpu.VMEM((ROWS, D), F32),
        ),
        us=15,
    )


def padded(rows, n):
    return -(-rows // (16 * n)) * (16 * n)


def put_halves(place, whole, mine, other):
    half = whole.shape[0] // 2
    core = place & 1
    mine[...] = whole[pl.ds(pl.multiple_of(core * half, 16), half), :]
    other[...] = whole[pl.ds(pl.multiple_of((1 - core) * half, 16), half), :]


def put_chunks(index, whole, outs):
    rows = outs[0].shape[0]
    for k, out in enumerate(outs):
        start = pl.multiple_of(jnp.bitwise_xor(index, k) * rows, 16)
        out[...] = whole[pl.ds(start, rows), :]


def swap(value, axis, k):
    n = lax.axis_size(axis)
    return lax.ppermute(value, axis, [(i, i ^ k) for i in range(n)])


def cross_chips(value):
    return [value] + [swap(value, "seq", k) for k in range(2, lax.axis_size("seq"), 2)]


def from_partner(blocks):
    got = []
    for block in blocks:
        got += [block, swap(block, "seq", 1)]
    return got


def over_seq(value):
    return from_partner(cross_chips(value))


def after(value, then):
    return lax.optimization_barrier((value, then))


HID_ORDER = (0, 2, 1, 3)


def hid_swap(value, j):
    return swap(value, "hid", HID_ORDER[j])


def far_swap(value):
    chips, parts = lax.axis_size("seq"), lax.axis_size("hid")
    pairs = []
    for s in range(chips):
        flip = HID_ORDER[3] if s % 2 else HID_ORDER[1]
        pairs += [(s * parts + h, s * parts + (h ^ flip)) for h in range(parts)]
    return lax.ppermute(value, ("seq", "hid"), pairs)


def over_hid(value):
    return [value] + [hid_swap(value, j) for j in range(1, len(HID_ORDER))]


def exchange(chunks):
    return [chunks[0]] + [hid_swap(chunks[j], j) for j in range(1, len(chunks))]


def flat(ref):
    return ref[...].reshape(1, -1)


def norm_stats(rows):
    center = rows - jnp.mean(rows, axis=-1, keepdims=True)
    inverse = lax.rsqrt(jnp.mean(center * center, axis=-1, keepdims=True) + NORM_EPS)
    return center * inverse, inverse


def norm_grad(grad, normed, inverse, gain):
    scaled = grad * gain
    return inverse * (
        scaled
        - jnp.mean(scaled, axis=-1, keepdims=True)
        - normed * jnp.mean(scaled * normed, axis=-1, keepdims=True)
    )


def column_sums(*rows):
    sums = [jnp.sum(r, axis=0, keepdims=True) for r in rows]
    return jnp.concatenate(sums + [jnp.zeros((8 - len(sums), D), F32)], axis=0)


def two_parts(sums):
    high = sums.astype(BF16).astype(F32)
    return jnp.concatenate([high, sums - high], axis=0).astype(BF16)


def bundle_body(place, up, down, mixer, shift, bundle):
    core = place[0] & 1
    size, rows = up.shape[0], mixer.shape[0] // 2

    @pl.when(core == 0)
    def _():
        bundle[0:size, :] = up[...]

    @pl.when(core == 1)
    def _():
        bundle[0:size, :] = down[...]

    mine = mixer[pl.ds(pl.multiple_of(core * rows, 16), rows), :]
    bundle[size : size + rows, :] = mine
    left = flat(shift)
    parts = []
    for _ in range(3):
        part = left.astype(BF16).astype(F32)
        parts.append(part)
        left = left - part
    parts.append(jnp.zeros((13, D), F32))
    bundle[size + rows :, :] = jnp.concatenate(parts, axis=0).astype(BF16)


def make_bundle(place, up, down, mixer, shift):
    rows = mixer.shape[0] // 2
    return call(
        bundle_body,
        "bundle",
        bf16(up.shape[0] + rows + 16, D),
        (place, up, down, mixer, shift),
        smem=1,
        us=20,
    )


def partner_weights(core, got, other, both):
    size = both.shape[1]
    both[core] = got[0:size, :]
    both[1 - core] = other[0:size, :]


def put_mixers(core, size, own, got, other, mine, theirs, mixers):
    rows = own.shape[0] // 2
    mixers[0] = own[...]
    start = pl.multiple_of(core * rows, 16)
    far = pl.multiple_of((1 - core) * rows, 16)
    mixers[2, pl.ds(start, rows), :] = got[size : size + rows, :]
    mixers[2, pl.ds(far, rows), :] = other[size : size + rows, :]
    mixers[1 + 2 * core] = mine[...]
    mixers[3 - 2 * core] = theirs[...]


def gelu_parts(x):
    cdf = 0.5 * (1.0 + lax.erf(x * math.sqrt(0.5)))
    slope = cdf + x * (jnp.exp(-0.5 * x * x) * (1.0 / math.sqrt(2.0 * math.pi)))
    return (x * cdf).astype(BF16), slope


def keep_and_send(partial, quarter, keep, send):
    rows = keep.shape[0]
    keep[...] = partial[pl.ds(pl.multiple_of(quarter * rows, 8), rows), :]
    other = pl.multiple_of((1 - quarter) * rows, 8)
    send[...] = partial[pl.ds(other, rows), :].astype(BF16)


def feed_body(parts, place, slot, *refs):
    tokens, mixer_shift, gain, shift, up, up_shift, down, got, other, mixer = refs[:10]
    far_mixer, other_mixer = refs[10:12]
    contexts = refs[12 : 12 + parts]
    first_mine, normed_mine, inverse_mine, low_out, slope_out, keep, send, mixers = refs[
        12 + parts : 20 + parts
    ]
    first, normed, inverse, partial, both = refs[20 + parts :]
    half = ROWS // 2
    core = place[0] & 1
    partner_weights(core, got, other, both)
    put_mixers(core, both.shape[1], mixer, got, other, far_mixer, other_mixer, mixers)
    mine = tokens[pl.ds(pl.multiple_of((slot[0] >> 1) * half, 16), half), :]
    mixed = flat(mixer_shift) + mine.astype(F32)
    for j, c in enumerate(contexts):
        mixed = mixed + dot(c[...], mixers[j])
    base = both.shape[1] + mixer.shape[0] // 2
    shift_rows = got[base : base + 16, :].astype(F32)
    far_shift = (shift_rows[0:1] + shift_rows[1:2]) + shift_rows[2:3]
    n1, r1 = norm_stats(mixed)
    rows1 = n1 * flat(gain) + flat(shift)
    first[...] = rows1
    normed[...] = n1
    inverse[...] = jnp.broadcast_to(r1, inverse.shape)
    low = rows1.astype(BF16)
    low_out[...] = low
    hidden, slope = gelu_parts(dot(low, up[...]) + flat(up_shift))
    slope_out[:, 0:D] = slope
    far_hidden, far_slope = gelu_parts(dot(low, both[0]) + far_shift)
    slope_out[:, D:] = far_slope
    partial[...] = dot(hidden, down[...]) + dot(far_hidden, both[1])
    quarter = slot[0] & 1
    keep_and_send(partial, quarter, keep, send)
    rows = first_mine.shape[0]
    start = pl.multiple_of(quarter * rows, 8)
    first_mine[...] = first[pl.ds(start, rows), :]
    normed_mine[...] = normed[pl.ds(start, rows), :]
    inverse_mine[...] = inverse[pl.ds(start, rows), :]


def second_body(slot, first, out_grad, down_shift, gain, shift, keep, got, layer, grad_out, low_out):
    rows = first.shape[0]
    total = first[...] + flat(down_shift) + keep[...] + got[...].astype(F32)
    n2, r2 = norm_stats(total)
    grad = out_grad[pl.ds(pl.multiple_of(slot[0] * rows, 8), rows), :]
    dh2 = norm_grad(grad, n2, r2, flat(gain))
    grad_out[...] = dh2
    low = dh2.astype(BF16)
    low_out[...] = low
    layer[0:rows, :] = (n2 * flat(gain) + flat(shift)).astype(BF16)
    layer[rows:, :] = two_parts(column_sums(grad * n2, grad, low.astype(F32)))


def feed_back_body(place, slot, slope, up, down, got, other, low_mine, low_got, low_half, keep, send, partial, both):
    partner_weights(place[0] & 1, got, other, both)
    quarter = slot[0] & 1
    take_chunks(quarter, (low_mine, low_got), low_half)
    low = low_half[...]
    near = (dot_nt(low, down[...]) * slope[:, 0:D]).astype(BF16)
    far = (dot_nt(low, both[1]) * slope[:, D:]).astype(BF16)
    partial[...] = dot_nt(near, up[...]) + dot_nt(far, both[0])
    keep_and_send(partial, quarter, keep, send)


def take_chunks(index, pieces, whole, first=0):
    rows = whole.shape[0] // len(pieces)
    for k, piece in enumerate(pieces):
        start = pl.multiple_of(jnp.bitwise_xor(index, k) * rows, 16)
        whole[pl.ds(start, rows), :] = piece[first : first + rows, :]


def first_back_body(parts, grad, normed, inverse, gain, keep, got, layer, mixers, *refs):
    dh1_out, payload = refs[:2]
    outs = refs[2:]
    total = grad[...] + keep[...] + got[...].astype(F32)
    n1 = normed[...]
    dh1 = norm_grad(total, n1, inverse[:, 0:1], flat(gain))
    dh1_out[...] = dh1
    low = dh1.astype(BF16)
    rows = dh1.shape[0]
    payload[0:rows, :] = low
    payload[rows : 2 * rows + 16, :] = layer[...]
    payload[2 * rows + 16 :, :] = two_parts(column_sums(total * n1, total, low.astype(F32)))
    for j, out in enumerate(outs):
        out[...] = dot_nt(low, mixers[j]).astype(BF16)


def split_body(parts, chunk, weighted, total, *refs):
    pieces, (grad_pack, row_totals), (whole,) = refs[:parts], refs[parts : parts + 2], refs[parts + 2 :]
    take_chunks(chunk[0], pieces, whole)
    dctx = whole[...].astype(F32)
    wide = HEADS * HS
    each = total[...]
    grad_pack[:, 0:wide] = (dctx / each).astype(BF16)
    product = dctx * weighted[...]
    cols = []
    for h in range(HEADS):
        norm = each[:, h * HS : h * HS + 1]
        inner = jnp.sum(product[:, h * HS : (h + 1) * HS], axis=1, keepdims=True)
        cols.append((-inner / (norm * norm), norm))
    lane = lax.broadcasted_iota(jnp.int32, (ROWS, 128), 1)
    side = jnp.zeros((ROWS, 128), F32)
    for h, (grad, norm) in enumerate(cols):
        high = grad.astype(BF16).astype(F32)
        side = jnp.where(lane == h, high, side)
        side = jnp.where(lane == HEADS + h, norm, side)
        side = jnp.where(lane == 2 * HEADS + h, grad - high, side)
        side = jnp.where(lane == 64 + h, grad, side)
    grad_pack[:, wide : wide + 64] = side[:, 0:64].astype(BF16)
    row_totals[...] = side.T[64:72, :]


def feed_grads_body(place, slot, low_mine, low_got, down_mine, down_got, up, up_shift, down, half_mine, half_other, sums, low_all, down_all):
    take_chunks(slot[0] >> 1, (low_mine, low_got), low_all)
    take_chunks(slot[0] >> 1, (down_mine, down_got), down_all)
    low, grad = low_all[...], down_all[...]
    hidden, slope = gelu_parts(dot(low, up[...]) + flat(up_shift))
    up_low = (dot_nt(grad, down[...]) * slope).astype(BF16)
    down_part = dot(hidden.T, grad).astype(BF16)
    up_part = dot(low.T, up_low).astype(BF16)
    core = place[0] & 1

    def put(first, second):
        first[0 : down_part.shape[0], :] = down_part
        second[0 : up_part.shape[0], :] = up_part

    pl.when(core == 0)(lambda: put(half_mine, half_other))
    pl.when(core == 1)(lambda: put(half_other, half_mine))
    sums[...] = jnp.broadcast_to(jnp.sum(up_low.astype(F32), axis=0, keepdims=True), sums.shape)


def mixer_grads_body(parts, place, slot, context, up_sums, taps, *refs):
    payloads = refs[:parts]
    half_mine, half_other, layer_out, whole, mixed = refs[parts:]
    wide = HEADS * HS
    rows = ROWS // parts
    take_chunks(slot[0], payloads, layer_out, rows)
    take_chunks(slot[0], payloads, mixed)

    def summed(row):
        total = jnp.zeros((8, D), F32)
        for r in payloads:
            total = total + r[row : row + 8, :].astype(F32) + r[row + 8 : row + 16, :].astype(F32)
        return total[0:3]

    context_t = context[...].astype(F32).T.astype(BF16)
    whole[0:wide, :] = dot(context_t, mixed[...]).astype(BF16)
    tap_block = jnp.concatenate([taps[0:HEADS, :], jnp.zeros((HEADS, D - 512), F32)], axis=1)
    small = jnp.concatenate(
        [summed(2 * rows), summed(2 * rows + 16), up_sums[0:1, :], tap_block, jnp.zeros((6, D), F32)],
        axis=0,
    )
    whole[wide : wide + 16, :] = small.astype(BF16)
    rest = whole.shape[0] - wide - 16
    if rest:
        whole[wide + 16 :, :] = jnp.zeros((rest, D), BF16)
    put_halves(place[0], whole, half_mine, half_other)


def halve_body(place, mine, other, *outs):
    rows = outs[0].shape[0]
    for k, out in enumerate(outs):
        start = pl.multiple_of(jnp.bitwise_xor(place[0] >> 1, k) * rows, 16)
        at = pl.ds(start, rows)
        out[...] = (mine[at, :].astype(F32) + other[at, :].astype(F32)).astype(BF16)


def settle_body(*refs):
    total = refs[0][...].astype(F32)
    for r in refs[1:-1]:
        total = total + r[...].astype(F32)
    refs[-1][...] = total.astype(BF16)


def join_body(place, *refs):
    take_chunks(place[0] >> 1, refs[:-1], refs[-1])


def chip_swaps(value, n):
    return [swap(value, "seq", 2 * k) for k in range(1, n // 2)]


def scatter_chips(mine, got, place, n):
    chips = n // 2
    half, width = mine.shape
    return call(
        halve_body,
        "halve",
        [bf16(half // chips, width)] * chips,
        (place, mine, got),
        smem=1,
    )


def halve_all_body(mine, other, out):
    out[...] = (mine[...].astype(F32) + other[...].astype(F32)).astype(BF16)


def total_body(place, *refs):
    pieces, out, stack = refs[:-2], refs[-2], refs[-1]
    for k, piece in enumerate(pieces):
        stack[jnp.bitwise_xor(place[0] >> 1, k)] = piece[...]
    total = stack[0].astype(F32)
    for k in range(1, len(pieces)):
        total = total + stack[k].astype(F32)
    out[...] = total.astype(BF16)


def total_chips(chip, got, place):
    terms = [chip] + list(got)
    return call(
        total_body,
        "total_small",
        bf16(*chip.shape),
        (place, *terms),
        smem=1,
        scratch=(pltpu.VMEM((len(terms), *chip.shape), BF16),),
    )


def both_halves(place, mine, other, whole):
    half = mine.shape[0]
    core = place & 1
    whole[pl.ds(pl.multiple_of(core * half, 16), half), :] = mine[...]
    whole[pl.ds(pl.multiple_of((1 - core) * half, 16), half), :] = other[...]


def finish_feed_body(place, mine, other, down, up):
    ff = down.shape[0]
    core = place[0] & 1

    def put(first, second):
        down[...] = first[0:ff, :].astype(F32)
        up[...] = second[0:D, :].astype(F32)

    pl.when(core == 0)(lambda: put(mine, other))
    pl.when(core == 1)(lambda: put(other, mine))


def finish_small_body(place, mine, other, mixer, g2, s2, od, g1, s1, om, ou, taps, whole):
    both_halves(place[0], mine, other, whole)
    wide = HEADS * HS
    mixer[...] = whole[0:wide, :].astype(F32)
    rows = whole[wide : wide + 16, :].astype(F32)
    for i, out in enumerate((g2, s2, od, g1, s1, om, ou)):
        out[...] = rows[i : i + 1, :].reshape(D)
    taps[...] = rows[7 : 7 + HEADS, TAP_LANE : TAP_LANE + CONV]


def weight_grads_body(n, *refs):
    blocks, tokens = refs[:n], refs[n : 2 * n]
    q, k, v, oq, ok, ov = refs[2 * n : 2 * n + 6]
    turned, rows = refs[2 * n + 6 :]
    wide = HEADS * HS
    for i in range(n):
        turned[:, i * ROWS : (i + 1) * ROWS] = blocks[i][...]
        rows[i * ROWS : (i + 1) * ROWS, :] = tokens[i][...]
    ones = jnp.ones((16, n * ROWS), BF16)
    for i, (grad, sums) in enumerate(((q, oq), (k, ok), (v, ov))):
        part = turned[i * wide : (i + 1) * wide, :]
        grad[...] = dot(part, rows[...])
        sums[...] = dot_nt(ones, part)[0:1, :].reshape(wide)


def tokens_sum_body(mine, other, out):
    out[...] = (mine[...].astype(F32) + other[...].astype(F32)).astype(BF16)


def tokens_out_body(mine, other, out):
    out[...] = mine[...].astype(F32) + other[...].astype(F32)


def on_device(
    tokens,
    query_weight,
    query_shift,
    key_weight,
    key_shift,
    value_weight,
    value_shift,
    mixer_weight,
    mixer_shift,
    conv_taps,
    first_gain,
    first_shift,
    up_weight,
    up_shift,
    down_weight,
    down_shift,
    second_gain,
    second_shift,
    hyperplanes,
    plane_choice,
    doc_lengths,
    out_grad,
):
    n = lax.axis_size("seq")
    parts = lax.axis_size("hid")
    place = lax.axis_index("seq").reshape(1).astype(jnp.int32)
    hid = lax.axis_index("hid")
    slot = sum(jnp.where(hid == h, HID_ORDER[h], 0) for h in range(parts))
    slot = slot.reshape(1).astype(jnp.int32)
    rows, half = ROWS // parts, ROWS // 2
    units, wide = up_weight.shape[1], HEADS * HS
    hot = plane_choice.reshape(-1, 1) == jnp.arange(PLANES, dtype=jnp.int32)
    choose = hot.astype(BF16)
    choose_back = hot.astype(F32).T
    planes_t = hyperplanes.T
    wq, wk, wv = query_weight.T, key_weight.T, value_weight.T
    side = (TAP_LANE, 512 - TAP_LANE - CONV)
    taps = jnp.pad(conv_taps, ((0, 5), side))
    taps_back = jnp.pad(conv_taps[:, ::-1], ((0, 5), side))

    far_mixer = far_swap(mixer_weight)
    bundle = make_bundle(place, up_weight, down_weight, mixer_weight, up_shift)
    got = hid_swap(bundle, 2)

    raw_q, raw_k, tan_q, tan_k, pack = project(
        tokens, wq, query_shift, wk, key_shift, wv, value_shift, hyperplanes, choose
    )
    far_mixer, pack = after(far_mixer, pack)
    other_mixer = swap(far_mixer, "seq", 1)
    packs = over_seq(pack)
    feat_q = local_feats(KEPT, pack)
    context, near_half, far_half, weighted, total = forward(
        doc_lengths, place, slot, feat_q, taps, packs
    )
    contexts = [
        near_half,
        hid_swap(near_half, 1),
        hid_swap(far_half, 2),
        hid_swap(far_half, 3),
    ]
    got, context = after(got, context)
    other = swap(got, "seq", 1)
    first_mine, normed_mine, inverse_mine, low, slope, keep, send, mixers = call(
        functools.partial(feed_body, parts),
        "feed",
        (
            f32(rows, D),
            f32(rows, D),
            f32(rows, 128),
            bf16(half, D),
            f32(half, 2 * units),
            f32(rows, D),
            bf16(rows, D),
            bf16(parts, wide, D),
        ),
        (
            place,
            slot,
            tokens,
            mixer_shift,
            first_gain,
            first_shift,
            up_weight,
            up_shift,
            down_weight,
            got,
            other,
            mixer_weight,
            far_mixer,
            other_mixer,
            *contexts,
        ),
        smem=2,
        scratch=(
            pltpu.VMEM((half, D), F32),
            pltpu.VMEM((half, D), F32),
            pltpu.VMEM((half, 128), F32),
            pltpu.VMEM((half, D), F32),
            pltpu.VMEM((2, D, units), BF16),
        ),
        us=5,
    )
    partial = hid_swap(send, 1)
    tokens_later, keep = after(tokens, keep)
    token_blocks = cross_chips(tokens_later)
    layer, dh2, down_low = call(
        second_body,
        "second_norm",
        (bf16(rows + 16, D), f32(rows, D), bf16(rows, D)),
        (
            slot,
            first_mine,
            out_grad,
            down_shift,
            second_gain,
            second_shift,
            keep,
            partial,
        ),
        smem=1,
    )
    pack_later, dh2 = after(pack, dh2)
    feat_k, slope = after(local_feats(0, pack_later), slope)
    down_half, keep, send = call(
        feed_back_body,
        "feed_back",
        (bf16(half, D), f32(rows, D), bf16(rows, D)),
        (
            place,
            slot,
            slope,
            up_weight,
            down_weight,
            got,
            other,
            down_low,
            hid_swap(down_low, 1),
        ),
        smem=2,
        scratch=(pltpu.VMEM((half, D), F32), pltpu.VMEM((2, D, units), BF16)),
        us=4,
    )
    token_blocks, mixers = after(token_blocks, mixers)
    first_back = call(
        functools.partial(first_back_body, parts),
        "first_norm_back",
        (f32(rows, D), bf16(2 * rows + 32, D), *[bf16(rows, wide)] * parts),
        (dh2, normed_mine, inverse_mine, first_gain, keep, hid_swap(send, 1), layer, mixers),
        us=3,
    )
    dh1, payload = first_back[:2]
    pieces = exchange(first_back[2:])
    feed_half = padded(2 * max(units, D), n) // 2
    feed_mine, feed_other, up_sums = call(
        feed_grads_body,
        "feed_grads",
        (bf16(feed_half, D), bf16(feed_half, D), f32(8, units)),
        (
            place,
            slot,
            low,
            hid_swap(low, 2),
            down_half,
            hid_swap(down_half, 2),
            up_weight,
            up_shift,
            down_weight,
        ),
        smem=2,
        scratch=(
            pltpu.VMEM((ROWS, D), BF16),
            pltpu.VMEM((ROWS, D), BF16),
        ),
        us=6,
    )
    pieces, feed_other = after(pieces, feed_other)
    grad_pack, row_totals = call(
        functools.partial(split_body, parts),
        "split",
        (bf16(ROWS, 4 * HS), f32(8, ROWS)),
        (slot, weighted, total, *pieces),
        smem=1,
        scratch=(pltpu.VMEM((ROWS, wide), BF16),),
    )
    payload, grad_pack = after(payload, grad_pack)
    grad_blocks = cross_chips(grad_pack)
    feed_pieces = scatter_chips(feed_mine, swap(feed_other, "seq", 1), place, n)
    feed_got = [swap(feed_pieces[k], "seq", 2 * k) for k in range(1, n // 2)]
    feed_own, row_totals = after(feed_pieces[0], row_totals)
    query_turned, query_input, tap_rows = query_back(
        doc_lengths,
        place,
        grad_pack,
        row_totals,
        tan_q,
        raw_q,
        choose_back,
        planes_t,
        wq,
        packs,
    )
    grad_blocks, query_turned = after(grad_blocks, query_turned)
    grad_packs = from_partner(grad_blocks)
    payloads = over_hid(payload)
    settled = call(settle_body, "settle", bf16(*feed_own.shape), (feed_own, *feed_got))
    small_half = -(-(wide + 16) // 32) * 16
    small_mine, small_other, layer_out = call(
        functools.partial(mixer_grads_body, parts),
        "mixer_grads",
        (bf16(small_half, D), bf16(small_half, D), bf16(ROWS, D)),
        (place, slot, context, up_sums, tap_rows, *payloads),
        smem=2,
        scratch=(pltpu.VMEM((2 * small_half, D), BF16), pltpu.VMEM((ROWS, D), BF16)),
    )
    (settled, small_other), grad_packs = after((settled, small_other), grad_packs)
    small_got = swap(small_other, "seq", 1)
    feed_chips = chip_swaps(settled, n)
    last = key_back(
        (
            doc_lengths,
            place,
            slot,
            feat_k,
            tan_k,
            raw_k,
            taps_back,
            choose_back,
            planes_t,
            wk,
            wv,
            query_input,
            query_turned,
            dh1,
        ),
        packs,
        grad_packs,
    )
    last, (small_got, feed_chips) = after(last, (small_got, feed_chips))
    near_tokens = hid_swap(last[1], 2)
    blocks = over_seq(last[0])
    both = call(tokens_sum_body, "tokens_sum", bf16(ROWS, D), (last[1], near_tokens))
    small_chip = call(halve_all_body, "halve_small", bf16(*small_mine.shape), (small_mine, small_got))
    both, small_chip = after(both, small_chip)
    feed_full = call(
        join_body, "join", bf16(feed_half, D), (place, settled, *feed_chips), smem=1
    )
    tokens_grad = call(tokens_out_body, "tokens_out", f32(ROWS, D), (both, hid_swap(both, 1)))
    feed_sums = (feed_full, swap(feed_full, "seq", 1))
    small_full = total_chips(small_chip, chip_swaps(small_chip, n), place)
    small_sums = (small_full, swap(small_full, "seq", 1))
    token_blocks = from_partner(token_blocks)
    down_grad, up_grad = call(
        finish_feed_body,
        "finish_feed",
        (f32(units, D), f32(D, units)),
        (place, *feed_sums),
        smem=1,
        us=4,
    )
    mixer_grad, g2, s2, od, g1, s1, om, ou, taps_grad = call(
        finish_small_body,
        "finish_small",
        (f32(wide, D), *[f32(D)] * 6, f32(units), f32(HEADS, CONV)),
        (place, *small_sums),
        smem=1,
        scratch=(pltpu.VMEM((2 * small_half, D), BF16),),
    )
    q, k, v, oq, ok, ov = call(
        functools.partial(weight_grads_body, n),
        "weight_grads",
        (*[f32(wide, D)] * 3, *[f32(wide)] * 3),
        (*blocks, *token_blocks),
        scratch=(pltpu.VMEM((3 * wide, n * ROWS), BF16), pltpu.VMEM((n * ROWS, D), BF16)),
        us=4,
    )
    return (
        layer_out,
        tokens_grad,
        q.T,
        oq,
        k.T,
        ok,
        v.T,
        ov,
        mixer_grad,
        om,
        taps_grad,
        g1,
        s1,
        up_grad,
        ou,
        down_grad,
        od,
        g2,
        s2,
    )


def solution(mesh):
    placed = (
        P("seq", None),
        P(None, "hid"),
        P("hid"),
        P(None, "hid"),
        P("hid"),
        P(None, "hid"),
        P("hid"),
        P("hid", None),
        P(),
        P("hid", None),
        P(),
        P(),
        P(None, "hid"),
        P("hid"),
        P("hid", None),
        P(),
        P(),
        P(),
        P(),
        P(),
        P(),
        P("seq", None),
    )
    return jax.shard_map(
        on_device,
        mesh=mesh,
        in_specs=placed,
        out_specs=(
            P("seq", None),
            P("seq", None),
            P(None, "hid"),
            P("hid"),
            P(None, "hid"),
            P("hid"),
            P(None, "hid"),
            P("hid"),
            P("hid", None),
            P(),
            P("hid", None),
            P(),
            P(),
            P(None, "hid"),
            P("hid"),
            P("hid", None),
            P(),
            P(),
            P(),
        ),
        check_vma=False,
    )
```

```python
import functools
import math

import jax
import jax.numpy as jnp
from jax import lax
from jax.experimental import pallas as pl
from jax.experimental.pallas import tpu as pltpu
from jax.sharding import PartitionSpec as P

D = 768
H = 12
HS = 64
BITS = 8
PLANES = 32
HASHES = 4
CONV = 35
RADIUS = 17
FEATS = HASHES * 2**BITS
SHARP = 2.0
NORM_EPS = 1e-05
UNIT_EPS = 1e-06
EXACT = lax.Precision.HIGHEST
F32 = jnp.float32
BF16 = jnp.bfloat16
ROWS = 256
HEADS = 3
KEPT = PLANES + HS
TAP_LANE = 111
VMEM = pl.BlockSpec(memory_space=pltpu.VMEM)
SMEM = pl.BlockSpec(memory_space=pltpu.SMEM)
LIMIT = 60 * 1024 * 1024


def dot(a, b):
    return lax.dot_general(a, b, (((1,), (0,)), ((), ())), preferred_element_type=F32)


def dot_nt(a, b):
    return lax.dot_general(a, b, (((1,), (1,)), ((), ())), preferred_element_type=F32)


def dot_tn(a, b):
    return lax.dot_general(a, b, (((0,), (0,)), ((), ())), preferred_element_type=F32)


def dot_exact(a, b):
    return lax.dot_general(
        a, b, (((1,), (0,)), ((), ())), precision=EXACT, preferred_element_type=F32
    )


def doc_count(pos, lengths):
    start = jnp.int32(0)
    found = jnp.zeros_like(pos)
    for d in range(lengths.shape[0]):
        found = found + (pos >= start).astype(jnp.int32)
        start = start + lengths[d]
    return found + (pos >= start).astype(jnp.int32)


def doc_range(block, lengths):
    return doc_count(block * ROWS, lengths), doc_count(block * ROWS + (ROWS - 1), lengths)


def doc_mask(block, doc, lengths):
    pos = block * ROWS + lax.broadcasted_iota(jnp.int32, (1, ROWS), 1)
    return (doc_count(pos, lengths) == doc).astype(F32)


def ones_rows():
    return (lax.broadcasted_iota(jnp.int32, (HS, ROWS), 0) < 2).astype(F32)


def add_states(n, mine, doc, lengths, codes, partners, phis, state):
    state[...] = jnp.zeros_like(state)

    def block(k, carry):
        other = jnp.bitwise_xor(mine, k)
        low, high = doc_range(other, lengths)

        @pl.when(jnp.logical_and(low <= doc, doc <= high))
        def _():
            mask = doc_mask(other, doc, lengths)
            for h in range(HEADS):
                lane = h * ROWS
                expand(codes[k, 0:PLANES, lane : lane + ROWS].astype(F32), phis[h])
                state[h] += dot_nt(phis[h][...], (partners(k, h) * mask).astype(BF16))

        return carry

    lax.fori_loop(0, n, block, 0)


def split_state(state, both):
    for row in range(0, FEATS, ROWS):
        part = state[row : row + ROWS, :]
        high = part.astype(BF16)
        both[row : row + ROWS, 0:128] = high
        both[row : row + ROWS, 128:256] = (part - high.astype(F32)).astype(BF16)


def own_feats(pack, row, feats):
    for h in range(HEADS):
        picks = pack[row : row + PLANES, h * ROWS : (h + 1) * ROWS].astype(F32)
        expand(picks, feats.at[h])


def with_ones(values, mask):
    rows = jnp.concatenate([values, ones_rows()], axis=0) * mask
    rows = rows.astype(BF16)
    return jnp.concatenate([rows, rows], axis=0)


def same_doc(row_start, rows, col_start, cols, lengths, reverse=False):
    rid = row_start + lax.broadcasted_iota(jnp.int32, (rows, 1), 0)
    cid = lax.broadcasted_iota(jnp.int32, (1, cols), 1)
    cid = col_start + ((cols - 1) - cid if reverse else cid)
    return doc_count(rid, lengths) == doc_count(cid, lengths)


def hash_base(picks, m, lanes):
    bit = lax.broadcasted_iota(jnp.int32, (8, lanes), 0)
    factors = []
    for b in range(3):
        on = (bit & (1 << b)) != 0
        row = jnp.broadcast_to(picks[m * BITS + b : m * BITS + b + 1, :], (8, lanes))
        factors.append((on, jnp.where(on, row, 1.0)))
    return factors


def hash_feats(picks, m, lanes, bits=BITS):
    factors = hash_base(picks, m, lanes)
    scale = 2.0 ** (-0.5 * BITS)
    feats = [(factors[0][1] * scale) * (factors[1][1] * factors[2][1])]
    rows = {}
    for b in range(3, bits):
        rows[b] = jnp.broadcast_to(picks[m * BITS + b : m * BITS + b + 1, :], (8, lanes))
        feats = feats + [f * rows[b] for f in feats]
    return feats, rows, factors


def expand(picks, phi_ref):
    lanes = picks.shape[1]
    for m in range(HASHES):
        feats = hash_feats(picks, m, lanes, BITS - 1)[0]
        last = m * BITS + BITS - 1
        row = jnp.broadcast_to(picks[last : last + 1, :], (16, lanes)).astype(BF16)
        for i in range(0, len(feats), 2):
            both = jnp.concatenate([feats[i], feats[i + 1]], axis=0).astype(BF16)
            at = m * 256 + i * 8
            phi_ref[at : at + 16, :] = both
            phi_ref[at + 128 : at + 144, :] = both * row


def expand_back(picks, dphi_ref, lane0, lanes):
    out = []
    scale = 2.0 ** (-0.5 * BITS)
    for m in range(HASHES):
        feats, rows, factors = hash_feats(picks, m, lanes)
        grads = [
            dphi_ref[m * 256 + i * 8 : m * 256 + i * 8 + 8, lane0 : lane0 + lanes]
            for i in range(32)
        ]
        found = {}
        for b in range(BITS - 1, 2, -1):
            half = len(grads) // 2
            total = grads[half] * feats[0]
            for i in range(1, half):
                total = total + grads[half + i] * feats[i]
            found[b] = jnp.sum(total, axis=0, keepdims=True)
            grads = [grads[i] + grads[half + i] * rows[b] for i in range(half)]
        g = grads[0] * scale
        (on0, f0), (on1, f1), (on2, f2) = factors
        found[0] = jnp.sum(jnp.where(on0, g * (f1 * f2), 0.0), axis=0, keepdims=True)
        found[1] = jnp.sum(jnp.where(on1, g * (f0 * f2), 0.0), axis=0, keepdims=True)
        found[2] = jnp.sum(jnp.where(on2, g * (f0 * f1), 0.0), axis=0, keepdims=True)
        out.extend(found[b] for b in range(BITS))
    return jnp.concatenate(out, axis=0)


def stacked(turned):
    return jnp.concatenate([turned[:, h * ROWS : (h + 1) * ROWS] for h in range(HEADS)], axis=0)


def column(row):
    n = row.shape[1]
    here = lax.broadcasted_iota(jnp.int32, (n, n), 0) == lax.broadcasted_iota(jnp.int32, (n, n), 1)
    return jnp.sum(jnp.where(here, row, 0.0), axis=1, keepdims=True)


def beside(rows):
    return jnp.concatenate([rows[h * HS : (h + 1) * HS] for h in range(HEADS)], axis=1)


def project_body(
    tokens, wq, bq, wk, bk, wv, bv, planes, choose, raw_q, raw_k, tan_q, tan_k, pack
):
    x = tokens[...]

    def codes(w, b, raw_ref, tan_ref):
        raw = beside(dot_nt(w[...], x) + column(b[...].reshape(1, -1)))
        raw_ref[...] = raw
        unit = raw * lax.rsqrt(jnp.sum(raw * raw, axis=0, keepdims=True) + UNIT_EPS)
        tan = jnp.tanh(SHARP * dot_exact(planes[...], unit))
        tan_ref[...] = tan
        return dot(choose[...], tan.astype(BF16)).astype(BF16)

    pack[0:PLANES, :] = codes(wk, bk, raw_k, tan_k)
    values = beside(dot_nt(wv[...], x) + column(bv[...].reshape(1, -1)))
    pack[PLANES : PLANES + HS, :] = values.astype(BF16)
    pack[KEPT:, :] = codes(wq, bq, raw_q, tan_q)


def call(body, name, out_shape, ins, smem=0, scratch=(), us=2):
    single = not isinstance(out_shape, (tuple, list))
    outs = (out_shape,) if single else tuple(out_shape)
    got = pl.pallas_call(
        body,
        out_shape=outs,
        in_specs=[SMEM] * smem + [VMEM] * (len(ins) - smem),
        out_specs=tuple([VMEM] * len(outs)),
        scratch_shapes=list(scratch),
        name=name,
        compiler_params=pltpu.CompilerParams(vmem_limit_bytes=LIMIT),
        cost_estimate=pl.CostEstimate(
            flops=int(us * 1e9), bytes_accessed=100_000, transcendentals=0
        ),
    )(*ins)
    return got[0] if single else got


def f32(*shape):
    return jax.ShapeDtypeStruct(shape, F32)


def bf16(*shape):
    return jax.ShapeDtypeStruct(shape, BF16)


def project(*ins):
    wide = HEADS * ROWS
    return call(
        project_body,
        "project",
        (
            f32(HS, wide),
            f32(HS, wide),
            f32(PLANES, wide),
            f32(PLANES, wide),
            bf16(KEPT + PLANES, wide),
        ),
        ins,
        us=0.1,
    )


def window(packs, mine, low, high, n):
    def at(h):
        before = jnp.bitwise_xor(mine, jnp.maximum(mine - 1, 0))
        after = jnp.bitwise_xor(mine, jnp.minimum(mine + 1, n - 1))
        lane = h * ROWS
        return jnp.concatenate(
            [
                packs[before, low:high, lane + 128 : lane + 256],
                packs[0, low:high, lane : lane + 256],
                packs[after, low:high, lane : lane + 128],
            ],
            axis=1,
        )

    return at


def band(row):
    return pltpu.roll(jnp.broadcast_to(row, (ROWS, 512)), 0, 1, stride=1, stride_axis=0)


def split_dot(a, b, mul):
    high = a.astype(BF16)
    low = (a - high.astype(F32)).astype(BF16)
    return mul(high, b) + mul(low, b)


def forward_body(n, lengths, place, slot, taps, *refs):
    pack_in, (context, near_half, far_half, weighted, total_out, states) = refs[:n], refs[n : n + 6]
    packs, phi0, phi1, phi2, feats, state, acc = refs[n + 6 :]
    phis = (phi0, phi1, phi2)
    mine = place[0]
    for k in range(n):
        packs[k] = pack_in[k][0:KEPT, :]
    acc[...] = jnp.zeros_like(acc)
    own_feats(pack_in[0], KEPT, feats)
    first, last = doc_range(mine, lengths)

    def values(k, h):
        rows = packs[k, PLANES:KEPT, h * ROWS : (h + 1) * ROWS].astype(F32)
        return jnp.concatenate([rows, ones_rows()], axis=0)

    def document(doc, carry):
        add_states(n, mine, doc, lengths, packs, values, phis, state)
        mask = doc_mask(mine, doc, lengths)
        for h in range(HEADS):
            split_state(state.at[h], states.at[doc - 1, h])
            got = dot_tn(states[doc - 1, h], feats[h])
            acc[h] += (got[0:128] + got[128:256]) * mask
        return carry

    lax.fori_loop(first, last + 1, document, 0)
    near = same_doc(mine * ROWS, ROWS, mine * ROWS - 128, 512, lengths)
    ext = window(packs, mine, PLANES, KEPT, n)
    outs = []
    total_out[...] = jnp.zeros_like(total_out)
    for h in range(HEADS):
        sums = acc[h] * (1.0 / HASHES)
        total = 1.0 + sums[HS : HS + 1]
        taps_band = jnp.where(near, band(taps[h : h + 1, :]), 0.0)
        conv = split_dot(taps_band, ext(h), lambda a, b: dot_nt(b, a))
        total_out[h : h + 1, :] = total
        weighted[h * HS : (h + 1) * HS, :] = sums[0:HS]
        outs.append(sums[0:HS] / total + conv)
    context[...] = jnp.concatenate(outs, axis=0).T.astype(BF16)
    half = ROWS // 2
    first = slot[0] >> 1
    near_half[...] = context[pl.ds(pl.multiple_of(first * half, 16), half), :]
    far_half[...] = context[pl.ds(pl.multiple_of((1 - first) * half, 16), half), :]


def forward(lengths, place, slot, taps, packs):
    n = len(packs)
    wide = HEADS * HS
    return call(
        functools.partial(forward_body, n),
        "attend",
        (
            bf16(ROWS, wide),
            bf16(ROWS // 2, wide),
            bf16(ROWS // 2, wide),
            f32(wide, ROWS),
            f32(8, ROWS),
            bf16(lengths.shape[0], HEADS, FEATS, 256),
        ),
        (lengths, place, slot, taps, *packs),
        smem=3,
        scratch=(
            pltpu.VMEM((n, KEPT, HEADS * ROWS), BF16),
            pltpu.VMEM((FEATS, ROWS), BF16),
            pltpu.VMEM((FEATS, ROWS), BF16),
            pltpu.VMEM((FEATS, ROWS), BF16),
            pltpu.VMEM((HEADS, FEATS, ROWS), BF16),
            pltpu.VMEM((HEADS, FEATS, 128), F32),
            pltpu.VMEM((HEADS, 128, ROWS), F32),
        ),
        us=9,
    )


GROUP = 16


def grad_rows(grads, h):
    base = HEADS * HS + h * GROUP
    return grads[h * HS : (h + 1) * HS].astype(F32), grads[base : base + GROUP].astype(F32)


def grad_partners(grads, h):
    rows, side = grad_rows(grads, h)
    return jnp.concatenate([rows, side, jnp.zeros((HS - GROUP, rows.shape[1]), F32)], axis=0)


def unit_back(code_grad, tan, raw, planes_t):
    scale = lax.rsqrt(jnp.sum(raw * raw, axis=0, keepdims=True) + UNIT_EPS)
    unit_grad = dot_exact(planes_t, code_grad * (SHARP * (1.0 - tan * tan)))
    inner = jnp.sum(raw * unit_grad, axis=0, keepdims=True)
    return unit_grad * scale - raw * (scale * scale * scale) * inner


def codes_to_raw(dphi, pack, row, tan, raw, choose_back, planes_t):
    parts = []
    for h in range(HEADS):
        for u in range(2):
            lane = h * ROWS + u * 128
            parts.append(
                expand_back(
                    pack[row : row + PLANES, lane : lane + 128].astype(F32), dphi.at[h], u * 128, 128
                )
            )
    pick_grad = jnp.concatenate(parts, axis=1) * (1.0 / HASHES)
    code_grad = dot_exact(choose_back[...], pick_grad)
    return unit_back(code_grad, tan[...], raw[...], planes_t[...])


def query_back_body(
    n, lengths, place, grads, states, tan, raw, choose_back, planes_t, weight, *refs
):
    pack_in, (grad_out, input_out, taps_out) = refs[:n], refs[n : n + 3]
    packs, dphi = refs[n + 3 :]
    mine = place[0]
    for k in range(n):
        packs[k] = pack_in[k][PLANES:KEPT, :]
    dphi[...] = jnp.zeros_like(dphi)
    first, last = doc_range(mine, lengths)

    def document(doc, carry):
        mask = doc_mask(mine, doc, lengths)
        for h in range(HEADS):
            rows = (grad_partners(grads[...], h) * mask).astype(BF16)
            dphi[h] += dot(states[doc - 1, h], jnp.concatenate([rows, rows], axis=0))
        return carry

    lax.fori_loop(first, last + 1, document, 0)
    raw_grad = codes_to_raw(dphi, pack_in[0], KEPT, tan, raw, choose_back, planes_t)
    turned = stacked(raw_grad).astype(BF16)
    grad_out[...] = turned
    input_out[...] = dot(turned.astype(F32).T.astype(BF16), weight[...])
    near_rev = same_doc(mine * ROWS, ROWS, mine * ROWS - 128, 512, lengths, reverse=True)
    turn = lax.broadcasted_iota(jnp.int32, (512, 512), 0) + lax.broadcasted_iota(
        jnp.int32, (512, 512), 1
    )
    flip = (turn == 511).astype(F32)
    flip_low = flip.astype(BF16)
    ext = window(packs, mine, 0, HS, n)
    tap_rows = []
    for h in range(HEADS):
        rows, side = grad_rows(grads[...], h)
        context_grad = (rows * side[2:3]).astype(BF16)
        flipped = dot(ext(h), flip_low).astype(BF16)
        cross = jnp.where(near_rev, dot_tn(context_grad, flipped), 0.0)
        cross = pltpu.roll(cross, 0, 1, stride=1, stride_axis=0)
        tap_rows.append(jnp.sum(cross, axis=0, keepdims=True))
    tap_rows.append(jnp.zeros((8 - HEADS, 512), F32))
    taps_out[...] = dot_exact(jnp.concatenate(tap_rows, axis=0), flip)


def query_back(*ins):
    packs = ins[-1]
    n = len(packs)
    return call(
        functools.partial(query_back_body, n),
        "query_back",
        (bf16(HEADS * HS, ROWS), f32(ROWS, D), f32(8, 512)),
        (*ins[:-1], *packs),
        smem=2,
        scratch=(
            pltpu.VMEM((n, HS, HEADS * ROWS), BF16),
            pltpu.VMEM((HEADS, FEATS, ROWS), F32),
        ),
        us=6,
    )


def key_back_body(
    n,
    lengths,
    place,
    slot,
    tan,
    raw,
    taps_back,
    choose_back,
    planes_t,
    wk,
    wv,
    query_input,
    query_turned,
    dh1,
    *refs,
):
    pack_in, grad_in = refs[:n], refs[n : 2 * n]
    pack = pack_in[0]
    turned_out, input_mine, input_other = refs[2 * n : 2 * n + 3]
    picks, grads, phi0, phi1, phi2, feats, state, both, dphi, acc, inputs = refs[2 * n + 3 :]
    phis = (phi0, phi1, phi2)
    mine = place[0]
    for k in range(n):
        picks[k] = pack_in[k][KEPT:, :]
        grads[k] = grad_in[k][...]
    dphi[...] = jnp.zeros_like(dphi)
    acc[...] = jnp.zeros_like(acc)
    own_feats(pack, 0, feats)
    first, last = doc_range(mine, lengths)

    def document(doc, carry):
        add_states(
            n, mine, doc, lengths, picks, lambda k, h: grad_partners(grads[k], h), phis, state
        )
        mask = doc_mask(mine, doc, lengths)
        for h in range(HEADS):
            split_state(state.at[h], both)
            values = pack[PLANES:KEPT, h * ROWS : (h + 1) * ROWS].astype(F32)
            dphi[h] += dot(both[...], with_ones(values, mask))
            got = dot_tn(both[...], feats[h])
            acc[h] += (got[0:HS] + got[128 : 128 + HS]) * (mask * (1.0 / HASHES))
        return carry

    lax.fori_loop(first, last + 1, document, 0)
    raw_grad = codes_to_raw(dphi, pack, 0, tan, raw, choose_back, planes_t)
    key_turned = stacked(raw_grad).astype(BF16)
    key_rows = key_turned.astype(F32).T

    before = jnp.bitwise_xor(mine, jnp.maximum(mine - 1, 0))
    after = jnp.bitwise_xor(mine, jnp.minimum(mine + 1, n - 1))
    near = same_doc(mine * ROWS, ROWS, mine * ROWS - 128, 512, lengths)
    ext = jnp.concatenate([grads[before, :, 128:], grads[0], grads[after, :, :128]], axis=1)
    outs = []
    for h in range(HEADS):
        rows, side = grad_rows(ext, h)
        context_grad = (rows * side[2:3]).astype(BF16)
        taps_band = jnp.where(near, band(taps_back[h : h + 1, :]), 0.0)
        outs.append(acc[h] + split_dot(taps_band, context_grad, lambda a, b: dot_nt(b, a)))
    value_turned = jnp.concatenate(outs, axis=0).astype(BF16)
    value_rows = value_turned.astype(F32).T.astype(BF16)
    wide = HEADS * HS
    turned_out[0:wide, :] = query_turned[...]
    turned_out[wide : 2 * wide, :] = key_turned
    turned_out[2 * wide :, :] = value_turned
    inputs[...] = query_input[...] + dot(key_rows.astype(BF16), wk[...]) + dot(value_rows, wv[...])
    rows = dh1.shape[0]
    own = pl.ds(pl.multiple_of(slot[0] * rows, 16), rows)
    inputs[own, :] = inputs[own, :] + dh1[...]
    half = input_mine.shape[0]
    kept = slot[0] >> 1
    input_mine[...] = inputs[pl.ds(pl.multiple_of(kept * half, 16), half), :].astype(BF16)
    input_other[...] = inputs[pl.ds(pl.multiple_of((1 - kept) * half, 16), half), :].astype(BF16)


def key_back(ins, packs, grads):
    n = len(packs)
    return call(
        functools.partial(key_back_body, n),
        "key_back",
        (bf16(3 * HEADS * HS, ROWS), *[bf16(ROWS // 2, D)] * 2),
        (*ins, *packs, *grads),
        smem=3,
        scratch=(
            pltpu.VMEM((n, PLANES, HEADS * ROWS), BF16),
            pltpu.VMEM((n, HEADS * (HS + GROUP), ROWS), BF16),
            pltpu.VMEM((FEATS, ROWS), BF16),
            pltpu.VMEM((FEATS, ROWS), BF16),
            pltpu.VMEM((FEATS, ROWS), BF16),
            pltpu.VMEM((HEADS, FEATS, ROWS), BF16),
            pltpu.VMEM((HEADS, FEATS, 128), F32),
            pltpu.VMEM((FEATS, ROWS), BF16),
            pltpu.VMEM((HEADS, FEATS, ROWS), F32),
            pltpu.VMEM((HEADS, HS, ROWS), F32),
            pltpu.VMEM((ROWS, D), F32),
        ),
        us=12,
    )


def padded(rows, n):
    return -(-rows // (16 * n)) * (16 * n)


def put_halves(place, whole, mine, other):
    half = whole.shape[0] // 2
    core = place & 1
    mine[...] = whole[pl.ds(pl.multiple_of(core * half, 16), half), :]
    other[...] = whole[pl.ds(pl.multiple_of((1 - core) * half, 16), half), :]


def put_chunks(index, whole, outs):
    rows = outs[0].shape[0]
    for k, out in enumerate(outs):
        start = pl.multiple_of(jnp.bitwise_xor(index, k) * rows, 16)
        out[...] = whole[pl.ds(start, rows), :]


def swap(value, axis, k):
    n = lax.axis_size(axis)
    return lax.ppermute(value, axis, [(i, i ^ k) for i in range(n)])


def cross_chips(value):
    return [value] + [swap(value, "seq", k) for k in range(2, lax.axis_size("seq"), 2)]


def from_partner(blocks):
    got = []
    for block in blocks:
        got += [block, swap(block, "seq", 1)]
    return got


def over_seq(value):
    return from_partner(cross_chips(value))


def after(value, then):
    return lax.optimization_barrier((value, then))


HID_ORDER = (0, 2, 1, 3)


def hid_swap(value, j):
    return swap(value, "hid", HID_ORDER[j])


def far_swap(value):
    chips, parts = lax.axis_size("seq"), lax.axis_size("hid")
    pairs = []
    for s in range(chips):
        flip = HID_ORDER[3] if s % 2 else HID_ORDER[1]
        pairs += [(s * parts + h, s * parts + (h ^ flip)) for h in range(parts)]
    return lax.ppermute(value, ("seq", "hid"), pairs)


def over_hid(value):
    return [value] + [hid_swap(value, j) for j in range(1, len(HID_ORDER))]


def exchange(chunks):
    return [chunks[0]] + [hid_swap(chunks[j], j) for j in range(1, len(chunks))]


def flat(ref):
    return ref[...].reshape(1, -1)


def norm_stats(rows):
    center = rows - jnp.mean(rows, axis=-1, keepdims=True)
    inverse = lax.rsqrt(jnp.mean(center * center, axis=-1, keepdims=True) + NORM_EPS)
    return center * inverse, inverse


def norm_grad(grad, normed, inverse, gain):
    scaled = grad * gain
    return inverse * (
        scaled
        - jnp.mean(scaled, axis=-1, keepdims=True)
        - normed * jnp.mean(scaled * normed, axis=-1, keepdims=True)
    )


def column_sums(*rows):
    sums = [jnp.sum(r, axis=0, keepdims=True) for r in rows]
    return jnp.concatenate(sums + [jnp.zeros((8 - len(sums), D), F32)], axis=0)


def two_parts(sums):
    high = sums.astype(BF16).astype(F32)
    return jnp.concatenate([high, sums - high], axis=0).astype(BF16)


def bundle_body(place, up, down, mixer, shift, bundle):
    core = place[0] & 1
    size, rows = up.shape[0], mixer.shape[0] // 2

    @pl.when(core == 0)
    def _():
        bundle[0:size, :] = up[...]

    @pl.when(core == 1)
    def _():
        bundle[0:size, :] = down[...]

    mine = mixer[pl.ds(pl.multiple_of(core * rows, 16), rows), :]
    bundle[size : size + rows, :] = mine
    left = flat(shift)
    parts = []
    for _ in range(3):
        part = left.astype(BF16).astype(F32)
        parts.append(part)
        left = left - part
    parts.append(jnp.zeros((13, D), F32))
    bundle[size + rows :, :] = jnp.concatenate(parts, axis=0).astype(BF16)


def make_bundle(place, up, down, mixer, shift):
    rows = mixer.shape[0] // 2
    return call(
        bundle_body,
        "bundle",
        bf16(up.shape[0] + rows + 16, D),
        (place, up, down, mixer, shift),
        smem=1,
        us=20,
    )


def partner_weights(core, got, other, both):
    size = both.shape[1]
    both[core] = got[0:size, :]
    both[1 - core] = other[0:size, :]


def put_mixers(core, size, own, got, other, mine, theirs, mixers):
    rows = own.shape[0] // 2
    mixers[0] = own[...]
    start = pl.multiple_of(core * rows, 16)
    far = pl.multiple_of((1 - core) * rows, 16)
    mixers[2, pl.ds(start, rows), :] = got[size : size + rows, :]
    mixers[2, pl.ds(far, rows), :] = other[size : size + rows, :]
    mixers[1 + 2 * core] = mine[...]
    mixers[3 - 2 * core] = theirs[...]


def gelu_parts(x):
    cdf = 0.5 * (1.0 + lax.erf(x * math.sqrt(0.5)))
    slope = cdf + x * (jnp.exp(-0.5 * x * x) * (1.0 / math.sqrt(2.0 * math.pi)))
    return (x * cdf).astype(BF16), slope


def keep_and_send(partial, quarter, keep, send):
    rows = keep.shape[0]
    keep[...] = partial[pl.ds(pl.multiple_of(quarter * rows, 8), rows), :]
    other = pl.multiple_of((1 - quarter) * rows, 8)
    send[...] = partial[pl.ds(other, rows), :].astype(BF16)


def feed_body(parts, place, slot, *refs):
    tokens, mixer_shift, gain, shift, up, up_shift, down, got, other, mixer = refs[:10]
    far_mixer, other_mixer = refs[10:12]
    contexts = refs[12 : 12 + parts]
    first_mine, normed_mine, inverse_mine, low_out, slope_out, keep, send, mixers = refs[
        12 + parts : 20 + parts
    ]
    first, normed, inverse, partial, both = refs[20 + parts :]
    half = ROWS // 2
    core = place[0] & 1
    partner_weights(core, got, other, both)
    put_mixers(core, both.shape[1], mixer, got, other, far_mixer, other_mixer, mixers)
    mine = tokens[pl.ds(pl.multiple_of((slot[0] >> 1) * half, 16), half), :]
    mixed = flat(mixer_shift) + mine.astype(F32)
    for j, c in enumerate(contexts):
        mixed = mixed + dot(c[...], mixers[j])
    base = both.shape[1] + mixer.shape[0] // 2
    shift_rows = got[base : base + 16, :].astype(F32)
    far_shift = (shift_rows[0:1] + shift_rows[1:2]) + shift_rows[2:3]
    n1, r1 = norm_stats(mixed)
    rows1 = n1 * flat(gain) + flat(shift)
    first[...] = rows1
    normed[...] = n1
    inverse[...] = jnp.broadcast_to(r1, inverse.shape)
    low = rows1.astype(BF16)
    low_out[...] = low
    hidden, slope = gelu_parts(dot(low, up[...]) + flat(up_shift))
    slope_out[:, 0:D] = slope
    far_hidden, far_slope = gelu_parts(dot(low, both[0]) + far_shift)
    slope_out[:, D:] = far_slope
    partial[...] = dot(hidden, down[...]) + dot(far_hidden, both[1])
    quarter = slot[0] & 1
    keep_and_send(partial, quarter, keep, send)
    rows = first_mine.shape[0]
    start = pl.multiple_of(quarter * rows, 8)
    first_mine[...] = first[pl.ds(start, rows), :]
    normed_mine[...] = normed[pl.ds(start, rows), :]
    inverse_mine[...] = inverse[pl.ds(start, rows), :]


def second_body(slot, first, out_grad, down_shift, gain, shift, keep, got, layer, grad_out, low_out):
    rows = first.shape[0]
    total = first[...] + flat(down_shift) + keep[...] + got[...].astype(F32)
    n2, r2 = norm_stats(total)
    grad = out_grad[pl.ds(pl.multiple_of(slot[0] * rows, 8), rows), :]
    dh2 = norm_grad(grad, n2, r2, flat(gain))
    grad_out[...] = dh2
    low = dh2.astype(BF16)
    low_out[...] = low
    layer[0:rows, :] = (n2 * flat(gain) + flat(shift)).astype(BF16)
    layer[rows:, :] = two_parts(column_sums(grad * n2, grad, low.astype(F32)))


def feed_back_body(place, slot, slope, up, down, got, other, low_mine, low_got, low_half, keep, send, partial, both):
    partner_weights(place[0] & 1, got, other, both)
    quarter = slot[0] & 1
    take_chunks(quarter, (low_mine, low_got), low_half)
    low = low_half[...]
    near = (dot_nt(low, down[...]) * slope[:, 0:D]).astype(BF16)
    far = (dot_nt(low, both[1]) * slope[:, D:]).astype(BF16)
    partial[...] = dot_nt(near, up[...]) + dot_nt(far, both[0])
    keep_and_send(partial, quarter, keep, send)


def take_chunks(index, pieces, whole, first=0):
    rows = whole.shape[0] // len(pieces)
    for k, piece in enumerate(pieces):
        start = pl.multiple_of(jnp.bitwise_xor(index, k) * rows, 16)
        whole[pl.ds(start, rows), :] = piece[first : first + rows, :]


def first_back_body(parts, grad, normed, inverse, gain, keep, got, layer, mixers, *refs):
    dh1_out, payload = refs[:2]
    outs = refs[2:]
    total = grad[...] + keep[...] + got[...].astype(F32)
    n1 = normed[...]
    dh1 = norm_grad(total, n1, inverse[:, 0:1], flat(gain))
    dh1_out[...] = dh1
    low = dh1.astype(BF16)
    rows = dh1.shape[0]
    payload[0:rows, :] = low
    payload[rows : 2 * rows + 16, :] = layer[...]
    payload[2 * rows + 16 :, :] = two_parts(column_sums(total * n1, total, low.astype(F32)))
    for j, out in enumerate(outs):
        out[...] = dot_nt(low, mixers[j]).astype(BF16)


def split_body(parts, chunk, weighted, total, *refs):
    pieces, grad_pack, whole = refs[:parts], refs[parts], refs[parts + 1]
    take_chunks(chunk[0], pieces, whole)
    dctx = whole[...].astype(F32).T
    wide = HEADS * HS
    for h in range(HEADS):
        norm = total[h : h + 1, :]
        rows = dctx[h * HS : (h + 1) * HS]
        grad_pack[h * HS : (h + 1) * HS, :] = (rows / norm).astype(BF16)
        inner = jnp.sum(rows * weighted[h * HS : (h + 1) * HS, :], axis=0, keepdims=True)
        grad = -inner / (norm * norm)
        high = grad.astype(BF16).astype(F32)
        side = [high, grad - high, norm, jnp.zeros((GROUP - 3, ROWS), F32)]
        base = wide + h * GROUP
        grad_pack[base : base + GROUP, :] = jnp.concatenate(side, axis=0).astype(BF16)


def feed_grads_body(place, slot, low_mine, low_got, down_mine, down_got, up, up_shift, down, half_mine, half_other, sums, low_all, down_all):
    take_chunks(slot[0] >> 1, (low_mine, low_got), low_all)
    take_chunks(slot[0] >> 1, (down_mine, down_got), down_all)
    low, grad = low_all[...], down_all[...]
    hidden, slope = gelu_parts(dot(low, up[...]) + flat(up_shift))
    up_low = (dot_nt(grad, down[...]) * slope).astype(BF16)
    down_part = dot(hidden.T, grad).astype(BF16)
    up_part = dot(low.T, up_low).astype(BF16)
    core = place[0] & 1

    def put(first, second):
        first[0 : down_part.shape[0], :] = down_part
        second[0 : up_part.shape[0], :] = up_part

    pl.when(core == 0)(lambda: put(half_mine, half_other))
    pl.when(core == 1)(lambda: put(half_other, half_mine))
    sums[...] = jnp.broadcast_to(jnp.sum(up_low.astype(F32), axis=0, keepdims=True), sums.shape)


def mixer_grads_body(parts, place, slot, context, up_sums, taps, *refs):
    payloads = refs[:parts]
    half_mine, half_other, layer_out, whole, mixed = refs[parts:]
    wide = HEADS * HS
    rows = ROWS // parts
    take_chunks(slot[0], payloads, layer_out, rows)
    take_chunks(slot[0], payloads, mixed)

    def summed(row):
        total = jnp.zeros((8, D), F32)
        for r in payloads:
            total = total + r[row : row + 8, :].astype(F32) + r[row + 8 : row + 16, :].astype(F32)
        return total[0:3]

    context_t = context[...].astype(F32).T.astype(BF16)
    whole[0:wide, :] = dot(context_t, mixed[...]).astype(BF16)
    tap_block = jnp.concatenate([taps[0:HEADS, :], jnp.zeros((HEADS, D - 512), F32)], axis=1)
    small = jnp.concatenate(
        [summed(2 * rows), summed(2 * rows + 16), up_sums[0:1, :], tap_block, jnp.zeros((6, D), F32)],
        axis=0,
    )
    whole[wide : wide + 16, :] = small.astype(BF16)
    rest = whole.shape[0] - wide - 16
    if rest:
        whole[wide + 16 :, :] = jnp.zeros((rest, D), BF16)
    put_halves(place[0], whole, half_mine, half_other)


def halve_body(place, mine, other, *outs):
    rows = outs[0].shape[0]
    for k, out in enumerate(outs):
        start = pl.multiple_of(jnp.bitwise_xor(place[0] >> 1, k) * rows, 16)
        at = pl.ds(start, rows)
        out[...] = (mine[at, :].astype(F32) + other[at, :].astype(F32)).astype(BF16)


def settle_body(*refs):
    total = refs[0][...].astype(F32)
    for r in refs[1:-1]:
        total = total + r[...].astype(F32)
    refs[-1][...] = total.astype(BF16)


def join_body(place, *refs):
    take_chunks(place[0] >> 1, refs[:-1], refs[-1])


def chip_swaps(value, n):
    return [swap(value, "seq", 2 * k) for k in range(1, n // 2)]


def scatter_chips(mine, got, place, n):
    chips = n // 2
    half, width = mine.shape
    return call(
        halve_body,
        "halve",
        [bf16(half // chips, width)] * chips,
        (place, mine, got),
        smem=1,
    )


def halve_all_body(mine, other, out):
    out[...] = (mine[...].astype(F32) + other[...].astype(F32)).astype(BF16)


def total_body(place, *refs):
    pieces, out, stack = refs[:-2], refs[-2], refs[-1]
    for k, piece in enumerate(pieces):
        stack[jnp.bitwise_xor(place[0] >> 1, k)] = piece[...]
    total = stack[0].astype(F32)
    for k in range(1, len(pieces)):
        total = total + stack[k].astype(F32)
    out[...] = total.astype(BF16)


def total_chips(chip, got, place):
    terms = [chip] + list(got)
    return call(
        total_body,
        "total_small",
        bf16(*chip.shape),
        (place, *terms),
        smem=1,
        scratch=(pltpu.VMEM((len(terms), *chip.shape), BF16),),
    )


def both_halves(place, mine, other, whole):
    half = mine.shape[0]
    core = place & 1
    whole[pl.ds(pl.multiple_of(core * half, 16), half), :] = mine[...]
    whole[pl.ds(pl.multiple_of((1 - core) * half, 16), half), :] = other[...]


def finish_feed_body(place, mine, other, down, up):
    ff = down.shape[0]
    core = place[0] & 1

    def put(first, second):
        down[...] = first[0:ff, :].astype(F32)
        up[...] = second[0:D, :].astype(F32)

    pl.when(core == 0)(lambda: put(mine, other))
    pl.when(core == 1)(lambda: put(other, mine))


def finish_small_body(place, mine, other, mixer, g2, s2, od, g1, s1, om, ou, taps, whole):
    both_halves(place[0], mine, other, whole)
    wide = HEADS * HS
    mixer[...] = whole[0:wide, :].astype(F32)
    rows = whole[wide : wide + 16, :].astype(F32)
    for i, out in enumerate((g2, s2, od, g1, s1, om, ou)):
        out[...] = rows[i : i + 1, :].reshape(D)
    taps[...] = rows[7 : 7 + HEADS, TAP_LANE : TAP_LANE + CONV]


def weight_grads_body(n, *refs):
    blocks, tokens = refs[:n], refs[n : 2 * n]
    q, k, v, oq, ok, ov = refs[2 * n : 2 * n + 6]
    turned, rows = refs[2 * n + 6 :]
    wide = HEADS * HS
    for i in range(n):
        turned[:, i * ROWS : (i + 1) * ROWS] = blocks[i][...]
        rows[i * ROWS : (i + 1) * ROWS, :] = tokens[i][...]
    ones = jnp.ones((16, n * ROWS), BF16)
    for i, (grad, sums) in enumerate(((q, oq), (k, ok), (v, ov))):
        part = turned[i * wide : (i + 1) * wide, :]
        grad[...] = dot(part, rows[...])
        sums[...] = dot_nt(ones, part)[0:1, :].reshape(wide)


def tokens_sum_body(mine, other, out):
    out[...] = (mine[...].astype(F32) + other[...].astype(F32)).astype(BF16)


def tokens_out_body(slot, mine, other, out):
    half = mine.shape[0]
    kept = slot[0] >> 1
    out[pl.ds(pl.multiple_of(kept * half, 16), half), :] = mine[...].astype(F32)
    out[pl.ds(pl.multiple_of((1 - kept) * half, 16), half), :] = other[...].astype(F32)


def on_device(
    tokens,
    query_weight,
    query_shift,
    key_weight,
    key_shift,
    value_weight,
    value_shift,
    mixer_weight,
    mixer_shift,
    conv_taps,
    first_gain,
    first_shift,
    up_weight,
    up_shift,
    down_weight,
    down_shift,
    second_gain,
    second_shift,
    hyperplanes,
    plane_choice,
    doc_lengths,
    out_grad,
):
    n = lax.axis_size("seq")
    parts = lax.axis_size("hid")
    place = lax.axis_index("seq").reshape(1).astype(jnp.int32)
    hid = lax.axis_index("hid")
    slot = sum(jnp.where(hid == h, HID_ORDER[h], 0) for h in range(parts))
    slot = slot.reshape(1).astype(jnp.int32)
    rows, half = ROWS // parts, ROWS // 2
    units, wide = up_weight.shape[1], HEADS * HS
    hot = plane_choice.reshape(-1, 1) == jnp.arange(PLANES, dtype=jnp.int32)
    choose = hot.astype(BF16)
    choose_back = hot.astype(F32).T
    planes_t = hyperplanes.T
    wq, wk, wv = query_weight.T, key_weight.T, value_weight.T
    side = (TAP_LANE, 512 - TAP_LANE - CONV)
    taps = jnp.pad(conv_taps, ((0, 5), side))
    taps_back = jnp.pad(conv_taps[:, ::-1], ((0, 5), side))

    far_mixer = far_swap(mixer_weight)
    bundle = make_bundle(place, up_weight, down_weight, mixer_weight, up_shift)
    got = hid_swap(bundle, 2)

    raw_q, raw_k, tan_q, tan_k, pack = project(
        tokens, wq, query_shift, wk, key_shift, wv, value_shift, hyperplanes, choose
    )
    (far_mixer, taps, taps_back, planes_t), pack = after(
        (far_mixer, taps, taps_back, planes_t), pack
    )
    other_mixer = swap(far_mixer, "seq", 1)
    packs = over_seq(pack)
    context, near_half, far_half, weighted, total, states = forward(
        doc_lengths, place, slot, taps, packs
    )
    contexts = [
        near_half,
        hid_swap(near_half, 1),
        hid_swap(far_half, 2),
        hid_swap(far_half, 3),
    ]
    got, contexts[1] = after(got, contexts[1])
    other = swap(got, "seq", 1)
    first_mine, normed_mine, inverse_mine, low, slope, keep, send, mixers = call(
        functools.partial(feed_body, parts),
        "feed",
        (
            f32(rows, D),
            f32(rows, D),
            f32(rows, 128),
            bf16(half, D),
            f32(half, 2 * units),
            f32(rows, D),
            bf16(rows, D),
            bf16(parts, wide, D),
        ),
        (
            place,
            slot,
            tokens,
            mixer_shift,
            first_gain,
            first_shift,
            up_weight,
            up_shift,
            down_weight,
            got,
            other,
            mixer_weight,
            far_mixer,
            other_mixer,
            *contexts,
        ),
        smem=2,
        scratch=(
            pltpu.VMEM((half, D), F32),
            pltpu.VMEM((half, D), F32),
            pltpu.VMEM((half, 128), F32),
            pltpu.VMEM((half, D), F32),
            pltpu.VMEM((2, D, units), BF16),
        ),
        us=5,
    )
    partial = hid_swap(send, 1)
    tokens_later, keep = after(tokens, keep)
    token_blocks = cross_chips(tokens_later)
    layer, dh2, down_low = call(
        second_body,
        "second_norm",
        (bf16(rows + 16, D), f32(rows, D), bf16(rows, D)),
        (
            slot,
            first_mine,
            out_grad,
            down_shift,
            second_gain,
            second_shift,
            keep,
            partial,
        ),
        smem=1,
    )
    down_half, keep, send = call(
        feed_back_body,
        "feed_back",
        (bf16(half, D), f32(rows, D), bf16(rows, D)),
        (
            place,
            slot,
            slope,
            up_weight,
            down_weight,
            got,
            other,
            down_low,
            hid_swap(down_low, 1),
        ),
        smem=2,
        scratch=(pltpu.VMEM((half, D), F32), pltpu.VMEM((2, D, units), BF16)),
        us=0.5,
    )
    token_blocks, mixers = after(token_blocks, mixers)
    first_back = call(
        functools.partial(first_back_body, parts),
        "first_norm_back",
        (f32(rows, D), bf16(2 * rows + 32, D), *[bf16(rows, wide)] * parts),
        (dh2, normed_mine, inverse_mine, first_gain, keep, hid_swap(send, 1), layer, mixers),
        us=3,
    )
    dh1, payload = first_back[:2]
    pieces = exchange(first_back[2:])
    feed_half = padded(2 * max(units, D), n) // 2
    feed_mine, feed_other, up_sums = call(
        feed_grads_body,
        "feed_grads",
        (bf16(feed_half, D), bf16(feed_half, D), f32(8, units)),
        (
            place,
            slot,
            low,
            hid_swap(low, 2),
            down_half,
            hid_swap(down_half, 2),
            up_weight,
            up_shift,
            down_weight,
        ),
        smem=2,
        scratch=(
            pltpu.VMEM((ROWS, D), BF16),
            pltpu.VMEM((ROWS, D), BF16),
        ),
        us=6,
    )
    pieces, feed_other = after(pieces, feed_other)
    grad_pack = call(
        functools.partial(split_body, parts),
        "split",
        bf16(HEADS * (HS + GROUP), ROWS),
        (slot, weighted, total, *pieces),
        smem=1,
        scratch=(pltpu.VMEM((ROWS, wide), BF16),),
    )
    payload, grad_pack = after(payload, grad_pack)
    grad_blocks = cross_chips(grad_pack)
    feed_pieces = scatter_chips(feed_mine, swap(feed_other, "seq", 1), place, n)
    feed_got = [swap(feed_pieces[k], "seq", 2 * k) for k in range(1, n // 2)]
    feed_own, tan_q = after(feed_pieces[0], tan_q)
    query_turned, query_input, tap_rows = query_back(
        doc_lengths,
        place,
        grad_pack,
        states,
        tan_q,
        raw_q,
        choose_back,
        planes_t,
        wq,
        packs,
    )
    grad_blocks, query_turned = after(grad_blocks, query_turned)
    grad_packs = from_partner(grad_blocks)
    payloads = over_hid(payload)
    settled = call(settle_body, "settle", bf16(*feed_own.shape), (feed_own, *feed_got))
    small_half = -(-(wide + 16) // 32) * 16
    small_mine, small_other, layer_out = call(
        functools.partial(mixer_grads_body, parts),
        "mixer_grads",
        (bf16(small_half, D), bf16(small_half, D), bf16(ROWS, D)),
        (place, slot, context, up_sums, tap_rows, *payloads),
        smem=2,
        scratch=(pltpu.VMEM((2 * small_half, D), BF16), pltpu.VMEM((ROWS, D), BF16)),
    )
    (settled, small_other), grad_packs = after((settled, small_other), grad_packs)
    small_got = swap(small_other, "seq", 1)
    feed_chips = chip_swaps(settled, n)
    last = key_back(
        (
            doc_lengths,
            place,
            slot,
            tan_k,
            raw_k,
            taps_back,
            choose_back,
            planes_t,
            wk,
            wv,
            query_input,
            query_turned,
            dh1,
        ),
        packs,
        grad_packs,
    )
    last, (small_got, feed_chips) = after(last, (small_got, feed_chips))
    near_tokens = hid_swap(last[2], 2)
    blocks = over_seq(last[0])

    def tokens_sum(mine, other):
        return call(tokens_sum_body, "tokens_sum", bf16(half, D), (mine, other), us=0.3)

    both = tokens_sum(last[1], near_tokens)
    token_blocks, both = after(token_blocks, both)
    small_chip = call(halve_all_body, "halve_small", bf16(*small_mine.shape), (small_mine, small_got))
    both, small_chip = after(both, small_chip)
    feed_full = call(
        join_body, "join", bf16(feed_half, D), (place, settled, *feed_chips), smem=1, us=0.3
    )
    summed = tokens_sum(both, hid_swap(both, 1))
    summed, tokens_first = after(summed, tokens_later)
    tokens_grad = call(
        tokens_out_body, "tokens_out", f32(ROWS, D), (slot, summed, hid_swap(summed, 2)), smem=1
    )
    feed_sums = (feed_full, swap(feed_full, "seq", 1))
    small_full = total_chips(small_chip, chip_swaps(small_chip, n), place)
    small_sums = (small_full, swap(small_full, "seq", 1))
    token_blocks = from_partner(token_blocks)
    token_blocks[0] = tokens_first
    down_grad, up_grad = call(
        finish_feed_body,
        "finish_feed",
        (f32(units, D), f32(D, units)),
        (place, *feed_sums),
        smem=1,
        us=4,
    )
    mixer_grad, g2, s2, od, g1, s1, om, ou, taps_grad = call(
        finish_small_body,
        "finish_small",
        (f32(wide, D), *[f32(D)] * 6, f32(units), f32(HEADS, CONV)),
        (place, *small_sums),
        smem=1,
        scratch=(pltpu.VMEM((2 * small_half, D), BF16),),
    )
    q, k, v, oq, ok, ov = call(
        functools.partial(weight_grads_body, n),
        "weight_grads",
        (*[f32(wide, D)] * 3, *[f32(wide)] * 3),
        (*blocks, *token_blocks),
        scratch=(pltpu.VMEM((3 * wide, n * ROWS), BF16), pltpu.VMEM((n * ROWS, D), BF16)),
        us=0.3,
    )
    return (
        layer_out,
        tokens_grad,
        q.T,
        oq,
        k.T,
        ok,
        v.T,
        ov,
        mixer_grad,
        om,
        taps_grad,
        g1,
        s1,
        up_grad,
        ou,
        down_grad,
        od,
        g2,
        s2,
    )


def solution(mesh):
    placed = (
        P("seq", None),
        P(None, "hid"),
        P("hid"),
        P(None, "hid"),
        P("hid"),
        P(None, "hid"),
        P("hid"),
        P("hid", None),
        P(),
        P("hid", None),
        P(),
        P(),
        P(None, "hid"),
        P("hid"),
        P("hid", None),
        P(),
        P(),
        P(),
        P(),
        P(),
        P(),
        P("seq", None),
    )
    return jax.shard_map(
        on_device,
        mesh=mesh,
        in_specs=placed,
        out_specs=(
            P("seq", None),
            P("seq", None),
            P(None, "hid"),
            P("hid"),
            P(None, "hid"),
            P("hid"),
            P(None, "hid"),
            P("hid"),
            P("hid", None),
            P(),
            P("hid", None),
            P(),
            P(),
            P(None, "hid"),
            P("hid"),
            P("hid", None),
            P(),
            P(),
            P(),
        ),
        check_vma=False,
    )
```

```python
import functools
import math

import jax
import jax.numpy as jnp
from jax import lax
from jax.experimental import pallas as pl
from jax.experimental.pallas import tpu as pltpu
from jax.sharding import PartitionSpec as P

D = 768
H = 12
HS = 64
BITS = 8
PLANES = 32
HASHES = 4
CONV = 35
RADIUS = 17
FEATS = HASHES * 2**BITS
SHARP = 2.0
NORM_EPS = 1e-05
UNIT_EPS = 1e-06
EXACT = lax.Precision.HIGHEST
F32 = jnp.float32
BF16 = jnp.bfloat16
ROWS = 256
HEADS = 3
KEPT = PLANES + HS
TAP_LANE = 111
VMEM = pl.BlockSpec(memory_space=pltpu.VMEM)
SMEM = pl.BlockSpec(memory_space=pltpu.SMEM)
LIMIT = 60 * 1024 * 1024


def dot(a, b):
    return lax.dot_general(a, b, (((1,), (0,)), ((), ())), preferred_element_type=F32)


def dot_nt(a, b):
    return lax.dot_general(a, b, (((1,), (1,)), ((), ())), preferred_element_type=F32)


def dot_tn(a, b):
    return lax.dot_general(a, b, (((0,), (0,)), ((), ())), preferred_element_type=F32)


def dot_exact(a, b):
    return lax.dot_general(
        a, b, (((1,), (0,)), ((), ())), precision=EXACT, preferred_element_type=F32
    )


def doc_count(pos, lengths):
    start = jnp.int32(0)
    found = jnp.zeros_like(pos)
    for d in range(lengths.shape[0]):
        found = found + (pos >= start).astype(jnp.int32)
        start = start + lengths[d]
    return found + (pos >= start).astype(jnp.int32)


def doc_range(block, lengths):
    return doc_count(block * ROWS, lengths), doc_count(block * ROWS + (ROWS - 1), lengths)


def doc_mask(block, doc, lengths):
    pos = block * ROWS + lax.broadcasted_iota(jnp.int32, (1, ROWS), 1)
    return (doc_count(pos, lengths) == doc).astype(F32)


def ones_rows():
    return (lax.broadcasted_iota(jnp.int32, (HS, ROWS), 0) < 2).astype(F32)


def add_states(n, mine, doc, lengths, codes, partners, phis, state):
    state[...] = jnp.zeros_like(state)

    def block(k, carry):
        other = jnp.bitwise_xor(mine, k)
        low, high = doc_range(other, lengths)

        @pl.when(jnp.logical_and(low <= doc, doc <= high))
        def _():
            mask = doc_mask(other, doc, lengths)
            for h in range(HEADS):
                lane = h * ROWS
                expand(codes[k, 0:PLANES, lane : lane + ROWS].astype(F32), phis[h])
                state[h] += dot_nt(phis[h][...], (partners(k, h) * mask).astype(BF16))

        return carry

    lax.fori_loop(0, n, block, 0)


def split_state(state, both):
    for row in range(0, FEATS, ROWS):
        part = state[row : row + ROWS, :]
        high = part.astype(BF16)
        both[row : row + ROWS, 0:128] = high
        both[row : row + ROWS, 128:256] = (part - high.astype(F32)).astype(BF16)


def own_feats(pack, row, feats):
    for h in range(HEADS):
        picks = pack[row : row + PLANES, h * ROWS : (h + 1) * ROWS].astype(F32)
        expand(picks, feats.at[h])


def with_ones(values, mask):
    rows = jnp.concatenate([values, ones_rows()], axis=0) * mask
    rows = rows.astype(BF16)
    return jnp.concatenate([rows, rows], axis=0)


def same_doc(row_start, rows, col_start, cols, lengths, reverse=False):
    rid = row_start + lax.broadcasted_iota(jnp.int32, (rows, 1), 0)
    cid = lax.broadcasted_iota(jnp.int32, (1, cols), 1)
    cid = col_start + ((cols - 1) - cid if reverse else cid)
    return doc_count(rid, lengths) == doc_count(cid, lengths)


def hash_base(picks, m, lanes):
    bit = lax.broadcasted_iota(jnp.int32, (8, lanes), 0)
    factors = []
    for b in range(3):
        on = (bit & (1 << b)) != 0
        row = jnp.broadcast_to(picks[m * BITS + b : m * BITS + b + 1, :], (8, lanes))
        factors.append((on, jnp.where(on, row, 1.0)))
    return factors


def hash_feats(picks, m, lanes, bits=BITS):
    factors = hash_base(picks, m, lanes)
    scale = 2.0 ** (-0.5 * BITS)
    feats = [(factors[0][1] * scale) * (factors[1][1] * factors[2][1])]
    rows = {}
    for b in range(3, bits):
        rows[b] = jnp.broadcast_to(picks[m * BITS + b : m * BITS + b + 1, :], (8, lanes))
        feats = feats + [f * rows[b] for f in feats]
    return feats, rows, factors


def expand(picks, phi_ref):
    lanes = picks.shape[1]
    for m in range(HASHES):
        feats = hash_feats(picks, m, lanes, BITS - 1)[0]
        last = m * BITS + BITS - 1
        row = jnp.broadcast_to(picks[last : last + 1, :], (16, lanes)).astype(BF16)
        for i in range(0, len(feats), 2):
            both = jnp.concatenate([feats[i], feats[i + 1]], axis=0).astype(BF16)
            at = m * 256 + i * 8
            phi_ref[at : at + 16, :] = both
            phi_ref[at + 128 : at + 144, :] = both * row


def expand_back(picks, dphi_ref, lane0, lanes):
    out = []
    scale = 2.0 ** (-0.5 * BITS)
    for m in range(HASHES):
        feats, rows, factors = hash_feats(picks, m, lanes)
        grads = [
            dphi_ref[m * 256 + i * 8 : m * 256 + i * 8 + 8, lane0 : lane0 + lanes]
            for i in range(32)
        ]
        found = {}
        for b in range(BITS - 1, 2, -1):
            half = len(grads) // 2
            total = grads[half] * feats[0]
            for i in range(1, half):
                total = total + grads[half + i] * feats[i]
            found[b] = jnp.sum(total, axis=0, keepdims=True)
            grads = [grads[i] + grads[half + i] * rows[b] for i in range(half)]
        g = grads[0] * scale
        (on0, f0), (on1, f1), (on2, f2) = factors
        found[0] = jnp.sum(jnp.where(on0, g * (f1 * f2), 0.0), axis=0, keepdims=True)
        found[1] = jnp.sum(jnp.where(on1, g * (f0 * f2), 0.0), axis=0, keepdims=True)
        found[2] = jnp.sum(jnp.where(on2, g * (f0 * f1), 0.0), axis=0, keepdims=True)
        out.extend(found[b] for b in range(BITS))
    return jnp.concatenate(out, axis=0)


def stacked(turned):
    return jnp.concatenate([turned[:, h * ROWS : (h + 1) * ROWS] for h in range(HEADS)], axis=0)


def column(row):
    n = row.shape[1]
    here = lax.broadcasted_iota(jnp.int32, (n, n), 0) == lax.broadcasted_iota(jnp.int32, (n, n), 1)
    return jnp.sum(jnp.where(here, row, 0.0), axis=1, keepdims=True)


def beside(rows):
    return jnp.concatenate([rows[h * HS : (h + 1) * HS] for h in range(HEADS)], axis=1)


def project_body(
    tokens, wq, bq, wk, bk, wv, bv, planes, choose, raw_q, raw_k, tan_q, tan_k, pack
):
    x = tokens[...]

    def codes(w, b, raw_ref, tan_ref):
        raw = beside(dot_nt(w[...], x) + column(b[...].reshape(1, -1)))
        raw_ref[...] = raw
        unit = raw * lax.rsqrt(jnp.sum(raw * raw, axis=0, keepdims=True) + UNIT_EPS)
        tan = jnp.tanh(SHARP * dot_exact(planes[...], unit))
        tan_ref[...] = tan
        return dot(choose[...], tan.astype(BF16)).astype(BF16)

    pack[0:PLANES, :] = codes(wk, bk, raw_k, tan_k)
    values = beside(dot_nt(wv[...], x) + column(bv[...].reshape(1, -1)))
    pack[PLANES : PLANES + HS, :] = values.astype(BF16)
    pack[KEPT:, :] = codes(wq, bq, raw_q, tan_q)


def call(body, name, out_shape, ins, smem=0, scratch=(), us=2):
    single = not isinstance(out_shape, (tuple, list))
    outs = (out_shape,) if single else tuple(out_shape)
    got = pl.pallas_call(
        body,
        out_shape=outs,
        in_specs=[SMEM] * smem + [VMEM] * (len(ins) - smem),
        out_specs=tuple([VMEM] * len(outs)),
        scratch_shapes=list(scratch),
        name=name,
        compiler_params=pltpu.CompilerParams(vmem_limit_bytes=LIMIT),
        cost_estimate=pl.CostEstimate(
            flops=int(us * 1e9), bytes_accessed=100_000, transcendentals=0
        ),
    )(*ins)
    return got[0] if single else got


def f32(*shape):
    return jax.ShapeDtypeStruct(shape, F32)


def bf16(*shape):
    return jax.ShapeDtypeStruct(shape, BF16)


def project(*ins):
    wide = HEADS * ROWS
    return call(
        project_body,
        "project",
        (
            f32(HS, wide),
            f32(HS, wide),
            f32(PLANES, wide),
            f32(PLANES, wide),
            bf16(KEPT + PLANES, wide),
        ),
        ins,
        us=0.1,
    )


def window(packs, mine, low, high, n):
    def at(h):
        before = jnp.bitwise_xor(mine, jnp.maximum(mine - 1, 0))
        after = jnp.bitwise_xor(mine, jnp.minimum(mine + 1, n - 1))
        lane = h * ROWS
        return jnp.concatenate(
            [
                packs[before, low:high, lane + 128 : lane + 256],
                packs[0, low:high, lane : lane + 256],
                packs[after, low:high, lane : lane + 128],
            ],
            axis=1,
        )

    return at


def band(row):
    return pltpu.roll(jnp.broadcast_to(row, (ROWS, 512)), 0, 1, stride=1, stride_axis=0)


def split_dot(a, b, mul):
    high = a.astype(BF16)
    low = (a - high.astype(F32)).astype(BF16)
    return mul(high, b) + mul(low, b)


def forward_body(n, lengths, place, slot, taps, *refs):
    pack_in, (context, near_half, far_half, weighted, total_out, states) = refs[:n], refs[n : n + 6]
    packs, phi0, phi1, phi2, feats, state, acc = refs[n + 6 :]
    phis = (phi0, phi1, phi2)
    mine = place[0]
    for k in range(n):
        packs[k] = pack_in[k][0:KEPT, :]
    acc[...] = jnp.zeros_like(acc)
    own_feats(pack_in[0], KEPT, feats)
    first, last = doc_range(mine, lengths)

    def values(k, h):
        rows = packs[k, PLANES:KEPT, h * ROWS : (h + 1) * ROWS].astype(F32)
        return jnp.concatenate([rows, ones_rows()], axis=0)

    def document(doc, carry):
        add_states(n, mine, doc, lengths, packs, values, phis, state)
        mask = doc_mask(mine, doc, lengths)
        for h in range(HEADS):
            split_state(state.at[h], states.at[doc - 1, h])
            got = dot_tn(states[doc - 1, h], feats[h])
            acc[h] += (got[0:128] + got[128:256]) * mask
        return carry

    lax.fori_loop(first, last + 1, document, 0)
    near = same_doc(mine * ROWS, ROWS, mine * ROWS - 128, 512, lengths)
    ext = window(packs, mine, PLANES, KEPT, n)
    outs = []
    total_out[...] = jnp.zeros_like(total_out)
    for h in range(HEADS):
        sums = acc[h] * (1.0 / HASHES)
        total = 1.0 + sums[HS : HS + 1]
        taps_band = jnp.where(near, band(taps[h : h + 1, :]), 0.0)
        conv = split_dot(taps_band, ext(h), lambda a, b: dot_nt(b, a))
        total_out[h : h + 1, :] = total
        weighted[h * HS : (h + 1) * HS, :] = sums[0:HS]
        outs.append(sums[0:HS] / total + conv)
    context[...] = jnp.concatenate(outs, axis=0).T.astype(BF16)
    half = ROWS // 2
    first = slot[0] >> 1
    near_half[...] = context[pl.ds(pl.multiple_of(first * half, 16), half), :]
    far_half[...] = context[pl.ds(pl.multiple_of((1 - first) * half, 16), half), :]


def forward(lengths, place, slot, taps, packs):
    n = len(packs)
    wide = HEADS * HS
    return call(
        functools.partial(forward_body, n),
        "attend",
        (
            bf16(ROWS, wide),
            bf16(ROWS // 2, wide),
            bf16(ROWS // 2, wide),
            f32(wide, ROWS),
            f32(8, ROWS),
            bf16(lengths.shape[0], HEADS, FEATS, 256),
        ),
        (lengths, place, slot, taps, *packs),
        smem=3,
        scratch=(
            pltpu.VMEM((n, KEPT, HEADS * ROWS), BF16),
            pltpu.VMEM((FEATS, ROWS), BF16),
            pltpu.VMEM((FEATS, ROWS), BF16),
            pltpu.VMEM((FEATS, ROWS), BF16),
            pltpu.VMEM((HEADS, FEATS, ROWS), BF16),
            pltpu.VMEM((HEADS, FEATS, 128), F32),
            pltpu.VMEM((HEADS, 128, ROWS), F32),
        ),
        us=9,
    )


GROUP = 16


def grad_rows(grads, h):
    base = HEADS * HS + h * GROUP
    return grads[h * HS : (h + 1) * HS].astype(F32), grads[base : base + GROUP].astype(F32)


def grad_partners(grads, h):
    rows, side = grad_rows(grads, h)
    return jnp.concatenate([rows, side, jnp.zeros((HS - GROUP, rows.shape[1]), F32)], axis=0)


def unit_back(code_grad, tan, raw, planes_t):
    scale = lax.rsqrt(jnp.sum(raw * raw, axis=0, keepdims=True) + UNIT_EPS)
    unit_grad = dot_exact(planes_t, code_grad * (SHARP * (1.0 - tan * tan)))
    inner = jnp.sum(raw * unit_grad, axis=0, keepdims=True)
    return unit_grad * scale - raw * (scale * scale * scale) * inner


def codes_to_raw(dphi, pack, row, tan, raw, choose_back, planes_t):
    parts = []
    for h in range(HEADS):
        for u in range(2):
            lane = h * ROWS + u * 128
            parts.append(
                expand_back(
                    pack[row : row + PLANES, lane : lane + 128].astype(F32), dphi.at[h], u * 128, 128
                )
            )
    pick_grad = jnp.concatenate(parts, axis=1) * (1.0 / HASHES)
    code_grad = dot_exact(choose_back[...], pick_grad)
    return unit_back(code_grad, tan[...], raw[...], planes_t[...])


def diagonal_sums(rows):
    lanes = rows.shape[1]
    total = rows[0:8]
    for i in range(8, rows.shape[0], 8):
        total = total + pltpu.roll(rows[i : i + 8], lanes - i, 1)
    at = lax.broadcasted_iota(jnp.int32, (8, lanes), 0)
    out = jnp.where(at == 0, total, 0.0)
    for b in range(1, 8):
        out = out + jnp.where(at == b, pltpu.roll(total, lanes - b, 1), 0.0)
    return jnp.sum(out, axis=0, keepdims=True)


def query_back_body(
    n, lengths, place, grads, states, tan, raw, choose_back, planes_t, weight, *refs
):
    pack_in, (grad_out, input_out, taps_out) = refs[:n], refs[n : n + 3]
    packs, dphi = refs[n + 3 :]
    mine = place[0]
    for k in range(n):
        packs[k] = pack_in[k][PLANES:KEPT, :]
    dphi[...] = jnp.zeros_like(dphi)
    first, last = doc_range(mine, lengths)

    def document(doc, carry):
        mask = doc_mask(mine, doc, lengths)
        for h in range(HEADS):
            rows = (grad_partners(grads[...], h) * mask).astype(BF16)
            dphi[h] += dot(states[doc - 1, h], jnp.concatenate([rows, rows], axis=0))
        return carry

    lax.fori_loop(first, last + 1, document, 0)
    raw_grad = codes_to_raw(dphi, pack_in[0], KEPT, tan, raw, choose_back, planes_t)
    turned = stacked(raw_grad).astype(BF16)
    grad_out[...] = turned
    input_out[...] = dot(turned.astype(F32).T.astype(BF16), weight[...])
    near = same_doc(mine * ROWS, ROWS, mine * ROWS - 128, 512, lengths)
    ext = window(packs, mine, 0, HS, n)
    tap_rows = []
    for h in range(HEADS):
        rows, side = grad_rows(grads[...], h)
        context_grad = (rows * side[2:3]).astype(BF16)
        cross = jnp.where(near, dot_tn(context_grad, ext(h)), 0.0)
        tap_rows.append(diagonal_sums(cross))
    tap_rows.append(jnp.zeros((8 - HEADS, 512), F32))
    taps_out[...] = jnp.concatenate(tap_rows, axis=0)


def query_back(*ins):
    packs = ins[-1]
    n = len(packs)
    return call(
        functools.partial(query_back_body, n),
        "query_back",
        (bf16(HEADS * HS, ROWS), f32(ROWS, D), f32(8, 512)),
        (*ins[:-1], *packs),
        smem=2,
        scratch=(
            pltpu.VMEM((n, HS, HEADS * ROWS), BF16),
            pltpu.VMEM((HEADS, FEATS, ROWS), F32),
        ),
        us=6,
    )


def key_back_body(
    n,
    lengths,
    place,
    slot,
    tan,
    raw,
    taps_back,
    choose_back,
    planes_t,
    wk,
    wv,
    query_input,
    query_turned,
    dh1,
    *refs,
):
    pack_in, grad_in = refs[:n], refs[n : 2 * n]
    pack = pack_in[0]
    turned_out, input_mine, input_other = refs[2 * n : 2 * n + 3]
    picks, grads, phi0, phi1, phi2, feats, state, both, dphi, acc, inputs = refs[2 * n + 3 :]
    phis = (phi0, phi1, phi2)
    mine = place[0]
    for k in range(n):
        picks[k] = pack_in[k][KEPT:, :]
        grads[k] = grad_in[k][...]
    dphi[...] = jnp.zeros_like(dphi)
    acc[...] = jnp.zeros_like(acc)
    own_feats(pack, 0, feats)
    first, last = doc_range(mine, lengths)

    def document(doc, carry):
        add_states(
            n, mine, doc, lengths, picks, lambda k, h: grad_partners(grads[k], h), phis, state
        )
        mask = doc_mask(mine, doc, lengths)
        for h in range(HEADS):
            split_state(state.at[h], both)
            values = pack[PLANES:KEPT, h * ROWS : (h + 1) * ROWS].astype(F32)
            dphi[h] += dot(both[...], with_ones(values, mask))
            got = dot_tn(both[...], feats[h])
            acc[h] += (got[0:HS] + got[128 : 128 + HS]) * (mask * (1.0 / HASHES))
        return carry

    lax.fori_loop(first, last + 1, document, 0)
    raw_grad = codes_to_raw(dphi, pack, 0, tan, raw, choose_back, planes_t)
    key_turned = stacked(raw_grad).astype(BF16)
    key_rows = key_turned.astype(F32).T

    before = jnp.bitwise_xor(mine, jnp.maximum(mine - 1, 0))
    after = jnp.bitwise_xor(mine, jnp.minimum(mine + 1, n - 1))
    near = same_doc(mine * ROWS, ROWS, mine * ROWS - 128, 512, lengths)
    ext = jnp.concatenate([grads[before, :, 128:], grads[0], grads[after, :, :128]], axis=1)
    outs = []
    for h in range(HEADS):
        rows, side = grad_rows(ext, h)
        context_grad = (rows * side[2:3]).astype(BF16)
        taps_band = jnp.where(near, band(taps_back[h : h + 1, :]), 0.0)
        outs.append(acc[h] + split_dot(taps_band, context_grad, lambda a, b: dot_nt(b, a)))
    value_turned = jnp.concatenate(outs, axis=0).astype(BF16)
    value_rows = value_turned.astype(F32).T.astype(BF16)
    wide = HEADS * HS
    turned_out[0:wide, :] = query_turned[...]
    turned_out[wide : 2 * wide, :] = key_turned
    turned_out[2 * wide :, :] = value_turned
    inputs[...] = query_input[...] + dot(key_rows.astype(BF16), wk[...]) + dot(value_rows, wv[...])
    rows = dh1.shape[0]
    own = pl.ds(pl.multiple_of(slot[0] * rows, 16), rows)
    inputs[own, :] = inputs[own, :] + dh1[...]
    half = input_mine.shape[0]
    kept = slot[0] >> 1
    input_mine[...] = inputs[pl.ds(pl.multiple_of(kept * half, 16), half), :].astype(BF16)
    input_other[...] = inputs[pl.ds(pl.multiple_of((1 - kept) * half, 16), half), :].astype(BF16)


def key_back(ins, packs, grads):
    n = len(packs)
    return call(
        functools.partial(key_back_body, n),
        "key_back",
        (bf16(3 * HEADS * HS, ROWS), *[bf16(ROWS // 2, D)] * 2),
        (*ins, *packs, *grads),
        smem=3,
        scratch=(
            pltpu.VMEM((n, PLANES, HEADS * ROWS), BF16),
            pltpu.VMEM((n, HEADS * (HS + GROUP), ROWS), BF16),
            pltpu.VMEM((FEATS, ROWS), BF16),
            pltpu.VMEM((FEATS, ROWS), BF16),
            pltpu.VMEM((FEATS, ROWS), BF16),
            pltpu.VMEM((HEADS, FEATS, ROWS), BF16),
            pltpu.VMEM((HEADS, FEATS, 128), F32),
            pltpu.VMEM((FEATS, ROWS), BF16),
            pltpu.VMEM((HEADS, FEATS, ROWS), F32),
            pltpu.VMEM((HEADS, HS, ROWS), F32),
            pltpu.VMEM((ROWS, D), F32),
        ),
        us=12,
    )


def padded(rows, n):
    return -(-rows // (16 * n)) * (16 * n)


def put_halves(place, whole, mine, other):
    half = whole.shape[0] // 2
    core = place & 1
    mine[...] = whole[pl.ds(pl.multiple_of(core * half, 16), half), :]
    other[...] = whole[pl.ds(pl.multiple_of((1 - core) * half, 16), half), :]


def put_chunks(index, whole, outs):
    rows = outs[0].shape[0]
    for k, out in enumerate(outs):
        start = pl.multiple_of(jnp.bitwise_xor(index, k) * rows, 16)
        out[...] = whole[pl.ds(start, rows), :]


def swap(value, axis, k):
    n = lax.axis_size(axis)
    return lax.ppermute(value, axis, [(i, i ^ k) for i in range(n)])


def cross_chips(value):
    return [value] + [swap(value, "seq", k) for k in range(2, lax.axis_size("seq"), 2)]


def from_partner(blocks):
    got = []
    for block in blocks:
        got += [block, swap(block, "seq", 1)]
    return got


def over_seq(value):
    return from_partner(cross_chips(value))


def after(value, then):
    return lax.optimization_barrier((value, then))


HID_ORDER = (0, 2, 1, 3)


def hid_swap(value, j):
    return swap(value, "hid", HID_ORDER[j])


def far_swap(value):
    chips, parts = lax.axis_size("seq"), lax.axis_size("hid")
    pairs = []
    for s in range(chips):
        flip = HID_ORDER[3] if s % 2 else HID_ORDER[1]
        pairs += [(s * parts + h, s * parts + (h ^ flip)) for h in range(parts)]
    return lax.ppermute(value, ("seq", "hid"), pairs)


def over_hid(value):
    return [value] + [hid_swap(value, j) for j in range(1, len(HID_ORDER))]


def exchange(chunks):
    return [chunks[0]] + [hid_swap(chunks[j], j) for j in range(1, len(chunks))]


def flat(ref):
    return ref[...].reshape(1, -1)


def norm_stats(rows):
    center = rows - jnp.mean(rows, axis=-1, keepdims=True)
    inverse = lax.rsqrt(jnp.mean(center * center, axis=-1, keepdims=True) + NORM_EPS)
    return center * inverse, inverse


def norm_grad(grad, normed, inverse, gain):
    scaled = grad * gain
    return inverse * (
        scaled
        - jnp.mean(scaled, axis=-1, keepdims=True)
        - normed * jnp.mean(scaled * normed, axis=-1, keepdims=True)
    )


def column_sums(*rows):
    sums = [jnp.sum(r, axis=0, keepdims=True) for r in rows]
    return jnp.concatenate(sums + [jnp.zeros((8 - len(sums), D), F32)], axis=0)


def two_parts(sums):
    high = sums.astype(BF16).astype(F32)
    return jnp.concatenate([high, sums - high], axis=0).astype(BF16)


def bundle_body(place, up, down, mixer, shift, bundle):
    core = place[0] & 1
    size, rows = up.shape[0], mixer.shape[0] // 2

    @pl.when(core == 0)
    def _():
        bundle[0:size, :] = up[...]

    @pl.when(core == 1)
    def _():
        bundle[0:size, :] = down[...]

    mine = mixer[pl.ds(pl.multiple_of(core * rows, 16), rows), :]
    bundle[size : size + rows, :] = mine
    left = flat(shift)
    parts = []
    for _ in range(3):
        part = left.astype(BF16).astype(F32)
        parts.append(part)
        left = left - part
    parts.append(jnp.zeros((13, D), F32))
    bundle[size + rows :, :] = jnp.concatenate(parts, axis=0).astype(BF16)


def make_bundle(place, up, down, mixer, shift):
    rows = mixer.shape[0] // 2
    return call(
        bundle_body,
        "bundle",
        bf16(up.shape[0] + rows + 16, D),
        (place, up, down, mixer, shift),
        smem=1,
        us=20,
    )


def partner_weights(core, got, other, both):
    size = both.shape[1]
    both[core] = got[0:size, :]
    both[1 - core] = other[0:size, :]


def put_mixers(core, size, own, got, other, mine, theirs, mixers):
    rows = own.shape[0] // 2
    mixers[0] = own[...]
    start = pl.multiple_of(core * rows, 16)
    far = pl.multiple_of((1 - core) * rows, 16)
    mixers[2, pl.ds(start, rows), :] = got[size : size + rows, :]
    mixers[2, pl.ds(far, rows), :] = other[size : size + rows, :]
    mixers[1 + 2 * core] = mine[...]
    mixers[3 - 2 * core] = theirs[...]


def gelu_parts(x):
    cdf = 0.5 * (1.0 + lax.erf(x * math.sqrt(0.5)))
    slope = cdf + x * (jnp.exp(-0.5 * x * x) * (1.0 / math.sqrt(2.0 * math.pi)))
    return (x * cdf).astype(BF16), slope


def keep_and_send(partial, quarter, keep, send):
    rows = keep.shape[0]
    keep[...] = partial[pl.ds(pl.multiple_of(quarter * rows, 8), rows), :]
    other = pl.multiple_of((1 - quarter) * rows, 8)
    send[...] = partial[pl.ds(other, rows), :].astype(BF16)


def feed_body(parts, place, slot, *refs):
    tokens, mixer_shift, gain, shift, up, up_shift, down, got, other, mixer = refs[:10]
    far_mixer, other_mixer = refs[10:12]
    contexts = refs[12 : 12 + parts]
    first_mine, normed_mine, inverse_mine, low_out, slope_out, keep, send, mixers = refs[
        12 + parts : 20 + parts
    ]
    first, normed, inverse, partial, both = refs[20 + parts :]
    half = ROWS // 2
    core = place[0] & 1
    partner_weights(core, got, other, both)
    put_mixers(core, both.shape[1], mixer, got, other, far_mixer, other_mixer, mixers)
    mine = tokens[pl.ds(pl.multiple_of((slot[0] >> 1) * half, 16), half), :]
    mixed = flat(mixer_shift) + mine.astype(F32)
    for j, c in enumerate(contexts):
        mixed = mixed + dot(c[...], mixers[j])
    base = both.shape[1] + mixer.shape[0] // 2
    shift_rows = got[base : base + 16, :].astype(F32)
    far_shift = (shift_rows[0:1] + shift_rows[1:2]) + shift_rows[2:3]
    n1, r1 = norm_stats(mixed)
    rows1 = n1 * flat(gain) + flat(shift)
    first[...] = rows1
    normed[...] = n1
    inverse[...] = jnp.broadcast_to(r1, inverse.shape)
    low = rows1.astype(BF16)
    low_out[...] = low
    hidden, slope = gelu_parts(dot(low, up[...]) + flat(up_shift))
    slope_out[:, 0:D] = slope
    far_hidden, far_slope = gelu_parts(dot(low, both[0]) + far_shift)
    slope_out[:, D:] = far_slope
    partial[...] = dot(hidden, down[...]) + dot(far_hidden, both[1])
    quarter = slot[0] & 1
    keep_and_send(partial, quarter, keep, send)
    rows = first_mine.shape[0]
    start = pl.multiple_of(quarter * rows, 8)
    first_mine[...] = first[pl.ds(start, rows), :]
    normed_mine[...] = normed[pl.ds(start, rows), :]
    inverse_mine[...] = inverse[pl.ds(start, rows), :]


def second_body(slot, first, out_grad, down_shift, gain, shift, keep, got, layer, grad_out, low_out):
    rows = first.shape[0]
    total = first[...] + flat(down_shift) + keep[...] + got[...].astype(F32)
    n2, r2 = norm_stats(total)
    grad = out_grad[pl.ds(pl.multiple_of(slot[0] * rows, 8), rows), :]
    dh2 = norm_grad(grad, n2, r2, flat(gain))
    grad_out[...] = dh2
    low = dh2.astype(BF16)
    low_out[...] = low
    layer[0:rows, :] = (n2 * flat(gain) + flat(shift)).astype(BF16)
    layer[rows:, :] = two_parts(column_sums(grad * n2, grad, low.astype(F32)))


def feed_back_body(place, slot, slope, up, down, got, other, low_mine, low_got, low_half, keep, send, partial, both):
    partner_weights(place[0] & 1, got, other, both)
    quarter = slot[0] & 1
    take_chunks(quarter, (low_mine, low_got), low_half)
    low = low_half[...]
    near = (dot_nt(low, down[...]) * slope[:, 0:D]).astype(BF16)
    far = (dot_nt(low, both[1]) * slope[:, D:]).astype(BF16)
    partial[...] = dot_nt(near, up[...]) + dot_nt(far, both[0])
    keep_and_send(partial, quarter, keep, send)


def take_chunks(index, pieces, whole, first=0):
    rows = whole.shape[0] // len(pieces)
    for k, piece in enumerate(pieces):
        start = pl.multiple_of(jnp.bitwise_xor(index, k) * rows, 16)
        whole[pl.ds(start, rows), :] = piece[first : first + rows, :]


def first_back_body(parts, grad, normed, inverse, gain, keep, got, layer, mixers, *refs):
    dh1_out, payload = refs[:2]
    outs = refs[2:]
    total = grad[...] + keep[...] + got[...].astype(F32)
    n1 = normed[...]
    dh1 = norm_grad(total, n1, inverse[:, 0:1], flat(gain))
    dh1_out[...] = dh1
    low = dh1.astype(BF16)
    rows = dh1.shape[0]
    payload[0:rows, :] = low
    payload[rows : 2 * rows + 16, :] = layer[...]
    payload[2 * rows + 16 :, :] = two_parts(column_sums(total * n1, total, low.astype(F32)))
    for j, out in enumerate(outs):
        out[...] = dot_nt(low, mixers[j]).astype(BF16)


def split_body(parts, chunk, weighted, total, *refs):
    pieces, grad_pack, whole = refs[:parts], refs[parts], refs[parts + 1]
    take_chunks(chunk[0], pieces, whole)
    dctx = whole[...].astype(F32).T
    wide = HEADS * HS
    for h in range(HEADS):
        norm = total[h : h + 1, :]
        rows = dctx[h * HS : (h + 1) * HS]
        grad_pack[h * HS : (h + 1) * HS, :] = (rows / norm).astype(BF16)
        inner = jnp.sum(rows * weighted[h * HS : (h + 1) * HS, :], axis=0, keepdims=True)
        grad = -inner / (norm * norm)
        high = grad.astype(BF16).astype(F32)
        side = [high, grad - high, norm, jnp.zeros((GROUP - 3, ROWS), F32)]
        base = wide + h * GROUP
        grad_pack[base : base + GROUP, :] = jnp.concatenate(side, axis=0).astype(BF16)


def feed_grads_body(place, slot, low_mine, low_got, down_mine, down_got, up, up_shift, down, half_mine, half_other, sums, low_all, down_all):
    take_chunks(slot[0] >> 1, (low_mine, low_got), low_all)
    take_chunks(slot[0] >> 1, (down_mine, down_got), down_all)
    low, grad = low_all[...], down_all[...]
    hidden, slope = gelu_parts(dot(low, up[...]) + flat(up_shift))
    up_low = (dot_nt(grad, down[...]) * slope).astype(BF16)
    down_part = dot(hidden.T, grad).astype(BF16)
    up_part = dot(low.T, up_low).astype(BF16)
    core = place[0] & 1

    def put(first, second):
        first[0 : down_part.shape[0], :] = down_part
        second[0 : up_part.shape[0], :] = up_part

    pl.when(core == 0)(lambda: put(half_mine, half_other))
    pl.when(core == 1)(lambda: put(half_other, half_mine))
    sums[...] = jnp.broadcast_to(jnp.sum(up_low.astype(F32), axis=0, keepdims=True), sums.shape)


def mixer_grads_body(parts, place, slot, context, up_sums, taps, *refs):
    payloads = refs[:parts]
    half_mine, half_other, layer_out, whole, mixed = refs[parts:]
    wide = HEADS * HS
    rows = ROWS // parts
    take_chunks(slot[0], payloads, layer_out, rows)
    take_chunks(slot[0], payloads, mixed)

    def summed(row):
        total = jnp.zeros((8, D), F32)
        for r in payloads:
            total = total + r[row : row + 8, :].astype(F32) + r[row + 8 : row + 16, :].astype(F32)
        return total[0:3]

    context_t = context[...].astype(F32).T.astype(BF16)
    whole[0:wide, :] = dot(context_t, mixed[...]).astype(BF16)
    tap_block = jnp.concatenate([taps[0:HEADS, :], jnp.zeros((HEADS, D - 512), F32)], axis=1)
    small = jnp.concatenate(
        [summed(2 * rows), summed(2 * rows + 16), up_sums[0:1, :], tap_block, jnp.zeros((6, D), F32)],
        axis=0,
    )
    whole[wide : wide + 16, :] = small.astype(BF16)
    rest = whole.shape[0] - wide - 16
    if rest:
        whole[wide + 16 :, :] = jnp.zeros((rest, D), BF16)
    put_halves(place[0], whole, half_mine, half_other)


def halve_body(place, mine, other, *outs):
    rows = outs[0].shape[0]
    for k, out in enumerate(outs):
        start = pl.multiple_of(jnp.bitwise_xor(place[0] >> 1, k) * rows, 16)
        at = pl.ds(start, rows)
        out[...] = (mine[at, :].astype(F32) + other[at, :].astype(F32)).astype(BF16)


def settle_body(*refs):
    total = refs[0][...].astype(F32)
    for r in refs[1:-1]:
        total = total + r[...].astype(F32)
    refs[-1][...] = total.astype(BF16)


def join_body(place, *refs):
    take_chunks(place[0] >> 1, refs[:-1], refs[-1])


def chip_swaps(value, n):
    return [swap(value, "seq", 2 * k) for k in range(1, n // 2)]


def scatter_chips(mine, got, place, n):
    chips = n // 2
    half, width = mine.shape
    return call(
        halve_body,
        "halve",
        [bf16(half // chips, width)] * chips,
        (place, mine, got),
        smem=1,
    )


def halve_all_body(mine, other, out):
    out[...] = (mine[...].astype(F32) + other[...].astype(F32)).astype(BF16)


def total_body(place, *refs):
    pieces, out, stack = refs[:-2], refs[-2], refs[-1]
    for k, piece in enumerate(pieces):
        stack[jnp.bitwise_xor(place[0] >> 1, k)] = piece[...]
    total = stack[0].astype(F32)
    for k in range(1, len(pieces)):
        total = total + stack[k].astype(F32)
    out[...] = total.astype(BF16)


def total_chips(chip, got, place):
    terms = [chip] + list(got)
    return call(
        total_body,
        "total_small",
        bf16(*chip.shape),
        (place, *terms),
        smem=1,
        scratch=(pltpu.VMEM((len(terms), *chip.shape), BF16),),
    )


def both_halves(place, mine, other, whole):
    half = mine.shape[0]
    core = place & 1
    whole[pl.ds(pl.multiple_of(core * half, 16), half), :] = mine[...]
    whole[pl.ds(pl.multiple_of((1 - core) * half, 16), half), :] = other[...]


def finish_feed_body(place, mine, other, down, up):
    ff = down.shape[0]
    core = place[0] & 1

    def put(first, second):
        down[...] = first[0:ff, :].astype(F32)
        up[...] = second[0:D, :].astype(F32)

    pl.when(core == 0)(lambda: put(mine, other))
    pl.when(core == 1)(lambda: put(other, mine))


def finish_small_body(place, mine, other, mixer, g2, s2, od, g1, s1, om, ou, taps, whole):
    both_halves(place[0], mine, other, whole)
    wide = HEADS * HS
    mixer[...] = whole[0:wide, :].astype(F32)
    rows = whole[wide : wide + 16, :].astype(F32)
    for i, out in enumerate((g2, s2, od, g1, s1, om, ou)):
        out[...] = rows[i : i + 1, :].reshape(D)
    taps[...] = rows[7 : 7 + HEADS, TAP_LANE : TAP_LANE + CONV]


def weight_grads_body(n, *refs):
    blocks, tokens = refs[:n], refs[n : 2 * n]
    q, k, v, oq, ok, ov = refs[2 * n : 2 * n + 6]
    turned, rows = refs[2 * n + 6 :]
    wide = HEADS * HS
    for i in range(n):
        turned[:, i * ROWS : (i + 1) * ROWS] = blocks[i][...]
        rows[i * ROWS : (i + 1) * ROWS, :] = tokens[i][...]
    ones = jnp.ones((16, n * ROWS), BF16)
    for i, (grad, sums) in enumerate(((q, oq), (k, ok), (v, ov))):
        part = turned[i * wide : (i + 1) * wide, :]
        grad[...] = dot(part, rows[...])
        sums[...] = dot_nt(ones, part)[0:1, :].reshape(wide)


def tokens_sum_body(mine, other, out):
    out[...] = (mine[...].astype(F32) + other[...].astype(F32)).astype(BF16)


def tokens_out_body(slot, mine, other, out):
    half = mine.shape[0]
    kept = slot[0] >> 1
    out[pl.ds(pl.multiple_of(kept * half, 16), half), :] = mine[...].astype(F32)
    out[pl.ds(pl.multiple_of((1 - kept) * half, 16), half), :] = other[...].astype(F32)


def on_device(
    tokens,
    query_weight,
    query_shift,
    key_weight,
    key_shift,
    value_weight,
    value_shift,
    mixer_weight,
    mixer_shift,
    conv_taps,
    first_gain,
    first_shift,
    up_weight,
    up_shift,
    down_weight,
    down_shift,
    second_gain,
    second_shift,
    hyperplanes,
    plane_choice,
    doc_lengths,
    out_grad,
):
    n = lax.axis_size("seq")
    parts = lax.axis_size("hid")
    place = lax.axis_index("seq").reshape(1).astype(jnp.int32)
    hid = lax.axis_index("hid")
    slot = sum(jnp.where(hid == h, HID_ORDER[h], 0) for h in range(parts))
    slot = slot.reshape(1).astype(jnp.int32)
    rows, half = ROWS // parts, ROWS // 2
    units, wide = up_weight.shape[1], HEADS * HS
    hot = plane_choice.reshape(-1, 1) == jnp.arange(PLANES, dtype=jnp.int32)
    choose = hot.astype(BF16)
    choose_back = hot.astype(F32).T
    planes_t = hyperplanes.T
    wq, wk, wv = query_weight.T, key_weight.T, value_weight.T
    side = (TAP_LANE, 512 - TAP_LANE - CONV)
    taps = jnp.pad(conv_taps, ((0, 5), side))
    taps_back = jnp.pad(conv_taps[:, ::-1], ((0, 5), side))

    far_mixer = far_swap(mixer_weight)
    bundle = make_bundle(place, up_weight, down_weight, mixer_weight, up_shift)
    got = hid_swap(bundle, 2)

    raw_q, raw_k, tan_q, tan_k, pack = project(
        tokens, wq, query_shift, wk, key_shift, wv, value_shift, hyperplanes, choose
    )
    (far_mixer, taps, taps_back, planes_t), pack = after(
        (far_mixer, taps, taps_back, planes_t), pack
    )
    other_mixer = swap(far_mixer, "seq", 1)
    packs = over_seq(pack)
    context, near_half, far_half, weighted, total, states = forward(
        doc_lengths, place, slot, taps, packs
    )
    contexts = [
        near_half,
        hid_swap(near_half, 1),
        hid_swap(far_half, 2),
        hid_swap(far_half, 3),
    ]
    got, contexts[1] = after(got, contexts[1])
    other = swap(got, "seq", 1)
    first_mine, normed_mine, inverse_mine, low, slope, keep, send, mixers = call(
        functools.partial(feed_body, parts),
        "feed",
        (
            f32(rows, D),
            f32(rows, D),
            f32(rows, 128),
            bf16(half, D),
            f32(half, 2 * units),
            f32(rows, D),
            bf16(rows, D),
            bf16(parts, wide, D),
        ),
        (
            place,
            slot,
            tokens,
            mixer_shift,
            first_gain,
            first_shift,
            up_weight,
            up_shift,
            down_weight,
            got,
            other,
            mixer_weight,
            far_mixer,
            other_mixer,
            *contexts,
        ),
        smem=2,
        scratch=(
            pltpu.VMEM((half, D), F32),
            pltpu.VMEM((half, D), F32),
            pltpu.VMEM((half, 128), F32),
            pltpu.VMEM((half, D), F32),
            pltpu.VMEM((2, D, units), BF16),
        ),
        us=5,
    )
    partial = hid_swap(send, 1)
    tokens_later, keep = after(tokens, keep)
    token_blocks = cross_chips(tokens_later)
    layer, dh2, down_low = call(
        second_body,
        "second_norm",
        (bf16(rows + 16, D), f32(rows, D), bf16(rows, D)),
        (
            slot,
            first_mine,
            out_grad,
            down_shift,
            second_gain,
            second_shift,
            keep,
            partial,
        ),
        smem=1,
    )
    down_half, keep, send = call(
        feed_back_body,
        "feed_back",
        (bf16(half, D), f32(rows, D), bf16(rows, D)),
        (
            place,
            slot,
            slope,
            up_weight,
            down_weight,
            got,
            other,
            down_low,
            hid_swap(down_low, 1),
        ),
        smem=2,
        scratch=(pltpu.VMEM((half, D), F32), pltpu.VMEM((2, D, units), BF16)),
        us=0.5,
    )
    token_blocks, mixers = after(token_blocks, mixers)
    first_back = call(
        functools.partial(first_back_body, parts),
        "first_norm_back",
        (f32(rows, D), bf16(2 * rows + 32, D), *[bf16(rows, wide)] * parts),
        (dh2, normed_mine, inverse_mine, first_gain, keep, hid_swap(send, 1), layer, mixers),
        us=3,
    )
    dh1, payload = first_back[:2]
    pieces = exchange(first_back[2:])
    feed_half = padded(2 * max(units, D), n) // 2
    feed_mine, feed_other, up_sums = call(
        feed_grads_body,
        "feed_grads",
        (bf16(feed_half, D), bf16(feed_half, D), f32(8, units)),
        (
            place,
            slot,
            low,
            hid_swap(low, 2),
            down_half,
            hid_swap(down_half, 2),
            up_weight,
            up_shift,
            down_weight,
        ),
        smem=2,
        scratch=(
            pltpu.VMEM((ROWS, D), BF16),
            pltpu.VMEM((ROWS, D), BF16),
        ),
        us=6,
    )
    pieces, feed_other = after(pieces, feed_other)
    grad_pack = call(
        functools.partial(split_body, parts),
        "split",
        bf16(HEADS * (HS + GROUP), ROWS),
        (slot, weighted, total, *pieces),
        smem=1,
        scratch=(pltpu.VMEM((ROWS, wide), BF16),),
    )
    payload, grad_pack = after(payload, grad_pack)
    grad_blocks = cross_chips(grad_pack)
    feed_pieces = scatter_chips(feed_mine, swap(feed_other, "seq", 1), place, n)
    feed_got = [swap(feed_pieces[k], "seq", 2 * k) for k in range(1, n // 2)]
    feed_own, tan_q = after(feed_pieces[0], tan_q)
    query_turned, query_input, tap_rows = query_back(
        doc_lengths,
        place,
        grad_pack,
        states,
        tan_q,
        raw_q,
        choose_back,
        planes_t,
        wq,
        packs,
    )
    grad_blocks, query_turned = after(grad_blocks, query_turned)
    grad_packs = from_partner(grad_blocks)
    payloads = over_hid(payload)
    settled = call(settle_body, "settle", bf16(*feed_own.shape), (feed_own, *feed_got))
    small_half = -(-(wide + 16) // 32) * 16
    small_mine, small_other, layer_out = call(
        functools.partial(mixer_grads_body, parts),
        "mixer_grads",
        (bf16(small_half, D), bf16(small_half, D), bf16(ROWS, D)),
        (place, slot, context, up_sums, tap_rows, *payloads),
        smem=2,
        scratch=(pltpu.VMEM((2 * small_half, D), BF16), pltpu.VMEM((ROWS, D), BF16)),
    )
    (settled, small_other), grad_packs = after((settled, small_other), grad_packs)
    small_got = swap(small_other, "seq", 1)
    feed_chips = chip_swaps(settled, n)
    last = key_back(
        (
            doc_lengths,
            place,
            slot,
            tan_k,
            raw_k,
            taps_back,
            choose_back,
            planes_t,
            wk,
            wv,
            query_input,
            query_turned,
            dh1,
        ),
        packs,
        grad_packs,
    )
    last, (small_got, feed_chips) = after(last, (small_got, feed_chips))
    near_tokens = hid_swap(last[2], 2)
    blocks = over_seq(last[0])

    def tokens_sum(mine, other):
        return call(tokens_sum_body, "tokens_sum", bf16(half, D), (mine, other), us=0.3)

    both = tokens_sum(last[1], near_tokens)
    token_blocks, both = after(token_blocks, both)
    small_chip = call(halve_all_body, "halve_small", bf16(*small_mine.shape), (small_mine, small_got))
    both, small_chip = after(both, small_chip)
    feed_full = call(
        join_body, "join", bf16(feed_half, D), (place, settled, *feed_chips), smem=1, us=0.3
    )
    summed = tokens_sum(both, hid_swap(both, 1))
    summed, tokens_first = after(summed, tokens_later)
    tokens_grad = call(
        tokens_out_body, "tokens_out", f32(ROWS, D), (slot, summed, hid_swap(summed, 2)), smem=1
    )
    feed_sums = (feed_full, swap(feed_full, "seq", 1))
    small_full = total_chips(small_chip, chip_swaps(small_chip, n), place)
    small_sums = (small_full, swap(small_full, "seq", 1))
    token_blocks = from_partner(token_blocks)
    token_blocks[0] = tokens_first
    down_grad, up_grad = call(
        finish_feed_body,
        "finish_feed",
        (f32(units, D), f32(D, units)),
        (place, *feed_sums),
        smem=1,
        us=4,
    )
    mixer_grad, g2, s2, od, g1, s1, om, ou, taps_grad = call(
        finish_small_body,
        "finish_small",
        (f32(wide, D), *[f32(D)] * 6, f32(units), f32(HEADS, CONV)),
        (place, *small_sums),
        smem=1,
        scratch=(pltpu.VMEM((2 * small_half, D), BF16),),
    )
    q, k, v, oq, ok, ov = call(
        functools.partial(weight_grads_body, n),
        "weight_grads",
        (*[f32(wide, D)] * 3, *[f32(wide)] * 3),
        (*blocks, *token_blocks),
        scratch=(pltpu.VMEM((3 * wide, n * ROWS), BF16), pltpu.VMEM((n * ROWS, D), BF16)),
        us=0.3,
    )
    return (
        layer_out,
        tokens_grad,
        q.T,
        oq,
        k.T,
        ok,
        v.T,
        ov,
        mixer_grad,
        om,
        taps_grad,
        g1,
        s1,
        up_grad,
        ou,
        down_grad,
        od,
        g2,
        s2,
    )


def solution(mesh):
    placed = (
        P("seq", None),
        P(None, "hid"),
        P("hid"),
        P(None, "hid"),
        P("hid"),
        P(None, "hid"),
        P("hid"),
        P("hid", None),
        P(),
        P("hid", None),
        P(),
        P(),
        P(None, "hid"),
        P("hid"),
        P("hid", None),
        P(),
        P(),
        P(),
        P(),
        P(),
        P(),
        P("seq", None),
    )
    return jax.shard_map(
        on_device,
        mesh=mesh,
        in_specs=placed,
        out_specs=(
            P("seq", None),
            P("seq", None),
            P(None, "hid"),
            P("hid"),
            P(None, "hid"),
            P("hid"),
            P(None, "hid"),
            P("hid"),
            P("hid", None),
            P(),
            P("hid", None),
            P(),
            P(),
            P(None, "hid"),
            P("hid"),
            P("hid", None),
            P(),
            P(),
            P(),
        ),
        check_vma=False,
    )
```
